32 devices in a mesh: dp: 8 (over y, x, core), fsdp: 4 (over z).
Axes of the slice: x: 2, y: 2, z: 4, core: 2. Of those that a mesh axis runs over, the one named last changes fastest.
Arguments:
- tokens: bfloat16 [6144, 2048], P(('dp', 'fsdp')), may hold values from -6 to 6
- cotangent: bfloat16 [6144, 2048], P(('dp', 'fsdp')), may hold values from -6 to 6
- segments: int32 [64, 96], P(('dp', 'fsdp')), may hold values from 0 to 2, never falling along the last dimension, each value on 1 to 48 neighbouring positions
- routes: int32 [6144, 8], P(('dp', 'fsdp')), may hold values from 0 to 15, all different within a row; in each aligned block of 96 rows (0 to 95, 96 to 191, ...) at most 72 rows name the same one
- w_qkv: bfloat16 [6144, 2048], P(('dp', 'fsdp')), may hold values from -0.125 to 0.125
- w_out: bfloat16 [2048, 2048], P(('dp', 'fsdp')), may hold values from -0.75 to 0.75
- norm_gains: bfloat16 [2048, 4], P(('dp', 'fsdp')), may hold values from 0.099609375 to 1.8984375
- w_router: bfloat16 [2048, 16], P(('dp', 'fsdp')), may hold values from -0.0625 to 0.0625
- w_gate_up: bfloat16 [16, 2048, 2048], P('fsdp', 'dp'), may hold values from -0.125 to 0.125
- w_down: bfloat16 [16, 2048, 1024], P('fsdp', 'dp'), may hold values from -1.5 to 1.5
Outputs:
- output: bfloat16 [6144, 2048], P(('dp', 'fsdp'))
- grad_tokens: float32 [6144, 2048], P(('dp', 'fsdp'))
- grad_qkv: float32 [6144, 2048], P(('dp', 'fsdp'))
- grad_out: float32 [2048, 2048], P(('dp', 'fsdp'))
- grad_gains: float32 [2048, 4], P(('dp', 'fsdp'))
- grad_router: float32 [2048, 16], P(('dp', 'fsdp'))
- grad_gate_up: float32 [16, 2048, 2048], P('fsdp', 'dp')
- grad_down: float32 [16, 2048, 1024], P('fsdp', 'dp')
The draws below stay inside these ranges and needn't reach their ends.
Inputs may be any that keep to these rules, and one draw needn't show every extreme that they name: Each row names 8 different experts. In each sequence (96 rows of routes, aligned) at most 72 rows name one expert, a bound that some block reaches there. `segments`: along each sequence the ids start at 0 and never fall; a document has at most 48 tokens.
All inputs are finite; a program needn't handle non-finite values.
Results may differ from the reference program's by a relative error of at most 0.015.
Values may be sent and summed in bfloat16 or wider, within the bound.
No kernel may reach another device: no remote copies, remote signals or barrier semaphores. Data moves between devices by JAX's collectives and lax.ppermute only.
A program may use at most 320 MiB of HBM per device.

```python
import math
import jax
import jax.numpy as jnp
import numpy as np
from jax import lax

D = 2048
H = 16
HD = 128
FF = 1024
TOP = 8
E = 16
LEN = 96
CAP = 72
DOCS = 3
TOKENS = 6144
SEQS = 64


def block_scale(stream_key, shape, split, smallest, largest):
    gain, own = 1.0, jax.random.fold_in(stream_key, 6)
    for dim, parts in split:
        heights = jnp.exp(jax.random.uniform(jax.random.fold_in(own, dim), (parts,), jnp.float32, smallest / len(split), largest / len(split)))
        gain = gain * jnp.repeat(heights, shape[dim] // parts).reshape([-1 if axis == dim else 1 for axis in range(len(shape))])
    return gain


def profile(count, total, limit, skew):
    portions = [(1 << 20) // math.isqrt(rank ** skew) + 1 for rank in range(2, count + 1)]
    surplus, counts = total - limit - (count - 1), [1] * (count - 1)
    while surplus > 0:
        candidates = [i for i in range(count - 1) if counts[i] < limit]
        whole, left = sum([portions[i] for i in candidates]), surplus
        for i in candidates:
            addition = min(limit - counts[i], max(1, left * portions[i] // whole), surplus)
            counts[i] = counts[i] + addition
            surplus = surplus - addition
    return np.array([limit] + counts)


def ragged_sizes(own_key, amount, total, limit, lean):
    if amount == 2:
        one = jax.random.randint(own_key, (), max(1, total - limit), min(limit, total - 1) + 1)
        return jnp.stack([one, total - one])
    lengths = jnp.asarray(profile(amount, total, limit, lean), jnp.int32)
    pairs = (amount - 1) // 2
    giver, taker = lengths[1:1 + 2 * pairs:2], lengths[2:2 + 2 * pairs:2]
    slack = jnp.minimum(giver - 1, limit - taker)
    passed = jax.random.randint(jax.random.fold_in(own_key, 1), (pairs,), 0, 1 << 20) % (slack + 1)
    lengths = lengths.at[1:1 + 2 * pairs:2].set(giver - passed).at[2:2 + 2 * pairs:2].set(taker + passed)
    return lengths[jax.random.permutation(jax.random.fold_in(own_key, 2), amount)]


def routed_block(own_key, own, number, rows, count, top, bound, slope):
    sequence = jax.random.permutation(own_key, count)
    packed, usual = load_shares(count, rows * top, bound, slope, True), load_shares(count, rows * top, bound, slope, False)
    places = jnp.arange(count)

    def named(lengths, offset_by):
        used = int((lengths > 0).sum())
        fixed = max(1, used // 4)
        moved = fixed + (places - fixed + offset_by * (used - fixed)) % max(1, count - fixed)
        return jnp.zeros((count,), jnp.int32).at[sequence[jnp.where(places < fixed, places, moved)]].set(jnp.asarray(lengths, jnp.int32))

    lengths = jnp.where(number % 4 == 0, named(packed, number // 4), named(usual, number - number // 4 - 1))
    mixed = jax.random.permutation(jax.random.fold_in(own, 3), count)
    giver, receiver = mixed[0:count // 2 * 2:2], mixed[1:count // 2 * 2:2]
    slack = jnp.minimum(lengths[giver] - 1, bound - lengths[receiver]) // 2
    slack = jnp.where((giver == sequence[0]) | (receiver == sequence[0]) | (lengths[receiver] == 0), 0, jnp.maximum(slack, 0))
    moved = jax.random.randint(jax.random.fold_in(own, 4), (count // 2,), 0, 1 << 20) % (slack + 1)
    lengths = lengths.at[giver].add(-moved).at[receiver].add(moved)
    labels = jnp.searchsorted(jnp.cumsum(lengths), jnp.arange(rows * top), side="right").astype(jnp.int32)
    listing = labels.reshape(top, rows).T
    listing = listing[jax.random.permutation(jax.random.fold_in(own, 1), rows)]
    offset_by = jax.random.randint(jax.random.fold_in(own, 2), (rows, 1), 0, top)
    return jnp.take_along_axis(listing, (jnp.arange(top)[None, :] + offset_by) % top, axis=1)


def load_shares(count, total, bound, skew, full):
    loads = [(1 << 20) // math.isqrt(standing ** skew) + 1 for standing in range(1, count + 1)]
    largest = bound if full else min(bound, max(-(-total // count), total * loads[0] // sum(loads)))
    least = 1 if total - largest >= count - 1 else 0
    given, rest = [largest] + [least] * (count - 1), total - largest - least * (count - 1)
    while rest > 0:
        free = [i for i in range(1, count) if given[i] < largest] or [i for i in range(1, count) if given[i] < bound]
        whole, budget = sum([loads[i] for i in free]), rest
        for i in free:
            addition = min(bound - given[i], max(1, budget * loads[i] // whole), rest)
            given[i] = given[i] + addition
            rest = rest - addition
    return np.array(given)


def centred(key, extent, spread, limit, split=(), kind=jnp.bfloat16):
    level = block_scale(key, extent, split, -0.22, 0.18) if split else 1.0
    array = jax.random.normal(key, extent, jnp.float32) * spread * level
    return jnp.minimum(jnp.maximum(array, -limit), limit).astype(kind)


def setup_inputs(seed: int = 0) -> dict:
    key_list = jax.random.split(jax.random.key(seed), 11)
    tokens = centred(key_list[0], (TOKENS, D), 1.0, 6.0, ((0, 32),))
    cotangent = centred(key_list[1], (TOKENS, D), 1.0, 6.0, ((0, 32),))
    segments = jax.vmap(lambda own: jnp.searchsorted(jnp.cumsum(ragged_sizes(own, DOCS, LEN, LEN // 2, 0)), jnp.arange(LEN), side="right"))(jax.random.split(key_list[2], SEQS)).reshape((SEQS, LEN)).astype(jnp.int32)
    routes_keys = jax.random.split(jax.random.fold_in(key_list[3], 1), TOKENS // LEN)
    routes_turns = jax.random.permutation(jax.random.fold_in(key_list[3], 3), TOKENS // LEN)
    routes = jax.vmap(lambda own, number: routed_block(jax.random.fold_in(key_list[3], 2), own, number, LEN, E, TOP, CAP, 2))(routes_keys, routes_turns).reshape((TOKENS, TOP))
    w_qkv = centred(key_list[4], (3 * D, D), D ** -0.5, 0.125, ((0, 32),))
    w_out = centred(key_list[5], (D, D), (D // 32) ** -0.5, 0.75, ((0, 32),))
    norm_gains = jnp.clip(1.0 + 0.18 * jax.random.normal(key_list[6], (D, 4), jnp.float32), 0.099609375, 1.8984375).astype(jnp.bfloat16)
    w_router = centred(key_list[7], (D, E), (4 * D) ** -0.5, 0.0625, ((0, 32),))
    w_gate_up = centred(key_list[8], (E, 2 * FF, D), D ** -0.5, 0.125, ((0, 4), (1, 8)))
    w_down = centred(key_list[9], (E, D, FF), (FF // 64) ** -0.5, 1.5, ((0, 4), (1, 8)))
    return dict(tokens=tokens, cotangent=cotangent, segments=segments, routes=routes, w_qkv=w_qkv, w_out=w_out, norm_gains=norm_gains, w_router=w_router, w_gate_up=w_gate_up, w_down=w_down)


NORM_EPS = 1e-05
ROPE_BASE = 10000.0
PRECISE = lax.Precision.HIGHEST

@jax.custom_vjp
def low(v):
    return lax.optimization_barrier(v.astype(jnp.bfloat16)).astype(jnp.float32)

@jax.custom_vjp
def low_back(v):
    return v

def low_keep(v):
    return (low(v), None)

def low_pass(kept, grad):
    return (grad,)

def back_keep(v):
    return (v, None)

def back_low(kept, grad):
    return (low(grad),)
low.defvjp(low_keep, low_pass)
low_back.defvjp(back_keep, back_low)

def inverse_rms(field_in):
    return lax.rsqrt(lax.optimization_barrier(jnp.mean(field_in * field_in, axis=-1, keepdims=True)) + NORM_EPS)

def rotate(field_in, cos_table, sin_table):
    half_dim = field_in.shape[-1] // 2
    first_half = field_in[..., :half_dim]
    second_half = field_in[..., half_dim:]
    return jnp.concatenate([first_half * cos_table - second_half * sin_table, second_half * cos_table + first_half * sin_table], axis=-1)

def rope_tables(length, head_dim):
    half_dim = head_dim // 2
    frequency = ROPE_BASE ** (-(jnp.arange(half_dim).astype(jnp.float32) * 2.0) / head_dim)
    angles = jnp.arange(length).astype(jnp.float32)[:, None] * frequency[None, :]
    return (jnp.cos(angles)[:, None, :], jnp.sin(angles)[:, None, :])

def attend_one(seq_parts):
    queries, keys_seq, values_seq, seg_row = seq_parts
    scores = jnp.einsum('qhd,khd->hqk', queries, keys_seq, precision=PRECISE) * HD ** (-0.5)
    scores = low_back(scores)
    position = jnp.arange(LEN)
    allowed = (position[:, None] >= position[None, :]) & (seg_row[:, None] == seg_row[None, :])
    scores = jnp.where(allowed[None], scores, -1e+30)
    weights = low(jax.nn.softmax(scores, axis=-1))
    blended = jnp.einsum('hqk,khd->qhd', weights, values_seq, precision=PRECISE)
    return low_back(low(blended)).reshape(LEN, D)

def expert_one(expert_parts):
    row_block, gate_up, down_proj = expert_parts
    gate_and_up = low_back(jnp.dot(row_block, gate_up.T, precision=PRECISE))
    gate_part = gate_and_up[:, :FF]
    up_part = gate_and_up[:, FF:]
    activation = low(jax.nn.silu(gate_part) * up_part)
    return low_back(low(jnp.dot(activation, down_proj.T, precision=PRECISE)))

def layer_forward(x_float, w_qkv, w_out, norm_gains, w_router, w_gate_up, w_down, segments, routes, place_index):
    normed_one = x_float * inverse_rms(x_float)
    hidden_one = low(normed_one * norm_gains[:, 0])
    projected = low_back(jnp.dot(hidden_one, w_qkv.T, precision=PRECISE))
    queries = projected[:, :D]
    keys_all = projected[:, D:2 * D]
    values_all = projected[:, 2 * D:]
    queries = queries * inverse_rms(queries) * norm_gains[:, 1]
    keys_all = keys_all * inverse_rms(keys_all) * norm_gains[:, 2]
    cos_table, sin_table = rope_tables(LEN, HD)
    head_shape = (SEQS, LEN, H, HD)
    queries = low(rotate(queries.reshape(head_shape), cos_table, sin_table))
    keys_all = low(rotate(keys_all.reshape(head_shape), cos_table, sin_table))
    values_all = low(values_all).reshape(head_shape)
    attended = lax.map(jax.checkpoint(attend_one), (queries, keys_all, values_all, segments)).reshape(TOKENS, D)
    residual = x_float + low_back(jnp.dot(attended, w_out.T, precision=PRECISE))
    normed_two = residual * inverse_rms(residual)
    hidden_two = low(normed_two * norm_gains[:, 3])
    router_probs = jax.nn.softmax(jnp.dot(hidden_two, w_router, precision=PRECISE), axis=-1)
    gate_vals = jnp.take_along_axis(router_probs, routes, axis=1)
    buffer = jnp.zeros((E, SEQS * CAP, D), jnp.float32).at[routes, place_index].set(jnp.broadcast_to(hidden_two[:, None, :], (TOKENS, TOP, D)))
    buffer = low_back(buffer)
    outputs = lax.map(jax.checkpoint(expert_one), (buffer, w_gate_up, w_down))
    chosen = outputs[routes, place_index]
    return residual + lax.optimization_barrier(jnp.sum(gate_vals[:, :, None] * chosen, axis=1))

def reference(tokens, cotangent, segments, routes, w_qkv, w_out, norm_gains, w_router, w_gate_up, w_down):
    blocks = routes.reshape(SEQS, LEN * TOP)
    onehot = (blocks[:, :, None] == jnp.arange(E, dtype=jnp.int32)[None, None, :]).astype(jnp.int32)
    earlier = jnp.cumsum(onehot, axis=1) - onehot
    slot_index = lax.optimization_barrier(jnp.sum(earlier * onehot, axis=2))
    place_index = (slot_index + (jnp.arange(SEQS, dtype=jnp.int32) * CAP)[:, None]).reshape(TOKENS, TOP).astype(jnp.int32)

    def apply_layer(x_float, qkv_f, out_f, gains_f, router_f, gate_up_f, down_f):
        return layer_forward(x_float, qkv_f, out_f, gains_f, router_f, gate_up_f, down_f, segments, routes, place_index)
    primals = (tokens.astype(jnp.float32), w_qkv.astype(jnp.float32), w_out.astype(jnp.float32), norm_gains.astype(jnp.float32), w_router.astype(jnp.float32), w_gate_up.astype(jnp.float32), w_down.astype(jnp.float32))
    result, pullback = jax.vjp(apply_layer, *primals)
    gradients = pullback(cotangent.astype(jnp.float32))
    return (result.astype(jnp.bfloat16), gradients[0], gradients[1], gradients[2], gradients[3], gradients[4], gradients[5], gradients[6])
```

```python
import jax
import jax.numpy as jnp
from jax import lax
from jax.sharding import Mesh
from jax.sharding import PartitionSpec as P

D = 2048
H = 16
HD = 128
FF = 1024
TOP = 8
E = 16
LEN = 96

NORM_EPS = 1e-05
ROPE_BASE = 10000.0
PRECISE = lax.Precision.HIGHEST
DP = ("q", "c")
ALL = ("q", "c", "z")
f32 = jnp.float32
bf16 = jnp.bfloat16


def inverse_rms(field_in):
    return lax.rsqrt(jnp.mean(field_in * field_in, axis=-1, keepdims=True) + NORM_EPS)


def rotate(field_in, cos_table, sin_table):
    half_dim = field_in.shape[-1] // 2
    first_half = field_in[..., :half_dim]
    second_half = field_in[..., half_dim:]
    return jnp.concatenate(
        [
            first_half * cos_table - second_half * sin_table,
            second_half * cos_table + first_half * sin_table,
        ],
        axis=-1,
    )


def rope_tables(length, head_dim):
    half_dim = head_dim // 2
    frequency = ROPE_BASE ** (-(jnp.arange(half_dim).astype(f32) * 2.0) / head_dim)
    angles = jnp.arange(length).astype(f32)[:, None] * frequency[None, :]
    return (jnp.cos(angles)[:, None, :], jnp.sin(angles)[:, None, :])


def norm_back(grad_normed, normed, inverse):
    return inverse * (grad_normed - normed * jnp.mean(grad_normed * normed, axis=-1, keepdims=True))


def mm(a, b, ca, cb):
    return lax.dot_general(a, b, (((ca,), (cb,)), ((), ())), preferred_element_type=f32)


def flip(value, size, bit):
    return lax.ppermute(value, DP, [(i, i ^ (1 << bit)) for i in range(size)])


def gather_xor(value, size, bits):
    lead = 0
    for bit in bits:
        other = flip(value, size, bit)
        value = jnp.stack([value, other], axis=lead)
        lead += 1
    return value


def bit_lists(size):
    high = list(range(1, size.bit_length() - 1))
    return high, high[::-1]


def gather_dp(value, size):
    width = value.shape[-1] // 2
    pieces = []
    for part, order in zip((value[:, :width], value[:, width:]), bit_lists(size)):
        out = part
        for k, bit in enumerate(order):
            out = jnp.stack([out, flip(out, size, bit)], axis=k)
        perm = [order.index(bit) for bit in range(len(order), 0, -1)]
        out = out.transpose(perm + [len(order), len(order) + 1])
        pieces.append(out.reshape((-1,) + part.shape))
    both = jnp.concatenate(pieces, axis=-1)
    other = flip(both, size, 0)
    return jnp.stack([both, other], axis=1).reshape((size,) + value.shape)


def scatter_dp(parts, size):
    rows, width = parts.shape[1], parts.shape[2]
    pair = parts.reshape(size // 2, 2, rows, width)
    got = flip(pair[:, 1], size, 0)
    summed = (pair[:, 0].astype(f32) + got.astype(f32)).astype(bf16)
    highs = size.bit_length() - 2
    halves = []
    for half, order in enumerate(bit_lists(size)):
        cur = summed[:, :, half * (width // 2) : (half + 1) * (width // 2)]
        cur = cur.reshape([2] * highs + [rows, width // 2])
        left = list(range(highs, 0, -1))
        for k, bit in enumerate(order):
            axis = left.index(bit)
            left.remove(bit)
            keep = lax.index_in_dim(cur, 0, axis, keepdims=False)
            send = lax.index_in_dim(cur, 1, axis, keepdims=False)
            total = keep.astype(f32) + flip(send, size, bit).astype(f32)
            cur = total if k == len(order) - 1 else total.astype(bf16)
        halves.append(cur)
    return jnp.concatenate(halves, axis=-1)


def gather_z(value, zs):
    spread = jnp.broadcast_to(value[None], (zs,) + value.shape)
    return lax.all_to_all(spread, "z", 0, 0, tiled=True)


def scatter_z(parts):
    got = lax.all_to_all(parts, "z", 0, 0, tiled=True)
    return jnp.sum(got.astype(f32), axis=0)


def swap_core(value):
    return lax.ppermute(value, "c", [(0, 1), (1, 0)])


def psum_dp(value, size):
    spread = jnp.broadcast_to(value[None], (size,) + value.shape)
    return jnp.sum(lax.all_to_all(spread, DP, 0, 0, tiled=True), axis=0)


def per_device(
    tokens, cotangent, segments, routes, w_qkv, w_out, norm_gains, w_router, w_gate_up, w_down
):
    zs = lax.axis_size("z")
    dps = lax.axis_size("q") * 2
    qi, ci, zi = lax.axis_index("q"), lax.axis_index("c"), lax.axis_index("z")
    di = qi * 2 + ci
    rows = tokens.shape[0]
    seqs = rows // LEN
    width = D // dps
    heads = width // HD
    local_experts = E // zs
    mine = local_experts // 2
    score_scale = HD ** (-0.5)
    sub = w_qkv.shape[0] // 3
    orow = w_out.shape[0]

    small = lax.all_gather(
        jnp.concatenate([norm_gains, w_router], axis=1), ALL, axis=0, tiled=True
    ).astype(f32)
    gains_f = small[:, :4]
    router_f = small[:, 4:]

    def unit_perm(t, back):
        pairs = []
        for i in range(dps):
            for j in range(zs):
                dest = (3 * i + (3 * j + t) // zs) % dps
                src_dev, dst_dev = i * zs + j, dest * zs + j
                pairs.append((dst_dev, src_dev) if back else (src_dev, dst_dev))
        return pairs

    moved = [
        lax.ppermute(w_qkv[t * sub : (t + 1) * sub], ALL, unit_perm(t, False)) for t in range(3)
    ]
    inv3 = pow(3, -1, dps)
    slot_of = [[0, 0, 0] for _ in range(dps)]
    type_of = [[0, 0, 0] for _ in range(dps)]
    for i in range(dps):
        for s in range(3):
            src = (inv3 * (i - s)) % dps
            kind = (3 * src + s) // dps
            slot_of[i][kind] = s
            type_of[i][s] = kind
    slot_of = jnp.asarray(slot_of, jnp.int32)[di]
    type_of = jnp.asarray(type_of, jnp.int32)[di]
    qkv_slots = gather_z(jnp.concatenate(moved, axis=0), zs).reshape(3, width, D)
    w_three = jnp.concatenate(
        [lax.dynamic_index_in_dim(qkv_slots, slot_of[k], 0, keepdims=False) for k in range(3)],
        axis=0,
    )
    out_cols = lax.all_to_all(
        w_out.reshape(orow, dps, width).transpose(1, 0, 2), DP, 0, 0, tiled=True
    )
    w_out_c = gather_z(out_cols, zs).transpose(1, 0, 2, 3).reshape(D, width)

    tok_g = gather_dp(tokens, dps).reshape(dps * rows, D)
    seg_g = lax.all_gather(segments, DP, axis=0, tiled=True).reshape(dps, seqs, LEN)
    order = jnp.arange(dps) ^ di
    seg_g = seg_g[order].reshape(dps * seqs, LEN)
    all_seqs = dps * seqs
    all_rows = dps * rows

    def core_half(weight):
        swapped = lax.all_to_all(
            weight.reshape((2, mine) + weight.shape[1:]), "c", 0, 0, tiled=True
        )
        return [swapped[:, e].reshape((2 * weight.shape[1], weight.shape[2])) for e in range(mine)]

    gu_half = core_half(w_gate_up)
    down_half = core_half(w_down)
    expert_w = []
    for e in range(mine):
        expert_w.append(
            (
                lax.all_gather(gu_half[e], "q", axis=0, tiled=True),
                lax.all_gather(down_half[e], "q", axis=0, tiled=True),
            )
        )

    def gather_cz(value):
        got = gather_z(value, zs).reshape((zs * value.shape[0],) + value.shape[1:])
        return jnp.concatenate([got, swap_core(got)], axis=0)

    def scatter_cz(parts):
        half = parts.shape[0] // 2
        mixed = parts[:half].astype(f32) + swap_core(parts[half:].astype(bf16)).astype(f32)
        return scatter_z(mixed.astype(bf16).reshape((zs, half // zs) + parts.shape[1:]))

    dy_g = gather_cz(cotangent)
    routes_g = gather_cz(routes)

    cos_table, sin_table = rope_tables(LEN, HD)
    position = jnp.arange(LEN)
    causal = position[:, None] >= position[None, :]
    head_shape = (all_seqs, LEN, heads, HD)

    x_g = tok_g.astype(f32)
    inv_one_g = inverse_rms(x_g)
    hidden_one = (x_g * inv_one_g * gains_f[:, 0]).astype(bf16)
    projected = mm(hidden_one, w_three, 1, 1)
    raw_q = projected[:, :width]
    raw_k = projected[:, width : 2 * width]
    raw_v = projected[:, 2 * width :]
    squares = psum_dp_stack(raw_q * raw_q, raw_k * raw_k, dps, di)
    inv_q = lax.rsqrt(squares[0] / D + NORM_EPS)[:, None]
    inv_k = lax.rsqrt(squares[1] / D + NORM_EPS)[:, None]
    normed_q = raw_q * inv_q
    normed_k = raw_k * inv_k
    own_gains = lax.dynamic_slice(gains_f, (di * width, 0), (width, 4))
    gain_q, gain_k = own_gains[:, 1], own_gains[:, 2]
    queries = rotate((normed_q * gain_q).reshape(head_shape), cos_table, sin_table).astype(bf16)
    keys_all = rotate((normed_k * gain_k).reshape(head_shape), cos_table, sin_table).astype(bf16)
    values_all = raw_v.reshape(head_shape).astype(bf16)
    allowed = causal[None] & (seg_g[:, :, None] == seg_g[:, None, :])
    scores = (
        jnp.einsum("sqhd,skhd->shqk", queries, keys_all, preferred_element_type=f32) * score_scale
    )
    scores = jnp.where(allowed[:, None], scores, -1e30)
    attn_probs = jax.nn.softmax(scores, axis=-1)
    probs_low = attn_probs.astype(bf16)
    attended = (
        jnp.einsum("shqk,skhd->sqhd", probs_low, values_all, preferred_element_type=f32)
        .astype(bf16)
        .reshape(all_rows, width)
    )
    attn_out = scatter_dp(mm(attended, w_out_c, 1, 1).astype(bf16).reshape(dps, rows, D), dps)

    x_float = tokens.astype(f32)
    inverse_one = inverse_rms(x_float)
    normed_one = x_float * inverse_one
    residual = x_float + attn_out
    inverse_two = inverse_rms(residual)
    normed_two = residual * inverse_two
    hidden_two = (normed_two * gains_f[:, 3]).astype(bf16)

    hidden_g = gather_cz(hidden_two)
    router_low = router_f.astype(bf16)
    router_g = jax.nn.softmax(mm(hidden_g, router_low, 1, 0), axis=-1)
    router_probs = jax.nn.softmax(mm(hidden_two, router_low, 1, 0), axis=-1)
    dy_f = dy_g.astype(f32)
    first_expert = zi * local_experts + ci * mine
    out_part = None
    hid_part = None
    gate_cols = []
    grad_gu, grad_dn = [], []
    for e in range(mine):
        gate_up, down = expert_w[e]
        expert = first_expert + e
        picked = jnp.any(routes_g == expert, axis=1, keepdims=True)
        prob = jnp.sum(
            jnp.where(jnp.arange(E)[None] == expert, router_g, 0.0), axis=1, keepdims=True
        )
        gate_val = jnp.where(picked, prob, 0.0)
        gate_and_up = mm(hidden_g, gate_up, 1, 1)
        g_part = gate_and_up[:, :FF]
        u_part = gate_and_up[:, FF:]
        sig = jax.nn.sigmoid(g_part)
        silu = g_part * sig
        act = (silu * u_part).astype(bf16)
        expert_out = mm(act, down, 1, 1).astype(bf16).astype(f32)
        piece = gate_val * expert_out
        out_part = piece if out_part is None else out_part + piece
        gate_cols.append(jnp.where(picked[:, 0], jnp.sum(dy_f * expert_out, axis=1), 0.0))
        grad_eo = (gate_val * dy_f).astype(bf16)
        grad_act = mm(grad_eo, down, 1, 0)
        grad_g = grad_act * u_part * sig * (1.0 + g_part * (1.0 - sig))
        grad_u = grad_act * silu
        grad_both = jnp.concatenate([grad_g, grad_u], axis=-1).astype(bf16)
        grad_dn.append(
            lax.psum_scatter(
                mm(grad_eo, act, 0, 0).astype(bf16), "q", scatter_dimension=0, tiled=True
            )
        )
        grad_gu.append(
            lax.psum_scatter(
                mm(grad_both, hidden_g, 0, 0).astype(bf16), "q", scatter_dimension=0, tiled=True
            )
        )
        rows_back = mm(grad_both, gate_up, 1, 0).astype(bf16).astype(f32)
        hid_part = rows_back if hid_part is None else hid_part + rows_back

    cols = jnp.stack(gate_cols, axis=0).reshape(mine, 2, zs, rows)
    other_cols = swap_core(cols[:, 1])
    both_cols = jnp.stack([cols[:, 0], other_cols], axis=0)
    back_cols = lax.all_to_all(both_cols.transpose(2, 0, 1, 3), "z", 0, 0, tiled=True)
    back_cols = jnp.where(ci == 0, back_cols, back_cols[:, ::-1])
    gp = back_cols.reshape(E, rows).T

    grad_hidden = scatter_cz(hid_part)
    result = residual + scatter_cz(out_part)

    grad_logits = router_probs * (gp - jnp.sum(router_probs * gp, axis=-1, keepdims=True))
    grad_router = lax.dot_general(
        hidden_two.astype(f32), grad_logits, (((0,), (0,)), ((), ())), precision=PRECISE
    )
    grad_hidden = grad_hidden + jnp.dot(grad_logits, router_f.T, precision=PRECISE)
    grad_gain_two = jnp.sum(grad_hidden * normed_two, axis=0)
    grad_residual = cotangent.astype(f32) + norm_back(
        grad_hidden * gains_f[:, 3], normed_two, inverse_two
    )
    grad_attn = grad_residual.astype(bf16)

    grad_attn_g = gather_dp(grad_attn, dps).reshape(all_rows, D)
    grad_heads = mm(grad_attn_g, w_out_c, 1, 0).astype(bf16).reshape(head_shape)
    grad_out_c = mm(grad_attn_g, attended, 0, 0)
    grad_probs = jnp.einsum("sqhd,skhd->shqk", grad_heads, values_all, preferred_element_type=f32)
    grad_values = jnp.einsum("shqk,sqhd->skhd", probs_low, grad_heads, preferred_element_type=f32)
    row_delta = jnp.sum(attn_probs * grad_probs, axis=-1, keepdims=True)
    grad_scores = (attn_probs * (grad_probs - row_delta)).astype(bf16)
    grad_queries = (
        jnp.einsum("shqk,skhd->sqhd", grad_scores, keys_all, preferred_element_type=f32)
        * score_scale
    )
    grad_keys = (
        jnp.einsum("shqk,sqhd->skhd", grad_scores, queries, preferred_element_type=f32)
        * score_scale
    )
    grad_nq = rotate(grad_queries, cos_table, -sin_table).reshape(all_rows, width)
    grad_nk = rotate(grad_keys, cos_table, -sin_table).reshape(all_rows, width)
    grad_gain_q = jnp.sum(grad_nq * normed_q, axis=0)
    grad_gain_k = jnp.sum(grad_nk * normed_k, axis=0)
    a_q = grad_nq * gain_q
    a_k = grad_nk * gain_k
    means = psum_dp_stack(a_q * normed_q, a_k * normed_k, dps, di) / D
    grad_raw_q = inv_q * (a_q - normed_q * means[0][:, None])
    grad_raw_k = inv_k * (a_k - normed_k * means[1][:, None])
    grad_projected = jnp.concatenate(
        [grad_raw_q, grad_raw_k, grad_values.reshape(all_rows, width)], axis=1
    ).astype(bf16)
    grad_h1 = scatter_dp(
        mm(grad_projected, w_three, 1, 0).astype(bf16).reshape(dps, rows, D), dps
    )
    grad_gain_one = jnp.sum(grad_h1 * normed_one, axis=0)
    grad_tokens = grad_residual + norm_back(grad_h1 * gains_f[:, 0], normed_one, inverse_one)

    grad_three = mm(grad_projected, hidden_one, 0, 0).astype(bf16).reshape(3, width, D)
    grad_slots = jnp.concatenate(
        [lax.dynamic_index_in_dim(grad_three, type_of[s], 0, keepdims=True) for s in range(3)],
        axis=0,
    )
    own_slots = scatter_z(grad_slots.reshape(zs, 3 * sub, D)).astype(bf16)
    grad_qkv = jnp.concatenate(
        [
            lax.ppermute(own_slots[t * sub : (t + 1) * sub], ALL, unit_perm(t, True))
            for t in range(3)
        ],
        axis=0,
    ).astype(f32)
    grad_cols = scatter_z(
        grad_out_c.astype(bf16).reshape(dps, zs, orow, width).transpose(1, 0, 2, 3)
    ).astype(bf16)
    grad_out = (
        lax.all_to_all(grad_cols, DP, 0, 0, tiled=True)
        .transpose(1, 0, 2)
        .reshape(orow, D)
        .astype(f32)
    )

    shard_cols = jnp.zeros((D, 2), f32)
    shard_cols = lax.dynamic_update_slice(
        shard_cols, jnp.stack([grad_gain_q, grad_gain_k], axis=1), (di * width, 0)
    )
    small_grads = jnp.concatenate(
        [grad_gain_one[:, None], shard_cols, grad_gain_two[:, None], grad_router], axis=1
    )
    small_own = lax.psum_scatter(small_grads, ALL, scatter_dimension=0, tiled=True)

    def core_back(parts):
        stacked = jnp.stack(parts, axis=0)
        split = stacked.reshape((mine, 2, stacked.shape[1] // 2, stacked.shape[2]))
        got = lax.all_to_all(split.transpose(1, 0, 2, 3), "c", 0, 0, tiled=True)
        return got.reshape((local_experts,) + got.shape[2:]).astype(f32)

    return (
        result.astype(bf16),
        grad_tokens,
        grad_qkv,
        grad_out,
        small_own[:, :4],
        small_own[:, 4:],
        core_back(grad_gu),
        core_back(grad_dn),
    )


def psum_dp_stack(first, second, size, own):
    count = first.shape[0]
    sums = jnp.stack([jnp.sum(first, axis=1), jnp.sum(second, axis=1)], axis=0)
    rel = sums.reshape(2, size, count // size)
    index = jnp.arange(size) ^ own
    true = rel[:, index].reshape(2, count)
    total = psum_dp(true, size).reshape(2, size, count // size)
    return total[:, index].reshape(2, count)


def solution(mesh):
    dps, zs = mesh.shape["dp"], mesh.shape["fsdp"]
    inner = Mesh(mesh.devices.reshape(dps // 2, 2, zs), ALL)
    rows = P(ALL, None)
    experts = P("z", DP, None)
    in_specs = (rows,) * 8 + (experts,) * 2
    out_specs = (rows,) * 6 + (experts,) * 2
    return jax.shard_map(
        per_device, mesh=inner, in_specs=in_specs, out_specs=out_specs, check_vma=False
    )
```

```python
import functools

import jax
import jax.numpy as jnp
from jax import lax
from jax.experimental import pallas as pl
from jax.experimental.pallas import tpu as pltpu
from jax.sharding import Mesh
from jax.sharding import PartitionSpec as P

D = 2048
H = 16
HD = 128
FF = 1024
TOP = 8
E = 16
LEN = 96

NORM_EPS = 1e-05
ROPE_BASE = 10000.0
PRECISE = lax.Precision.HIGHEST
DP = ("q", "c")
ALL = ("q", "c", "z")
f32 = jnp.float32
bf16 = jnp.bfloat16


def inverse_rms(field_in):
    return lax.rsqrt(jnp.mean(field_in * field_in, axis=-1, keepdims=True) + NORM_EPS)


def rope_tables(length, head_dim):
    half_dim = head_dim // 2
    frequency = ROPE_BASE ** (-(jnp.arange(half_dim).astype(f32) * 2.0) / head_dim)
    angles = jnp.arange(length).astype(f32)[:, None] * frequency[None, :]
    return jnp.cos(angles), jnp.sin(angles)


def norm_back(grad_normed, normed, inverse):
    return inverse * (grad_normed - normed * jnp.mean(grad_normed * normed, axis=-1, keepdims=True))


def mm(a, b, ca, cb):
    return lax.dot_general(a, b, (((ca,), (cb,)), ((), ())), preferred_element_type=f32)


def flip(value, size, bit):
    return lax.ppermute(value, DP, [(i, i ^ (1 << bit)) for i in range(size)])


def relative(size):
    return [high * 2 + core for core in range(2) for high in range(size // 2)]


def bit_lists(size):
    high = list(range(1, size.bit_length() - 1))
    return high, high[::-1]


def gather_dp(value, size):
    width = value.shape[-1] // 2
    pieces = []
    for part, order in zip((value[:, :width], value[:, width:]), bit_lists(size)):
        out, have = part, []
        for bit in order:
            axis = sum(1 for other in have if other > bit)
            out = jnp.stack([out, flip(out, size, bit)], axis=axis)
            have.append(bit)
        pieces.append(out.reshape(-1, width))
    both = jnp.concatenate(pieces, axis=-1)
    return jnp.concatenate([both, flip(both, size, 0)], axis=0)


def scatter_dp(parts, size):
    rows, width = parts.shape[0] // size, parts.shape[1]
    half_rows = parts.shape[0] // 2
    got = flip(parts[half_rows:], size, 0)
    summed = (parts[:half_rows].astype(f32) + got.astype(f32)).astype(bf16)
    highs = size.bit_length() - 2
    halves = []
    for half, order in enumerate(bit_lists(size)):
        cur = summed[:, half * (width // 2) : (half + 1) * (width // 2)]
        cur = cur.reshape([2] * highs + [rows, width // 2])
        left = list(range(highs, 0, -1))
        for k, bit in enumerate(order):
            axis = left.index(bit)
            left.remove(bit)
            keep = lax.index_in_dim(cur, 0, axis, keepdims=False)
            send = lax.index_in_dim(cur, 1, axis, keepdims=False)
            total = keep.astype(f32) + flip(send, size, bit).astype(f32)
            cur = total if k == len(order) - 1 else total.astype(bf16)
        halves.append(cur)
    return jnp.concatenate(halves, axis=-1)


def sum_dp(value, size):
    count = size.bit_length() - 1
    shape = value.shape
    value = value[:2].reshape((2,) + (2,) * count + (-1,))
    for bit in range(count):
        value = value + jnp.flip(flip(value, size, bit), 1 if bit == 0 else count - bit + 1)
    return jnp.pad(value.reshape(2, shape[1]), ((0, 6), (0, 0)))


def line(value, zs, step):
    return lax.ppermute(value, "z", [(j, j + step) for j in range(zs) if 0 <= j + step < zs])


def gather_z(value, zs, zi):
    right, left = [value], [value]
    for _ in range(zs - 1):
        right.append(line(right[-1], zs, 1))
        left.append(line(left[-1], zs, -1))
    return [value] + [jnp.where(zi >= k, right[k], left[zs - k]) for k in range(1, zs)]


def gather_z_true(value, zs, zi):
    blocks = jnp.stack(gather_z(value, zs, zi)[::-1] * 2, axis=0)
    return lax.dynamic_slice_in_dim(blocks, zs - 1 - zi, zs, 0)


def scatter_z(parts):
    zs = len(parts)
    right, left = None, None
    for s in range(1, zs):
        go_right = parts[s] if right is None else (parts[s].astype(f32) + right).astype(bf16)
        go_left = parts[zs - s] if left is None else (parts[zs - s].astype(f32) + left).astype(bf16)
        right = line(go_right, zs, 1).astype(f32)
        left = line(go_left, zs, -1).astype(f32)
    return parts[0].astype(f32) + right + left


def swap_core(value):
    return lax.ppermute(value, "c", [(0, 1), (1, 0)])


def gather_cz(value, zs, zi):
    got = jnp.concatenate(gather_z(value, zs, zi), axis=0)
    return jnp.concatenate([got, swap_core(got)], axis=0)


def scatter_cz(parts, zs):
    half = parts.shape[0] // 2
    mixed = parts[:half].astype(f32) + swap_core(parts[half:].astype(bf16)).astype(f32)
    mixed = mixed.astype(bf16)
    block = half // zs
    return scatter_z([mixed[k * block : (k + 1) * block] for k in range(zs)])


BLOCK = 4 * LEN


def kdot(a, b, ca, cb):
    return lax.dot_general(a, b, (((ca,), (cb,)), ((), ())), preferred_element_type=f32)


def to_rows(first, second):
    lane = lax.broadcasted_iota(jnp.int32, (first.shape[0], 128), 1)
    both = jnp.where(lane == 0, first, jnp.where(lane == 1, second, 0.0))
    return both.T[:8]


def to_cols(block):
    cols = jnp.concatenate([block] * 16, axis=0).T
    return cols[:, 0:1], cols[:, 1:2]


def qkv_kernel(width, tok_ref, gain_ref, w_ref, hid_ref, raw_ref, sum_ref):
    x = tok_ref[...].astype(f32)
    inverse = lax.rsqrt(jnp.mean(x * x, axis=-1, keepdims=True) + NORM_EPS)
    hidden = (x * inverse * gain_ref[...]).astype(bf16)
    hid_ref[...] = hidden
    raw = kdot(hidden, w_ref[...], 1, 1)
    raw_ref[...] = raw
    q, k = raw[:, :width], raw[:, width : 2 * width]
    sum_ref[...] = to_rows(
        jnp.sum(q * q, axis=-1, keepdims=True), jnp.sum(k * k, axis=-1, keepdims=True)
    )


def spin(x, cos, sin):
    return x * cos + pltpu.roll(x, HD // 2, 1) * sin


def heads_of(raw, inv_q, inv_k, gain_ref, cos, sin, width, head):
    lo = head * HD
    normed_q = raw[:, lo : lo + HD] * inv_q
    normed_k = raw[:, width + lo : width + lo + HD] * inv_k
    query = spin(normed_q * gain_ref[0:1, lo : lo + HD], cos, sin).astype(bf16)
    key = spin(normed_k * gain_ref[1:2, lo : lo + HD], cos, sin).astype(bf16)
    value = raw[:, 2 * width + lo : 2 * width + lo + HD].astype(bf16)
    return normed_q, normed_k, query, key, value


def probs_of(query, key, mask):
    scores = jnp.where(mask > 0.5, kdot(query, key, 1, 1) * HD ** (-0.5), -1e30)
    scores = jnp.exp(scores - jnp.max(scores, axis=-1, keepdims=True))
    return scores / jnp.sum(scores, axis=-1, keepdims=True)


def inverses(sum_ref):
    ss_q, ss_k = to_cols(sum_ref[...])
    return lax.rsqrt(ss_q / D + NORM_EPS), lax.rsqrt(ss_k / D + NORM_EPS)


def attend_kernel(width, raw_ref, sum_ref, gain_ref, cos_ref, sin_ref, mask_ref, w_ref, att_ref, part_ref):
    inv_q, inv_k = inverses(sum_ref)
    raw = raw_ref[...]
    cos, sin = cos_ref[...], sin_ref[...]
    for head in range(width // HD):
        _, _, query, key, value = heads_of(raw, inv_q, inv_k, gain_ref, cos, sin, width, head)
        for s in range(BLOCK // LEN):
            at = slice(s * LEN, (s + 1) * LEN)
            probs = probs_of(query[at], key[at], mask_ref[s])
            att_ref[at, head * HD : (head + 1) * HD] = kdot(
                probs.astype(bf16), value[at], 1, 0
            ).astype(bf16)
    part_ref[...] = kdot(att_ref[...], w_ref[...], 1, 1).astype(bf16)


def attend_back_kernel(
    width, raw_ref, sum_ref, gain_ref, cos_ref, sin_ref, mask_ref, w_ref, grad_ref,
    back_ref, dv_ref, dot_ref, gsum_ref,
):
    inv_q, inv_k = inverses(sum_ref)
    raw = raw_ref[...]
    cos, sin = cos_ref[...], sin_ref[...]
    grad_heads = kdot(grad_ref[...], w_ref[...], 1, 0).astype(bf16)

    @pl.when(pl.program_id(0) == 0)
    def _():
        gsum_ref[...] = jnp.zeros_like(gsum_ref)

    dot_q = dot_k = 0.0
    for head in range(width // HD):
        lo = head * HD
        normed_q, normed_k, query, key, value = heads_of(
            raw, inv_q, inv_k, gain_ref, cos, sin, width, head
        )
        grads_q, grads_k = [], []
        for s in range(BLOCK // LEN):
            at = slice(s * LEN, (s + 1) * LEN)
            probs = probs_of(query[at], key[at], mask_ref[s])
            grad = grad_heads[at, lo : lo + HD]
            grad_probs = kdot(grad, value[at], 1, 1)
            dv_ref[at, lo : lo + HD] = kdot(probs.astype(bf16), grad, 0, 0).astype(bf16)
            delta = jnp.sum(probs * grad_probs, axis=-1, keepdims=True)
            grad_scores = (probs * (grad_probs - delta)).astype(bf16)
            grads_q.append(kdot(grad_scores, key[at], 1, 0))
            grads_k.append(kdot(grad_scores, query[at], 0, 0))
        grad_nq = spin(jnp.concatenate(grads_q, axis=0) * HD ** (-0.5), cos, -sin)
        grad_nk = spin(jnp.concatenate(grads_k, axis=0) * HD ** (-0.5), cos, -sin)
        prod_q, prod_k = grad_nq * normed_q, grad_nk * normed_k
        gsum_ref[0:1, lo : lo + HD] += jnp.sum(prod_q, axis=0, keepdims=True)
        gsum_ref[1:2, lo : lo + HD] += jnp.sum(prod_k, axis=0, keepdims=True)
        gain_q, gain_k = gain_ref[0:1, lo : lo + HD], gain_ref[1:2, lo : lo + HD]
        dot_q = dot_q + jnp.sum(prod_q * gain_q, axis=-1, keepdims=True)
        dot_k = dot_k + jnp.sum(prod_k * gain_k, axis=-1, keepdims=True)
        back_ref[:, lo : lo + HD] = grad_nq * gain_q
        back_ref[:, width + lo : width + lo + HD] = grad_nk * gain_k
    dot_ref[...] = to_rows(dot_q, dot_k)


def project_back_kernel(
    width, raw_ref, sum_ref, back_ref, dv_ref, dot_ref, w_ref, proj_ref, part_ref
):
    inv_q, inv_k = inverses(sum_ref)
    mean_q, mean_k = to_cols(dot_ref[...] / D)
    normed_q = raw_ref[:, :width] * inv_q
    normed_k = raw_ref[:, width : 2 * width] * inv_k
    proj_ref[:, :width] = (inv_q * (back_ref[:, :width] - normed_q * mean_q)).astype(bf16)
    proj_ref[:, width : 2 * width] = (
        inv_k * (back_ref[:, width:] - normed_k * mean_k)
    ).astype(bf16)
    proj_ref[:, 2 * width :] = dv_ref[...]
    part_ref[...] = kdot(proj_ref[...], w_ref[...], 1, 0).astype(bf16)


def by_rows(cols):
    return pl.BlockSpec((BLOCK, cols), lambda i: (i, 0))


def across(rows):
    return pl.BlockSpec((rows, BLOCK), lambda i: (0, i))


def whole(shape):
    return pl.BlockSpec(shape, lambda i: (0,) * len(shape))


def run_blocks(body, rows, in_specs, out_specs, out_shape, args, flops):
    nbytes = sum(arg.size * arg.dtype.itemsize for arg in args)
    nbytes += sum(out.size * out.dtype.itemsize for out in out_shape)
    return pl.pallas_call(
        body,
        grid=(rows // BLOCK,),
        in_specs=in_specs,
        out_specs=out_specs,
        out_shape=out_shape,
        cost_estimate=pl.CostEstimate(flops=flops, bytes_accessed=nbytes, transcendentals=0),
    )(*args)


def shape_of(rows, cols, dtype):
    return jax.ShapeDtypeStruct((rows, cols), dtype)


def per_device(
    tokens, cotangent, segments, routes, w_qkv, w_out, norm_gains, w_router, w_gate_up, w_down
):
    zs = lax.axis_size("z")
    dps = lax.axis_size("q") * 2
    world = dps * zs
    qi, ci, zi = lax.axis_index("q"), lax.axis_index("c"), lax.axis_index("z")
    di = qi * 2 + ci
    rows = tokens.shape[0]
    seqs = rows // LEN
    width = D // dps
    local_experts = E // zs
    mine = local_experts // 2
    sub = w_qkv.shape[0] // 3
    orow = w_out.shape[0]
    all_rows = dps * rows
    all_seqs = dps * seqs

    def unit_perm(t, back):
        pairs = []
        for i in range(dps):
            for j in range(zs):
                dest = (3 * i + (3 * j + t) // zs) % dps
                src_dev, dst_dev = i * zs + j, dest * zs + j
                pairs.append((dst_dev, src_dev) if back else (src_dev, dst_dev))
        return pairs

    moved = [
        lax.ppermute(w_qkv[t * sub : (t + 1) * sub], ALL, unit_perm(t, False)) for t in range(3)
    ]
    inv3 = pow(3, -1, dps)
    slot_of = [[0, 0, 0] for _ in range(dps)]
    type_of = [[0, 0, 0] for _ in range(dps)]
    for i in range(dps):
        for s in range(3):
            src = (inv3 * (i - s)) % dps
            kind = (3 * src + s) // dps
            slot_of[i][kind] = s
            type_of[i][s] = kind
    slot_of = jnp.asarray(slot_of, jnp.int32)[di]
    type_of = jnp.asarray(type_of, jnp.int32)[di]

    mini = jnp.concatenate(
        [
            norm_gains.reshape(-1),
            w_router.reshape(-1),
            segments.astype(bf16).reshape(-1),
            routes.astype(bf16).reshape(-1),
        ]
    )
    minis = lax.all_to_all(
        jnp.broadcast_to(mini[None], (world,) + mini.shape), ALL, 0, 0, tiled=True
    )
    at = 0
    split = []
    for part in (norm_gains, w_router, segments, routes):
        split.append(minis[:, at : at + part.size])
        at += part.size
    gains_f = split[0].reshape(D, 4).astype(f32)
    router_low = split[1].reshape(D, E)
    router_f = router_low.astype(f32)
    seg_all = split[2].reshape(dps, zs, seqs, LEN)
    seg_own = lax.dynamic_index_in_dim(seg_all, zi, 1, keepdims=False)
    seg_own = seg_own[jnp.asarray(relative(dps)) ^ di].reshape(all_seqs, LEN)
    routes_all = split[3].reshape(dps // 2, 2, zs, rows, TOP)
    routes_own = lax.dynamic_index_in_dim(routes_all, qi, 0, keepdims=False)
    routes_own = routes_own[jnp.stack([ci, 1 - ci])][:, (zi - jnp.arange(zs)) % zs]
    routes_g = routes_own.reshape(2 * zs * rows, TOP).astype(jnp.int32)
    position = jnp.arange(LEN)
    causal = position[:, None] >= position[None, :]
    mask = (causal[None] & (seg_own[:, :, None] == seg_own[:, None, :])).astype(f32)
    own_gains = lax.dynamic_slice(gains_f, (di * width, 0), (width, 4))
    gain_rows = jnp.pad(own_gains[:, 1:3].T, ((0, 6), (0, 0)))
    cos_table, sin_table = rope_tables(LEN, HD)
    cos_full = jnp.tile(jnp.concatenate([cos_table, cos_table], axis=1), (BLOCK // LEN, 1))
    sin_full = jnp.tile(jnp.concatenate([-sin_table, sin_table], axis=1), (BLOCK // LEN, 1))

    tok_g = gather_dp(tokens, dps)
    qkv_slots = gather_z_true(jnp.concatenate(moved, axis=0), zs, zi).reshape(3, width, D)
    w_three = jnp.concatenate(
        [lax.dynamic_index_in_dim(qkv_slots, slot_of[k], 0, keepdims=False) for k in range(3)],
        axis=0,
    )
    out_cols = lax.all_to_all(
        w_out.reshape(orow, dps, width).transpose(1, 0, 2), DP, 0, 0, tiled=True
    )
    w_out_c = gather_z_true(out_cols, zs, zi).transpose(1, 0, 2, 3).reshape(D, width)

    def core_half(weight):
        swapped = lax.all_to_all(
            weight.reshape((2, mine) + weight.shape[1:]), "c", 0, 0, tiled=True
        )
        return [swapped[:, e].reshape((2 * weight.shape[1], weight.shape[2])) for e in range(mine)]

    gu_half = core_half(w_gate_up)
    down_half = core_half(w_down)
    expert_w = []
    for e in range(mine):
        expert_w.append(
            (
                lax.all_gather(gu_half[e], "q", axis=0, tiled=True),
                lax.all_gather(down_half[e], "q", axis=0, tiled=True),
            )
        )

    hidden_one, raw, sums = run_blocks(
        functools.partial(qkv_kernel, width),
        all_rows,
        [by_rows(D), whole((1, D)), whole((3 * width, D))],
        [by_rows(D), by_rows(3 * width), across(8)],
        [
            shape_of(all_rows, D, bf16),
            shape_of(all_rows, 3 * width, f32),
            shape_of(8, all_rows, f32),
        ],
        (tok_g, gains_f[:, 0][None], w_three),
        6 * all_rows * width * D,
    )
    dy_g = gather_cz(cotangent, zs, zi)
    sums = sum_dp(sums, dps)
    mask_spec = pl.BlockSpec((BLOCK // LEN, LEN, LEN), lambda i: (i, 0, 0))
    table_specs = [whole((8, width)), whole((BLOCK, HD)), whole((BLOCK, HD)), mask_spec]
    tables = (gain_rows, cos_full, sin_full, mask)
    attended, part = run_blocks(
        functools.partial(attend_kernel, width),
        all_rows,
        [by_rows(3 * width), across(8)] + table_specs + [whole((D, width))],
        [by_rows(width), by_rows(D)],
        [shape_of(all_rows, width, bf16), shape_of(all_rows, D, bf16)],
        (raw, sums) + tables + (w_out_c,),
        3 * all_rows * width * D,
    )
    part, dy_g = lax.optimization_barrier((part, dy_g))
    attn_out = scatter_dp(part, dps)
    x_float = tokens.astype(f32)
    inverse_one = inverse_rms(x_float)
    normed_one = x_float * inverse_one
    residual = x_float + attn_out
    inverse_two = inverse_rms(residual)
    normed_two = residual * inverse_two
    hidden_two = (normed_two * gains_f[:, 3]).astype(bf16)
    router_probs = jax.nn.softmax(mm(hidden_two, router_low, 1, 0), axis=-1)

    hidden_g = gather_cz(hidden_two, zs, zi)
    router_g = jax.nn.softmax(mm(hidden_g, router_low, 1, 0), axis=-1)
    dy_f = dy_g.astype(f32)
    first_expert = zi * local_experts + ci * mine

    passes = []
    for e in range(mine):
        gate_up, down = expert_w[e]
        expert = first_expert + e
        picked = jnp.any(routes_g == expert, axis=1, keepdims=True)
        prob = jnp.sum(
            jnp.where(jnp.arange(E)[None] == expert, router_g, 0.0), axis=1, keepdims=True
        )
        gate_val = jnp.where(picked, prob, 0.0)
        gate_and_up = mm(hidden_g, gate_up, 1, 1)
        g_part = gate_and_up[:, :FF]
        u_part = gate_and_up[:, FF:]
        sig = jax.nn.sigmoid(g_part)
        silu = g_part * sig
        act = (silu * u_part).astype(bf16)
        expert_out = mm(act, down, 1, 1).astype(bf16).astype(f32)
        grad_gate = jnp.where(picked[:, 0], jnp.sum(dy_f * expert_out, axis=1), 0.0)
        grad_eo = (gate_val * dy_f).astype(bf16)
        grad_act = mm(grad_eo, down, 1, 0)
        grad_g = grad_act * u_part * sig * (1.0 + g_part * (1.0 - sig))
        grad_u = grad_act * silu
        grad_both = jnp.concatenate([grad_g, grad_u], axis=-1).astype(bf16)
        rows_back = mm(grad_both, gate_up, 1, 0).astype(bf16).astype(f32)
        dn = mm(grad_eo, act, 0, 0).astype(bf16)
        gu = mm(grad_both, hidden_g, 0, 0).astype(bf16)
        passes.append(
            dict(
                out=gate_val * expert_out,
                back=rows_back,
                gate=grad_gate,
                dn=lax.psum_scatter(dn, "q", scatter_dimension=0, tiled=True),
                gu=lax.psum_scatter(gu, "q", scatter_dimension=0, tiled=True),
            )
        )

    hid_part = sum([p["back"] for p in passes[1:]], passes[0]["back"])
    out_part = sum([p["out"] for p in passes[1:]], passes[0]["out"])
    grad_hidden = scatter_cz(hid_part, zs)
    cols = jnp.stack([p["gate"] for p in passes], axis=0).reshape(mine, 2, zs, rows)
    cols = jnp.where(ci == 0, cols, cols[:, ::-1])
    cols = cols[:, :, (zi - jnp.arange(zs)) % zs]
    got = lax.all_to_all(
        cols.transpose(1, 2, 0, 3).reshape(2 * zs, mine, rows), ("c", "z"), 0, 0, tiled=True
    )
    gp = got.reshape(2, zs, mine, rows).transpose(1, 0, 2, 3).reshape(E, rows).T

    grad_logits = router_probs * (gp - jnp.sum(router_probs * gp, axis=-1, keepdims=True))
    grad_router = lax.dot_general(
        hidden_two.astype(f32), grad_logits, (((0,), (0,)), ((), ())), precision=PRECISE
    )
    grad_hidden = grad_hidden + jnp.dot(grad_logits, router_f.T, precision=PRECISE)
    gain_two = jnp.sum(grad_hidden * normed_two, axis=0)
    grad_residual = cotangent.astype(f32) + norm_back(
        grad_hidden * gains_f[:, 3], normed_two, inverse_two
    )

    grad_attn_g = gather_dp(grad_residual.astype(bf16), dps)
    back, dv, dots, gain_sums = run_blocks(
        functools.partial(attend_back_kernel, width),
        all_rows,
        [by_rows(3 * width), across(8)] + table_specs + [whole((D, width)), by_rows(D)],
        [by_rows(2 * width), by_rows(width), across(8), whole((8, width))],
        [
            shape_of(all_rows, 2 * width, f32),
            shape_of(all_rows, width, bf16),
            shape_of(8, all_rows, f32),
            shape_of(8, width, f32),
        ],
        (raw, sums) + tables + (w_out_c, grad_attn_g),
        5 * all_rows * width * D,
    )
    dots = sum_dp(dots, dps)
    grad_projected, part = run_blocks(
        functools.partial(project_back_kernel, width),
        all_rows,
        [
            by_rows(3 * width), across(8), by_rows(2 * width), by_rows(width), across(8),
            whole((3 * width, D)),
        ],
        [by_rows(3 * width), by_rows(D)],
        [shape_of(all_rows, 3 * width, bf16), shape_of(all_rows, D, bf16)],
        (raw, sums, back, dv, dots, w_three),
        6 * all_rows * width * D,
    )
    grad_h1 = scatter_dp(part, dps)
    gain_one = jnp.sum(grad_h1 * normed_one, axis=0)
    grad_tokens = grad_residual + norm_back(grad_h1 * gains_f[:, 0], normed_one, inverse_one)
    result = residual + scatter_cz(out_part, zs)

    def z_parts(value):
        return [
            lax.dynamic_index_in_dim(value, (zi - k) % zs, 0, keepdims=False) for k in range(zs)
        ]

    grad_out_c = mm(grad_attn_g, attended, 0, 0)
    grad_cols = scatter_z(
        z_parts(grad_out_c.astype(bf16).reshape(dps, zs, orow, width).transpose(1, 0, 2, 3))
    ).astype(bf16)
    grad_out = (
        lax.all_to_all(grad_cols, DP, 0, 0, tiled=True)
        .transpose(1, 0, 2)
        .reshape(orow, D)
        .astype(f32)
    )
    grad_three = mm(grad_projected, hidden_one, 0, 0).astype(bf16).reshape(3, width, D)
    grad_slots = jnp.concatenate(
        [lax.dynamic_index_in_dim(grad_three, type_of[s], 0, keepdims=True) for s in range(3)],
        axis=0,
    )
    own_slots = scatter_z(z_parts(grad_slots.reshape(zs, 3 * sub, D))).astype(bf16)
    grad_qkv = jnp.concatenate(
        [
            lax.ppermute(own_slots[t * sub : (t + 1) * sub], ALL, unit_perm(t, True))
            for t in range(3)
        ],
        axis=0,
    ).astype(f32)

    shard_cols = lax.dynamic_update_slice(jnp.zeros((D, 2), f32), gain_sums[:2].T, (di * width, 0))
    small_grads = jnp.concatenate(
        [gain_one[:, None], shard_cols, gain_two[:, None], grad_router], axis=1
    )
    small_own = jnp.sum(
        lax.all_to_all(
            small_grads.reshape(world, D * (E + 4) // world), ALL, 0, 0, tiled=True
        ),
        axis=0,
    ).reshape(D // world, E + 4)

    def core_back(parts):
        stacked = jnp.stack(parts, axis=0)
        split = stacked.reshape((mine, 2, stacked.shape[1] // 2, stacked.shape[2]))
        got = lax.all_to_all(split.transpose(1, 0, 2, 3), "c", 0, 0, tiled=True)
        return got.reshape((local_experts,) + got.shape[2:]).astype(f32)

    return (
        result.astype(bf16),
        grad_tokens,
        grad_qkv,
        grad_out,
        small_own[:, :4],
        small_own[:, 4:],
        core_back([p["gu"] for p in passes]),
        core_back([p["dn"] for p in passes]),
    )


def solution(mesh):
    dps, zs = mesh.shape["dp"], mesh.shape["fsdp"]
    inner = Mesh(mesh.devices.reshape(dps // 2, 2, zs), ALL)
    rows = P(ALL, None)
    experts = P("z", DP, None)
    in_specs = (rows,) * 8 + (experts,) * 2
    out_specs = (rows,) * 6 + (experts,) * 2
    return jax.shard_map(
        per_device, mesh=inner, in_specs=in_specs, out_specs=out_specs, check_vma=False
    )
```

```python
import functools

import jax
import jax.numpy as jnp
from jax import lax
from jax.experimental import pallas as pl
from jax.experimental.pallas import tpu as pltpu
from jax.sharding import Mesh
from jax.sharding import PartitionSpec as P

D = 2048
H = 16
HD = 128
FF = 1024
TOP = 8
E = 16
LEN = 96

NORM_EPS = 1e-05
ROPE_BASE = 10000.0
PRECISE = lax.Precision.HIGHEST
DP = ("q", "c")
ALL = ("q", "c", "z")
f32 = jnp.float32
bf16 = jnp.bfloat16


def inverse_rms(field_in):
    return lax.rsqrt(jnp.mean(field_in * field_in, axis=-1, keepdims=True) + NORM_EPS)


def rope_tables(length, head_dim):
    half_dim = head_dim // 2
    frequency = ROPE_BASE ** (-(jnp.arange(half_dim).astype(f32) * 2.0) / head_dim)
    angles = jnp.arange(length).astype(f32)[:, None] * frequency[None, :]
    return jnp.cos(angles), jnp.sin(angles)


def norm_back(grad_normed, normed, inverse):
    return inverse * (grad_normed - normed * jnp.mean(grad_normed * normed, axis=-1, keepdims=True))


def mm(a, b, ca, cb):
    return lax.dot_general(a, b, (((ca,), (cb,)), ((), ())), preferred_element_type=f32)


def after(value, *deps):
    return lax.optimization_barrier((value,) + tuple(deps))[0]


def flip(value, size, bit):
    return lax.ppermute(value, DP, [(i, i ^ (1 << bit)) for i in range(size)])


def relative(size):
    return [high * 2 + core for core in range(2) for high in range(size // 2)]


def bit_lists(size):
    high = list(range(1, size.bit_length() - 1))
    return high, high[::-1]


def gather_dp(value, size, gate=()):
    width = value.shape[-1] // 2
    pieces = []
    for part, order in zip((value[:, :width], value[:, width:]), bit_lists(size)):
        out, have = part, []
        for bit in order:
            axis = sum(1 for other in have if other > bit)
            out = jnp.stack([out, flip(out, size, bit)], axis=axis)
            have.append(bit)
        pieces.append(out.reshape(-1, width))
    sent = [after(piece, *gate) for piece in pieces] if gate else pieces
    return pieces + [flip(piece, size, 0) for piece in sent]


def scatter_dp(own, other, size):
    rows, width = own.shape[0] * 2 // size, own.shape[1]
    got = flip(other, size, 0)
    summed = (own.astype(f32) + got.astype(f32)).astype(bf16)
    highs = size.bit_length() - 2
    halves, last = [], []
    for half, order in enumerate(bit_lists(size)):
        cur = summed[:, half * (width // 2) : (half + 1) * (width // 2)]
        cur = cur.reshape([2] * highs + [rows, width // 2])
        left = list(range(highs, 0, -1))
        for k, bit in enumerate(order):
            axis = left.index(bit)
            left.remove(bit)
            keep = lax.index_in_dim(cur, 0, axis, keepdims=False)
            send = lax.index_in_dim(cur, 1, axis, keepdims=False)
            brought = flip(send, size, bit)
            total = keep.astype(f32) + brought.astype(f32)
            cur = total if k == len(order) - 1 else total.astype(bf16)
        halves.append(cur)
        last.append(brought)
    return jnp.concatenate(halves, axis=-1), summed, last


def sum_dp(value, size):
    count = size.bit_length() - 1
    shape = value.shape
    value = value[:2].reshape((2,) + (2,) * count + (-1,))
    for bit in range(count):
        value = value + jnp.flip(flip(value, size, bit), 1 if bit == 0 else count - bit + 1)
    return jnp.pad(value.reshape(2, shape[1]), ((0, 6), (0, 0)))


def line(value, zs, step):
    return lax.ppermute(value, "z", [(j, j + step) for j in range(zs) if 0 <= j + step < zs])


def all_after(values, deps):
    return list(lax.optimization_barrier(tuple(values) + tuple(deps))[: len(values)])


def gather_z(value, zs, zi, gates={}):
    right, left = [value], [value]
    for s in range(1, zs):
        sent = all_after([right[-1], left[-1]], gates[s]) if s in gates else [right[-1], left[-1]]
        right.append(line(sent[0], zs, 1))
        left.append(line(sent[1], zs, -1))
    blocks = [value] + [jnp.where(zi >= k, right[k], left[zs - k]) for k in range(1, zs)]
    return blocks, list(zip(right, left))


def true_order(blocks, zs, zi):
    blocks = jnp.stack(blocks[::-1] * 2, axis=0)
    return lax.dynamic_slice_in_dim(blocks, zs - 1 - zi, zs, 0)


def scatter_z(parts, gates={}):
    zs = len(parts)
    right, left = None, None
    steps = []
    for s in range(1, zs):
        go_right = parts[s] if right is None else (parts[s].astype(f32) + right).astype(bf16)
        go_left = parts[zs - s] if left is None else (parts[zs - s].astype(f32) + left).astype(bf16)
        if s in gates:
            go_right, go_left = all_after([go_right, go_left], gates[s](steps))
        got_right, got_left = line(go_right, zs, 1), line(go_left, zs, -1)
        steps.append((got_right, got_left))
        right, left = got_right.astype(f32), got_left.astype(f32)
    return parts[0].astype(f32) + right + left, steps


def swap_core(value):
    return lax.ppermute(value, "c", [(0, 1), (1, 0)])


def both_cores(blocks):
    got = jnp.concatenate(blocks, axis=0)
    return jnp.concatenate([got, swap_core(got)], axis=0)


def mix_cores(parts):
    half = parts.shape[0] // 2
    return (parts[:half].astype(f32) + swap_core(parts[half:]).astype(f32)).astype(bf16)


def z_blocks(mixed, zs):
    block = mixed.shape[0] // zs
    return [mixed[k * block : (k + 1) * block] for k in range(zs)]


BLOCK = 4 * LEN


def kdot(a, b, ca, cb):
    return lax.dot_general(a, b, (((ca,), (cb,)), ((), ())), preferred_element_type=f32)


def to_rows(first, second):
    lane = lax.broadcasted_iota(jnp.int32, (first.shape[0], 128), 1)
    both = jnp.where(lane == 0, first, jnp.where(lane == 1, second, 0.0))
    return both.T[:8]


def to_cols(block):
    cols = jnp.concatenate([block] * 16, axis=0).T
    return cols[:, 0:1], cols[:, 1:2]


def own_rows(half):
    return pl.program_id(0) < half


def picked_rows(half, own_ref, other_ref):
    return jnp.where(own_rows(half), own_ref[...].astype(f32), other_ref[...].astype(f32))


def store_rows(half, own_ref, other_ref, value):
    @pl.when(own_rows(half))
    def _():
        own_ref[...] = value

    @pl.when(jnp.logical_not(own_rows(half)))
    def _():
        other_ref[...] = value


def qkv_kernel(
    width, half, a_own, b_own, a_other, b_other, gain_ref, w_ref, hid_ref, raw_ref, sum_ref
):
    x_a = picked_rows(half, a_own, a_other)
    x_b = picked_rows(half, b_own, b_other)
    square = jnp.sum(x_a * x_a, axis=-1, keepdims=True) + jnp.sum(x_b * x_b, axis=-1, keepdims=True)
    inverse = lax.rsqrt(square / D + NORM_EPS)
    hid_ref[:, : D // 2] = (x_a * inverse * gain_ref[:, : D // 2]).astype(bf16)
    hid_ref[:, D // 2 :] = (x_b * inverse * gain_ref[:, D // 2 :]).astype(bf16)
    raw = kdot(hid_ref[...], w_ref[...], 1, 1)
    raw_ref[...] = raw
    q, k = raw[:, :width], raw[:, width : 2 * width]
    sum_ref[...] = to_rows(
        jnp.sum(q * q, axis=-1, keepdims=True), jnp.sum(k * k, axis=-1, keepdims=True)
    )


def spin(x, cos, sin):
    return x * cos + pltpu.roll(x, HD // 2, 1) * sin


def heads_of(raw, inv_q, inv_k, gain_ref, cos, sin, width, head):
    lo = head * HD
    normed_q = raw[:, lo : lo + HD] * inv_q
    normed_k = raw[:, width + lo : width + lo + HD] * inv_k
    query = spin(normed_q * gain_ref[0:1, lo : lo + HD], cos, sin).astype(bf16)
    key = spin(normed_k * gain_ref[1:2, lo : lo + HD], cos, sin).astype(bf16)
    value = raw[:, 2 * width + lo : 2 * width + lo + HD].astype(bf16)
    return normed_q, normed_k, query, key, value


def probs_of(query, key, mask):
    scores = jnp.where(mask > 0.5, kdot(query, key, 1, 1) * HD ** (-0.5), -1e30)
    scores = jnp.exp(scores - jnp.max(scores, axis=-1, keepdims=True))
    return scores / jnp.sum(scores, axis=-1, keepdims=True)


def inverses(sum_ref):
    ss_q, ss_k = to_cols(sum_ref[...])
    return lax.rsqrt(ss_q / D + NORM_EPS), lax.rsqrt(ss_k / D + NORM_EPS)


def attend_kernel(
    width, half, raw_ref, sum_ref, gain_ref, cos_ref, sin_ref, mask_ref, w_ref,
    att_ref, own_ref, other_ref,
):
    inv_q, inv_k = inverses(sum_ref)
    raw = raw_ref[...]
    cos, sin = cos_ref[...], sin_ref[...]
    for head in range(width // HD):
        _, _, query, key, value = heads_of(raw, inv_q, inv_k, gain_ref, cos, sin, width, head)
        for s in range(BLOCK // LEN):
            at = slice(s * LEN, (s + 1) * LEN)
            probs = probs_of(query[at], key[at], mask_ref[s])
            att_ref[at, head * HD : (head + 1) * HD] = kdot(
                probs.astype(bf16), value[at], 1, 0
            ).astype(bf16)
    store_rows(half, own_ref, other_ref, kdot(att_ref[...], w_ref[...], 1, 1).astype(bf16))


def attend_back_kernel(
    width, half, raw_ref, sum_ref, gain_ref, cos_ref, sin_ref, mask_ref, w_ref, att_ref,
    a_own, b_own, a_other, b_other, back_ref, dv_ref, dot_ref, gsum_ref, gout_ref,
):
    inv_q, inv_k = inverses(sum_ref)
    raw = raw_ref[...]
    cos, sin = cos_ref[...], sin_ref[...]
    grad_a = picked_rows(half, a_own, a_other).astype(bf16)
    grad_b = picked_rows(half, b_own, b_other).astype(bf16)
    grad_heads = kdot(grad_a, w_ref[: D // 2], 1, 0) + kdot(grad_b, w_ref[D // 2 :], 1, 0)
    grad_heads = grad_heads.astype(bf16)

    @pl.when(pl.program_id(0) == 0)
    def _():
        gsum_ref[...] = jnp.zeros_like(gsum_ref)
        gout_ref[...] = jnp.zeros_like(gout_ref)

    gout_ref[: D // 2] += kdot(grad_a, att_ref[...], 0, 0)
    gout_ref[D // 2 :] += kdot(grad_b, att_ref[...], 0, 0)

    dot_q = dot_k = 0.0
    for head in range(width // HD):
        lo = head * HD
        normed_q, normed_k, query, key, value = heads_of(
            raw, inv_q, inv_k, gain_ref, cos, sin, width, head
        )
        grads_q, grads_k = [], []
        for s in range(BLOCK // LEN):
            at = slice(s * LEN, (s + 1) * LEN)
            probs = probs_of(query[at], key[at], mask_ref[s])
            grad = grad_heads[at, lo : lo + HD]
            grad_probs = kdot(grad, value[at], 1, 1)
            dv_ref[at, lo : lo + HD] = kdot(probs.astype(bf16), grad, 0, 0).astype(bf16)
            delta = jnp.sum(probs * grad_probs, axis=-1, keepdims=True)
            grad_scores = (probs * (grad_probs - delta)).astype(bf16)
            grads_q.append(kdot(grad_scores, key[at], 1, 0))
            grads_k.append(kdot(grad_scores, query[at], 0, 0))
        grad_nq = spin(jnp.concatenate(grads_q, axis=0) * HD ** (-0.5), cos, -sin)
        grad_nk = spin(jnp.concatenate(grads_k, axis=0) * HD ** (-0.5), cos, -sin)
        prod_q, prod_k = grad_nq * normed_q, grad_nk * normed_k
        gsum_ref[0:1, lo : lo + HD] += jnp.sum(prod_q, axis=0, keepdims=True)
        gsum_ref[1:2, lo : lo + HD] += jnp.sum(prod_k, axis=0, keepdims=True)
        gain_q, gain_k = gain_ref[0:1, lo : lo + HD], gain_ref[1:2, lo : lo + HD]
        dot_q = dot_q + jnp.sum(prod_q * gain_q, axis=-1, keepdims=True)
        dot_k = dot_k + jnp.sum(prod_k * gain_k, axis=-1, keepdims=True)
        back_ref[:, lo : lo + HD] = grad_nq * gain_q
        back_ref[:, width + lo : width + lo + HD] = grad_nk * gain_k
    dot_ref[...] = to_rows(dot_q, dot_k)


def project_back_kernel(
    width, half, raw_ref, sum_ref, back_ref, dv_ref, dot_ref, w_ref, proj_ref, own_ref, other_ref
):
    inv_q, inv_k = inverses(sum_ref)
    mean_q, mean_k = to_cols(dot_ref[...] / D)
    normed_q = raw_ref[:, :width] * inv_q
    normed_k = raw_ref[:, width : 2 * width] * inv_k
    proj_ref[:, :width] = (inv_q * (back_ref[:, :width] - normed_q * mean_q)).astype(bf16)
    proj_ref[:, width : 2 * width] = (
        inv_k * (back_ref[:, width:] - normed_k * mean_k)
    ).astype(bf16)
    proj_ref[:, 2 * width :] = dv_ref[...]
    store_rows(half, own_ref, other_ref, kdot(proj_ref[...], w_ref[...], 1, 0).astype(bf16))


def by_rows(cols):
    return pl.BlockSpec((BLOCK, cols), lambda i: (i, 0))


def pieces_spec(half, cols):
    own = pl.BlockSpec((BLOCK, cols), lambda i: (jnp.minimum(i, half - 1), 0))
    other = pl.BlockSpec((BLOCK, cols), lambda i: (jnp.maximum(i - half, 0), 0))
    return own, other


def across(rows):
    return pl.BlockSpec((rows, BLOCK), lambda i: (0, i))


def whole(shape):
    return pl.BlockSpec(shape, lambda i: (0,) * len(shape))


def run_blocks(body, rows, in_specs, out_specs, out_shape, args):
    return pl.pallas_call(
        body,
        grid=(rows // BLOCK,),
        in_specs=in_specs,
        out_specs=out_specs,
        out_shape=out_shape,
        cost_estimate=pl.CostEstimate(flops=1, bytes_accessed=1, transcendentals=0),
    )(*args)


def weight_grad_kernel(a_ref, b_ref, out_ref):
    out_ref[...] = kdot(a_ref[...], b_ref[...], 0, 0).astype(bf16)


def weight_grad(a, b):
    tile_a, tile_b = 512, 1024
    return pl.pallas_call(
        weight_grad_kernel,
        grid=(b.shape[1] // tile_b, a.shape[1] // tile_a),
        in_specs=[
            pl.BlockSpec((a.shape[0], tile_a), lambda n, m: (0, m)),
            pl.BlockSpec((b.shape[0], tile_b), lambda n, m: (0, n)),
        ],
        out_specs=pl.BlockSpec((tile_a, tile_b), lambda n, m: (m, n)),
        out_shape=jax.ShapeDtypeStruct((a.shape[1], b.shape[1]), bf16),
        cost_estimate=pl.CostEstimate(flops=1, bytes_accessed=1, transcendentals=0),
    )(a, b)


def shape_of(rows, cols, dtype):
    return jax.ShapeDtypeStruct((rows, cols), dtype)


def per_device(
    tokens, cotangent, segments, routes, w_qkv, w_out, norm_gains, w_router, w_gate_up, w_down
):
    zs = lax.axis_size("z")
    dps = lax.axis_size("q") * 2
    world = dps * zs
    qi, ci, zi = lax.axis_index("q"), lax.axis_index("c"), lax.axis_index("z")
    di = qi * 2 + ci
    rows = tokens.shape[0]
    seqs = rows // LEN
    width = D // dps
    local_experts = E // zs
    mine = local_experts // 2
    sub = w_qkv.shape[0] // 3
    orow = w_out.shape[0]
    all_rows = dps * rows
    all_seqs = dps * seqs

    def unit_perm(t, back):
        pairs = []
        for i in range(dps):
            for j in range(zs):
                dest = (3 * i + (3 * j + t) // zs) % dps
                src_dev, dst_dev = i * zs + j, dest * zs + j
                pairs.append((dst_dev, src_dev) if back else (src_dev, dst_dev))
        return pairs

    moved = [
        lax.ppermute(w_qkv[t * sub : (t + 1) * sub], ALL, unit_perm(t, False)) for t in range(3)
    ]
    slots, slot_steps = gather_z(jnp.concatenate(moved, axis=0), zs, zi)
    tok_pieces = gather_dp(tokens, dps)
    inv3 = pow(3, -1, dps)
    slot_of = [[0, 0, 0] for _ in range(dps)]
    type_of = [[0, 0, 0] for _ in range(dps)]
    for i in range(dps):
        for s in range(3):
            src = (inv3 * (i - s)) % dps
            kind = (3 * src + s) // dps
            slot_of[i][kind] = s
            type_of[i][s] = kind
    slot_of = jnp.asarray(slot_of, jnp.int32)[di]
    type_of = jnp.asarray(type_of, jnp.int32)[di]

    mini = jnp.concatenate(
        [
            norm_gains.reshape(-1),
            w_router.reshape(-1),
            segments.astype(bf16).reshape(-1),
            routes.astype(bf16).reshape(-1),
        ]
    )
    mini = after(mini, *slot_steps[1])
    minis = lax.all_to_all(
        jnp.broadcast_to(mini[None], (world,) + mini.shape), ALL, 0, 0, tiled=True
    )
    at = 0
    split = []
    for part in (norm_gains, w_router, segments, routes):
        split.append(minis[:, at : at + part.size])
        at += part.size
    gains_f = split[0].reshape(D, 4).astype(f32)
    router_low = split[1].reshape(D, E)
    router_f = router_low.astype(f32)
    seg_all = split[2].reshape(dps, zs, seqs, LEN)
    seg_own = lax.dynamic_index_in_dim(seg_all, zi, 1, keepdims=False)
    seg_own = seg_own[jnp.asarray(relative(dps)) ^ di].reshape(all_seqs, LEN)
    routes_all = split[3].reshape(dps // 2, 2, zs, rows, TOP)
    routes_own = lax.dynamic_index_in_dim(routes_all, qi, 0, keepdims=False)
    routes_own = routes_own[jnp.stack([ci, 1 - ci])][:, (zi - jnp.arange(zs)) % zs]
    routes_g = routes_own.reshape(2 * zs * rows, TOP).astype(jnp.int32)
    position = jnp.arange(LEN)
    causal = position[:, None] >= position[None, :]
    mask = (causal[None] & (seg_own[:, :, None] == seg_own[:, None, :])).astype(f32)
    own_gains = lax.dynamic_slice(gains_f, (di * width, 0), (width, 4))
    gain_rows = jnp.pad(own_gains[:, 1:3].T, ((0, 6), (0, 0)))
    cos_table, sin_table = rope_tables(LEN, HD)
    cos_full = jnp.tile(jnp.concatenate([cos_table, cos_table], axis=1), (BLOCK // LEN, 1))
    sin_full = jnp.tile(jnp.concatenate([-sin_table, sin_table], axis=1), (BLOCK // LEN, 1))

    qkv_slots = true_order(slots, zs, zi).reshape(3, width, D)
    w_three = jnp.concatenate(
        [lax.dynamic_index_in_dim(qkv_slots, slot_of[k], 0, keepdims=False) for k in range(3)],
        axis=0,
    )
    out_cols = lax.all_to_all(
        after(w_out, *slot_steps[1]).reshape(orow, dps, width).transpose(1, 0, 2),
        DP, 0, 0, tiled=True,
    )
    out_blocks, out_w_steps = gather_z(after(out_cols, *slot_steps[-1]), zs, zi)
    w_out_c = true_order(out_blocks, zs, zi).transpose(1, 0, 2, 3).reshape(D, width)
    dy_blocks, dy_steps = gather_z(after(cotangent, *out_w_steps[-1]), zs, zi)

    def in_core_order(own, got):
        first = ci == 0
        return jnp.where(first, own, got), jnp.where(first, got, own)

    def core_half(weight):
        split = weight.reshape((2, mine) + weight.shape[1:])
        got = swap_core(lax.dynamic_index_in_dim(split, 1 - ci, 0, keepdims=False))
        own = lax.dynamic_index_in_dim(split, ci, 0, keepdims=False)
        both = in_core_order(own, got)
        return [jnp.concatenate([half[e] for half in both], axis=0) for e in range(mine)]

    gu_half = core_half(after(w_gate_up, *moved))
    down_half = core_half(after(w_down, *moved))
    blocks = all_rows // BLOCK
    half = blocks // 2
    own_spec, other_spec = pieces_spec(half, D // 2)
    piece_specs = [own_spec, own_spec, other_spec, other_spec]
    part_specs = list(pieces_spec(half, D))
    part_shapes = [shape_of(all_rows // 2, D, bf16)] * 2
    hidden_one, raw, sums = run_blocks(
        functools.partial(qkv_kernel, width, half),
        all_rows,
        piece_specs + [whole((1, D)), whole((3 * width, D))],
        [by_rows(D), by_rows(3 * width), across(8)],
        [
            shape_of(all_rows, D, bf16),
            shape_of(all_rows, 3 * width, f32),
            shape_of(8, all_rows, f32),
        ],
        tuple(tok_pieces) + (gains_f[:, 0][None], w_three),
    )
    sums = sum_dp(sums, dps)
    mask_spec = pl.BlockSpec((BLOCK // LEN, LEN, LEN), lambda i: (i, 0, 0))
    table_specs = [whole((8, width)), whole((BLOCK, HD)), whole((BLOCK, HD)), mask_spec]
    tables = (gain_rows, cos_full, sin_full, mask)
    attended, own, other = run_blocks(
        functools.partial(attend_kernel, width, half),
        all_rows,
        [by_rows(3 * width), across(8)] + table_specs + [whole((D, width))],
        [by_rows(width)] + part_specs,
        [shape_of(all_rows, width, bf16)] + part_shapes,
        (raw, sums) + tables + (w_out_c,),
    )
    attn_out, _, attn_last = scatter_dp(own, other, dps)

    expert_w = []
    for e in range(mine):
        if e > 0:
            gu_half[e], down_half[e] = all_after([gu_half[e], down_half[e]], attn_last)
        expert_w.append(
            (
                lax.all_gather(gu_half[e], "q", axis=0, tiled=True),
                lax.all_gather(down_half[e], "q", axis=0, tiled=True),
            )
        )

    x_float = tokens.astype(f32)
    inverse_one = inverse_rms(x_float)
    normed_one = x_float * inverse_one
    residual = x_float + attn_out
    inverse_two = inverse_rms(residual)
    normed_two = residual * inverse_two
    hidden_two = (normed_two * gains_f[:, 3]).astype(bf16)
    router_probs = jax.nn.softmax(mm(hidden_two, router_low, 1, 0), axis=-1)

    dy_g = both_cores(dy_blocks)
    hidden_blocks, _ = gather_z(after(hidden_two, *dy_steps[-1]), zs, zi, {2: [dy_g, router_probs]})
    hidden_g = both_cores(hidden_blocks)
    router_g = jax.nn.softmax(mm(hidden_g, router_low, 1, 0), axis=-1)
    dy_f = dy_g.astype(f32)
    first_expert = zi * local_experts + ci * mine

    early = [w for pair in expert_w for w in pair]
    early = list(lax.optimization_barrier(tuple(early[:-1]))) + early[-1:]
    expert_w = [tuple(early[2 * e : 2 * e + 2]) for e in range(mine)]

    passes = []
    for e in range(mine):
        gate_up, down = expert_w[e]
        expert = first_expert + e
        picked = jnp.any(routes_g == expert, axis=1, keepdims=True)
        prob = jnp.sum(
            jnp.where(jnp.arange(E)[None] == expert, router_g, 0.0), axis=1, keepdims=True
        )
        gate_val = jnp.where(picked, prob, 0.0)
        hidden_e = after(hidden_g, passes[-1]["act"]) if passes else hidden_g
        gate_and_up = mm(hidden_e, gate_up, 1, 1)
        g_part = gate_and_up[:, :FF]
        u_part = gate_and_up[:, FF:]
        sig = jax.nn.sigmoid(g_part)
        silu = g_part * sig
        act = (silu * u_part).astype(bf16)
        expert_out = mm(act, down, 1, 1).astype(bf16).astype(f32)
        grad_gate = jnp.where(picked[:, 0], jnp.sum(dy_f * expert_out, axis=1), 0.0)
        grad_eo = (gate_val * dy_f).astype(bf16)
        grad_act = mm(grad_eo, down, 1, 0)
        grad_g = grad_act * u_part * sig * (1.0 + g_part * (1.0 - sig))
        grad_u = grad_act * silu
        grad_both = jnp.concatenate([grad_g, grad_u], axis=-1).astype(bf16)
        rows_back = mm(grad_both, gate_up, 1, 0).astype(bf16).astype(f32)
        dn = mm(grad_eo, act, 0, 0).astype(bf16)
        passes.append(
            dict(
                out=gate_val * expert_out,
                back=rows_back,
                gate=grad_gate,
                both=grad_both,
                act=act,
                dn=lax.psum_scatter(dn, "q", scatter_dimension=0, tiled=True),
            )
        )

    hid_part = sum([p["back"] for p in passes[1:]], passes[0]["back"])
    out_part = sum([p["out"] for p in passes[1:]], passes[0]["out"])
    cols = jnp.stack([p["gate"] for p in passes], axis=0).reshape(mine, 2, zs, rows)
    cols = jnp.where(ci == 0, cols, cols[:, ::-1])
    cols = cols[:, :, (zi - jnp.arange(zs)) % zs]
    hid_mixed = mix_cores(hid_part.astype(bf16))
    out_mixed = mix_cores(out_part.astype(bf16))
    gus = []

    def fill(*deps):
        p = passes[len(gus)]
        gus.append(weight_grad(after(p["both"], *deps), hidden_g))
        return gus[-1:]

    hid_gates = {2: lambda steps: fill(hid_mixed), 3: lambda steps: [cols, out_mixed]}
    if mine > 1:
        hid_gates[3] = lambda steps: fill(*steps[0]) + [cols, out_mixed]
    hid_sum, hid_steps = scatter_z(z_blocks(hid_mixed, zs), hid_gates)
    while len(gus) < mine:
        fill(*hid_steps[1])
    grad_hidden = hid_sum
    got = lax.all_to_all(
        cols.transpose(1, 2, 0, 3).reshape(2 * zs, mine, rows), ("c", "z"), 0, 0, tiled=True
    )
    gp = got.reshape(2, zs, mine, rows).transpose(1, 0, 2, 3).reshape(E, rows).T

    grad_logits = router_probs * (gp - jnp.sum(router_probs * gp, axis=-1, keepdims=True))
    grad_router = lax.dot_general(
        hidden_two.astype(f32), grad_logits, (((0,), (0,)), ((), ())), precision=PRECISE
    )
    grad_hidden = grad_hidden + jnp.dot(grad_logits, router_f.T, precision=PRECISE)
    gain_two = jnp.sum(grad_hidden * normed_two, axis=0)
    grad_residual = cotangent.astype(f32) + norm_back(
        grad_hidden * gains_f[:, 3], normed_two, inverse_two
    )

    def core_back(parts):
        stacked = jnp.stack(parts, axis=0)
        split = stacked.reshape((mine, 2, stacked.shape[1] // 2, stacked.shape[2]))
        got = swap_core(lax.dynamic_index_in_dim(split, 1 - ci, 1, keepdims=False))
        own = lax.dynamic_index_in_dim(split, ci, 1, keepdims=False)
        return jnp.concatenate(in_core_order(own, got), axis=0).astype(f32)

    grad_pieces = []

    def out_gate(steps):
        if len(steps) == 1:
            grad_pieces.extend(
                gather_dp(grad_residual.astype(bf16), dps, gate=gus[-1:] + list(steps[0]))
            )
        return []

    out_total, out_steps = scatter_z(
        z_blocks(after(out_mixed, *hid_steps[-1]), zs), {s: out_gate for s in range(2, zs)}
    )
    gus = [after(gu, *hid_steps[0]) for gu in gus[:-1]] + [after(gus[-1], *grad_pieces)]
    gus = [lax.psum_scatter(gu, "q", scatter_dimension=0, tiled=True) for gu in gus]
    back, dv, dots, gain_sums, grad_out_c = run_blocks(
        functools.partial(attend_back_kernel, width, half),
        all_rows,
        [by_rows(3 * width), across(8)] + table_specs + [whole((D, width)), by_rows(width)]
        + piece_specs,
        [by_rows(2 * width), by_rows(width), across(8), whole((8, width)), whole((D, width))],
        [
            shape_of(all_rows, 2 * width, f32),
            shape_of(all_rows, width, bf16),
            shape_of(8, all_rows, f32),
            shape_of(8, width, f32),
            shape_of(D, width, f32),
        ],
        (raw, sums) + tables + (w_out_c, attended) + tuple(grad_pieces),
    )

    def z_parts(value):
        return [
            lax.dynamic_index_in_dim(value, (zi - k) % zs, 0, keepdims=False) for k in range(zs)
        ]

    dots = sum_dp(after(dots, *out_steps[1]), dps)
    grad_projected, own, other = run_blocks(
        functools.partial(project_back_kernel, width, half),
        all_rows,
        [
            by_rows(3 * width), across(8), by_rows(2 * width), by_rows(width), across(8),
            whole((3 * width, D)),
        ],
        [by_rows(3 * width)] + part_specs,
        [shape_of(all_rows, 3 * width, bf16)] + part_shapes,
        (raw, sums, back, dv, dots, w_three),
    )
    grad_h1, h1_summed, h1_last = scatter_dp(own, other, dps)
    gain_one = jnp.sum(grad_h1 * normed_one, axis=0)
    grad_tokens = grad_residual + norm_back(grad_h1 * gains_f[:, 0], normed_one, inverse_one)
    result = residual + out_total

    hidden_late = after(hidden_one, *out_steps[-1])
    grad_three = mm(grad_projected, hidden_late, 0, 0).astype(bf16).reshape(3, width, D)
    grad_slots = jnp.concatenate(
        [lax.dynamic_index_in_dim(grad_three, type_of[s], 0, keepdims=True) for s in range(3)],
        axis=0,
    )
    grad_cols = grad_out_c.astype(bf16).reshape(dps, zs, orow, width).transpose(1, 2, 0, 3)
    parts = jnp.concatenate(
        [grad_slots.reshape(zs, 3 * sub, D), grad_cols.reshape(zs, orow, D)], axis=1
    )
    dns = [p["dn"] for p in passes]
    grad_down = core_back([after(dns[0], grad_projected)] + dns[1:])
    own_sum, own_steps = scatter_z(z_parts(parts), {1: lambda steps: [h1_summed]})
    grad_gate_up = core_back([after(gus[0], *own_steps[1])] + gus[1:])
    own_sum = after(own_sum.astype(bf16), grad_gate_up, grad_down)
    grad_qkv = jnp.concatenate(
        [
            lax.ppermute(own_sum[t * sub : (t + 1) * sub], ALL, unit_perm(t, True))
            for t in range(3)
        ],
        axis=0,
    ).astype(f32)
    own_cols = own_sum[3 * sub :].reshape(orow, dps, width).transpose(1, 0, 2)
    grad_out = (
        lax.all_to_all(own_cols, DP, 0, 0, tiled=True)
        .transpose(1, 0, 2)
        .reshape(orow, D)
        .astype(f32)
    )

    shard_cols = lax.dynamic_update_slice(jnp.zeros((D, 2), f32), gain_sums[:2].T, (di * width, 0))
    small_grads = jnp.concatenate(
        [gain_one[:, None], shard_cols, gain_two[:, None], grad_router], axis=1
    )
    small_own = jnp.sum(
        lax.all_to_all(
            small_grads.reshape(world, D * (E + 4) // world), ALL, 0, 0, tiled=True
        ),
        axis=0,
    ).reshape(D // world, E + 4)

    return (
        result.astype(bf16),
        grad_tokens,
        grad_qkv,
        grad_out,
        small_own[:, :4],
        small_own[:, 4:],
        grad_gate_up,
        grad_down,
    )


def solution(mesh):
    dps, zs = mesh.shape["dp"], mesh.shape["fsdp"]
    inner = Mesh(mesh.devices.reshape(dps // 2, 2, zs), ALL)
    rows = P(ALL, None)
    experts = P("z", DP, None)
    in_specs = (rows,) * 8 + (experts,) * 2
    out_specs = (rows,) * 6 + (experts,) * 2
    return jax.shard_map(
        per_device, mesh=inner, in_specs=in_specs, out_specs=out_specs, check_vma=False
    )
```

```python
import functools

import jax
import jax.numpy as jnp
from jax import lax
from jax.experimental import pallas as pl
from jax.experimental.pallas import tpu as pltpu
from jax.sharding import Mesh
from jax.sharding import PartitionSpec as P

D = 2048
H = 16
HD = 128
FF = 1024
TOP = 8
E = 16
LEN = 96

NORM_EPS = 1e-05
ROPE_BASE = 10000.0
PRECISE = lax.Precision.HIGHEST
DP = ("q", "c")
ALL = ("q", "c", "z")
f32 = jnp.float32
bf16 = jnp.bfloat16


def inverse_rms(field_in):
    return lax.rsqrt(jnp.mean(field_in * field_in, axis=-1, keepdims=True) + NORM_EPS)


def rope_tables(length, head_dim):
    half_dim = head_dim // 2
    frequency = ROPE_BASE ** (-(jnp.arange(half_dim).astype(f32) * 2.0) / head_dim)
    angles = jnp.arange(length).astype(f32)[:, None] * frequency[None, :]
    return jnp.cos(angles), jnp.sin(angles)


def norm_back(grad_normed, normed, inverse):
    return inverse * (grad_normed - normed * jnp.mean(grad_normed * normed, axis=-1, keepdims=True))


def mm(a, b, ca, cb):
    return lax.dot_general(a, b, (((ca,), (cb,)), ((), ())), preferred_element_type=f32)


def after(value, *deps):
    return lax.optimization_barrier((value,) + tuple(deps))[0]


def flip(value, size, bit):
    return lax.ppermute(value, DP, [(i, i ^ (1 << bit)) for i in range(size)])


def relative(size):
    return [high * 2 + core for core in range(2) for high in range(size // 2)]


def bit_lists(size):
    high = list(range(1, size.bit_length() - 1))
    return high, high[::-1]


def gather_dp(value, size, gate=()):
    width = value.shape[-1] // 2
    pieces = []
    for part, order in zip((value[:, :width], value[:, width:]), bit_lists(size)):
        out, have = part, []
        for bit in order:
            axis = sum(1 for other in have if other > bit)
            out = jnp.stack([out, flip(out, size, bit)], axis=axis)
            have.append(bit)
        pieces.append(out.reshape(-1, width))
    sent = [after(piece, *gate) for piece in pieces] if gate else pieces
    return pieces + [flip(piece, size, 0) for piece in sent]


def scatter_dp(own, other, size):
    rows, width = own.shape[0] * 2 // size, own.shape[1]
    got = flip(other, size, 0)
    summed = (own.astype(f32) + got.astype(f32)).astype(bf16)
    highs = size.bit_length() - 2
    halves, last = [], []
    for half, order in enumerate(bit_lists(size)):
        cur = summed[:, half * (width // 2) : (half + 1) * (width // 2)]
        cur = cur.reshape([2] * highs + [rows, width // 2])
        left = list(range(highs, 0, -1))
        for k, bit in enumerate(order):
            axis = left.index(bit)
            left.remove(bit)
            keep = lax.index_in_dim(cur, 0, axis, keepdims=False)
            send = lax.index_in_dim(cur, 1, axis, keepdims=False)
            brought = flip(send, size, bit)
            total = keep.astype(f32) + brought.astype(f32)
            cur = total if k == len(order) - 1 else total.astype(bf16)
        halves.append(cur)
        last.append(brought)
    return jnp.concatenate(halves, axis=-1), summed, last


def sum_dp(value, size):
    count = size.bit_length() - 1
    shape = value.shape
    value = value[:2].reshape((2,) + (2,) * count + (-1,))
    for bit in range(count):
        value = value + jnp.flip(flip(value, size, bit), 1 if bit == 0 else count - bit + 1)
    return jnp.pad(value.reshape(2, shape[1]), ((0, 6), (0, 0)))


def line(value, zs, step):
    return lax.ppermute(value, "z", [(j, j + step) for j in range(zs) if 0 <= j + step < zs])


def all_after(values, deps):
    return list(lax.optimization_barrier(tuple(values) + tuple(deps))[: len(values)])


def gather_z(value, zs, zi, gates={}):
    right, left = [value], [value]
    for s in range(1, zs):
        sent = all_after([right[-1], left[-1]], gates[s]) if s in gates else [right[-1], left[-1]]
        right.append(line(sent[0], zs, 1))
        left.append(line(sent[1], zs, -1))
    blocks = [value] + [jnp.where(zi >= k, right[k], left[zs - k]) for k in range(1, zs)]
    return blocks, list(zip(right, left))


def true_order(blocks, zs, zi):
    out = jnp.zeros((zs,) + blocks[0].shape, blocks[0].dtype)
    for k, block in enumerate(blocks):
        out = lax.dynamic_update_index_in_dim(out, block, (zi - k) % zs, 0)
    return out


def scatter_z(parts, gates={}):
    zs = len(parts)
    right, left = None, None
    steps = []
    for s in range(1, zs):
        go_right = parts[s] if right is None else (parts[s].astype(f32) + right).astype(bf16)
        go_left = parts[zs - s] if left is None else (parts[zs - s].astype(f32) + left).astype(bf16)
        if s in gates:
            go_right, go_left = all_after([go_right, go_left], gates[s](steps))
        got_right, got_left = line(go_right, zs, 1), line(go_left, zs, -1)
        steps.append((got_right, got_left))
        right, left = got_right.astype(f32), got_left.astype(f32)
    return parts[0].astype(f32) + right + left, steps


def swap_core(value):
    return lax.ppermute(value, "c", [(0, 1), (1, 0)])


def both_cores(blocks):
    got = jnp.concatenate(blocks, axis=0)
    return jnp.concatenate([got, swap_core(got)], axis=0)


def mix_cores(parts):
    half = parts.shape[0] // 2
    return (parts[:half].astype(f32) + swap_core(parts[half:]).astype(f32)).astype(bf16)


def z_blocks(mixed, zs):
    block = mixed.shape[0] // zs
    return [mixed[k * block : (k + 1) * block] for k in range(zs)]


BLOCK = 4 * LEN


def kdot(a, b, ca, cb):
    return lax.dot_general(a, b, (((ca,), (cb,)), ((), ())), preferred_element_type=f32)


def to_rows(first, second):
    lane = lax.broadcasted_iota(jnp.int32, (first.shape[0], 128), 1)
    both = jnp.where(lane == 0, first, jnp.where(lane == 1, second, 0.0))
    return both.T[:8]


def to_cols(block):
    cols = jnp.concatenate([block] * 16, axis=0).T
    return cols[:, 0:1], cols[:, 1:2]


def own_rows(half):
    return pl.program_id(0) < half


def picked_rows(half, own_ref, other_ref):
    return jnp.where(own_rows(half), own_ref[...].astype(f32), other_ref[...].astype(f32))


def store_rows(half, own_ref, other_ref, value):
    @pl.when(own_rows(half))
    def _():
        own_ref[...] = value

    @pl.when(jnp.logical_not(own_rows(half)))
    def _():
        other_ref[...] = value


def qkv_kernel(
    width, half, a_own, b_own, a_other, b_other, gain_ref, w_ref, hid_ref, raw_ref, sum_ref
):
    x_a = picked_rows(half, a_own, a_other)
    x_b = picked_rows(half, b_own, b_other)
    square = jnp.sum(x_a * x_a, axis=-1, keepdims=True) + jnp.sum(x_b * x_b, axis=-1, keepdims=True)
    inverse = lax.rsqrt(square / D + NORM_EPS)
    hid_ref[:, : D // 2] = (x_a * inverse * gain_ref[:, : D // 2]).astype(bf16)
    hid_ref[:, D // 2 :] = (x_b * inverse * gain_ref[:, D // 2 :]).astype(bf16)
    raw = kdot(hid_ref[...], w_ref[...], 1, 1)
    raw_ref[...] = raw
    q, k = raw[:, :width], raw[:, width : 2 * width]
    sum_ref[...] = to_rows(
        jnp.sum(q * q, axis=-1, keepdims=True), jnp.sum(k * k, axis=-1, keepdims=True)
    )


def spin(x, cos, sin):
    return x * cos + pltpu.roll(x, HD // 2, 1) * sin


def heads_of(raw, inv_q, inv_k, gain_ref, cos, sin, width, head):
    lo = head * HD
    normed_q = raw[:, lo : lo + HD] * inv_q
    normed_k = raw[:, width + lo : width + lo + HD] * inv_k
    query = spin(normed_q * gain_ref[0:1, lo : lo + HD], cos, sin).astype(bf16)
    key = spin(normed_k * gain_ref[1:2, lo : lo + HD], cos, sin).astype(bf16)
    value = raw[:, 2 * width + lo : 2 * width + lo + HD].astype(bf16)
    return normed_q, normed_k, query, key, value


def probs_of(query, key, mask):
    scores = jnp.where(mask > 0.5, kdot(query, key, 1, 1) * HD ** (-0.5), -1e30)
    scores = jnp.exp(scores - jnp.max(scores, axis=-1, keepdims=True))
    return scores / jnp.sum(scores, axis=-1, keepdims=True)


def inverses(sum_ref):
    ss_q, ss_k = to_cols(sum_ref[...])
    return lax.rsqrt(ss_q / D + NORM_EPS), lax.rsqrt(ss_k / D + NORM_EPS)


def attend_kernel(
    width, half, raw_ref, sum_ref, gain_ref, cos_ref, sin_ref, mask_ref, w_ref,
    att_ref, own_ref, other_ref,
):
    inv_q, inv_k = inverses(sum_ref)
    raw = raw_ref[...]
    cos, sin = cos_ref[...], sin_ref[...]
    for head in range(width // HD):
        _, _, query, key, value = heads_of(raw, inv_q, inv_k, gain_ref, cos, sin, width, head)
        for s in range(BLOCK // LEN):
            at = slice(s * LEN, (s + 1) * LEN)
            probs = probs_of(query[at], key[at], mask_ref[s])
            att_ref[at, head * HD : (head + 1) * HD] = kdot(
                probs.astype(bf16), value[at], 1, 0
            ).astype(bf16)
    store_rows(half, own_ref, other_ref, kdot(att_ref[...], w_ref[...], 1, 1).astype(bf16))


def attend_back_kernel(
    width, half, raw_ref, sum_ref, gain_ref, cos_ref, sin_ref, mask_ref, w_ref, att_ref,
    a_own, b_own, a_other, b_other, back_ref, dv_ref, dot_ref, gsum_ref, gout_ref,
):
    inv_q, inv_k = inverses(sum_ref)
    raw = raw_ref[...]
    cos, sin = cos_ref[...], sin_ref[...]
    grad_a = picked_rows(half, a_own, a_other).astype(bf16)
    grad_b = picked_rows(half, b_own, b_other).astype(bf16)
    grad_heads = kdot(grad_a, w_ref[: D // 2], 1, 0) + kdot(grad_b, w_ref[D // 2 :], 1, 0)
    grad_heads = grad_heads.astype(bf16)

    @pl.when(pl.program_id(0) == 0)
    def _():
        gsum_ref[...] = jnp.zeros_like(gsum_ref)
        gout_ref[...] = jnp.zeros_like(gout_ref)

    gout_ref[: D // 2] += kdot(grad_a, att_ref[...], 0, 0)
    gout_ref[D // 2 :] += kdot(grad_b, att_ref[...], 0, 0)

    dot_q = dot_k = 0.0
    for head in range(width // HD):
        lo = head * HD
        normed_q, normed_k, query, key, value = heads_of(
            raw, inv_q, inv_k, gain_ref, cos, sin, width, head
        )
        grads_q, grads_k = [], []
        for s in range(BLOCK // LEN):
            at = slice(s * LEN, (s + 1) * LEN)
            probs = probs_of(query[at], key[at], mask_ref[s])
            grad = grad_heads[at, lo : lo + HD]
            grad_probs = kdot(grad, value[at], 1, 1)
            dv_ref[at, lo : lo + HD] = kdot(probs.astype(bf16), grad, 0, 0).astype(bf16)
            delta = jnp.sum(probs * grad_probs, axis=-1, keepdims=True)
            grad_scores = (probs * (grad_probs - delta)).astype(bf16)
            grads_q.append(kdot(grad_scores, key[at], 1, 0))
            grads_k.append(kdot(grad_scores, query[at], 0, 0))
        grad_nq = spin(jnp.concatenate(grads_q, axis=0) * HD ** (-0.5), cos, -sin)
        grad_nk = spin(jnp.concatenate(grads_k, axis=0) * HD ** (-0.5), cos, -sin)
        prod_q, prod_k = grad_nq * normed_q, grad_nk * normed_k
        gsum_ref[0:1, lo : lo + HD] += jnp.sum(prod_q, axis=0, keepdims=True)
        gsum_ref[1:2, lo : lo + HD] += jnp.sum(prod_k, axis=0, keepdims=True)
        gain_q, gain_k = gain_ref[0:1, lo : lo + HD], gain_ref[1:2, lo : lo + HD]
        dot_q = dot_q + jnp.sum(prod_q * gain_q, axis=-1, keepdims=True)
        dot_k = dot_k + jnp.sum(prod_k * gain_k, axis=-1, keepdims=True)
        back_ref[:, lo : lo + HD] = grad_nq * gain_q
        back_ref[:, width + lo : width + lo + HD] = grad_nk * gain_k
    dot_ref[...] = to_rows(dot_q, dot_k)


def project_back_kernel(
    width, half, raw_ref, sum_ref, back_ref, dv_ref, dot_ref, w_ref, proj_ref, own_ref, other_ref
):
    inv_q, inv_k = inverses(sum_ref)
    mean_q, mean_k = to_cols(dot_ref[...] / D)
    normed_q = raw_ref[:, :width] * inv_q
    normed_k = raw_ref[:, width : 2 * width] * inv_k
    proj_ref[:, :width] = (inv_q * (back_ref[:, :width] - normed_q * mean_q)).astype(bf16)
    proj_ref[:, width : 2 * width] = (
        inv_k * (back_ref[:, width:] - normed_k * mean_k)
    ).astype(bf16)
    proj_ref[:, 2 * width :] = dv_ref[...]
    store_rows(half, own_ref, other_ref, kdot(proj_ref[...], w_ref[...], 1, 0).astype(bf16))


def by_rows(cols):
    return pl.BlockSpec((BLOCK, cols), lambda i: (i, 0))


def pieces_spec(half, cols):
    own = pl.BlockSpec((BLOCK, cols), lambda i: (jnp.minimum(i, half - 1), 0))
    other = pl.BlockSpec((BLOCK, cols), lambda i: (jnp.maximum(i - half, 0), 0))
    return own, other


def across(rows):
    return pl.BlockSpec((rows, BLOCK), lambda i: (0, i))


def whole(shape):
    return pl.BlockSpec(shape, lambda i: (0,) * len(shape))


def run_blocks(body, rows, in_specs, out_specs, out_shape, args):
    return pl.pallas_call(
        body,
        grid=(rows // BLOCK,),
        in_specs=in_specs,
        out_specs=out_specs,
        out_shape=out_shape,
        cost_estimate=pl.CostEstimate(flops=1, bytes_accessed=1, transcendentals=0),
    )(*args)


def weight_grad_kernel(half, g_ref, u_ref, b_ref, out_ref):
    @pl.when(pl.program_id(1) < half)
    def _():
        out_ref[...] = kdot(g_ref[...], b_ref[...], 0, 0).astype(bf16)

    @pl.when(pl.program_id(1) >= half)
    def _():
        out_ref[...] = kdot(u_ref[...], b_ref[...], 0, 0).astype(bf16)


def weight_grad(g, u, b):
    tile_a, tile_b = 512, 1024
    half = g.shape[1] // tile_a
    return pl.pallas_call(
        functools.partial(weight_grad_kernel, half),
        grid=(b.shape[1] // tile_b, 2 * half),
        in_specs=[
            pl.BlockSpec((g.shape[0], tile_a), lambda n, m: (0, jnp.minimum(m, half - 1))),
            pl.BlockSpec((u.shape[0], tile_a), lambda n, m: (0, jnp.maximum(m - half, 0))),
            pl.BlockSpec((b.shape[0], tile_b), lambda n, m: (0, n)),
        ],
        out_specs=pl.BlockSpec((tile_a, tile_b), lambda n, m: (m, n)),
        out_shape=jax.ShapeDtypeStruct((2 * g.shape[1], b.shape[1]), bf16),
        cost_estimate=pl.CostEstimate(flops=1, bytes_accessed=1, transcendentals=0),
    )(g, u, b)


def shape_of(rows, cols, dtype):
    return jax.ShapeDtypeStruct((rows, cols), dtype)


def per_device(
    tokens, cotangent, segments, routes, w_qkv, w_out, norm_gains, w_router, w_gate_up, w_down
):
    zs = lax.axis_size("z")
    dps = lax.axis_size("q") * 2
    world = dps * zs
    qi, ci, zi = lax.axis_index("q"), lax.axis_index("c"), lax.axis_index("z")
    di = qi * 2 + ci
    rows = tokens.shape[0]
    seqs = rows // LEN
    width = D // dps
    local_experts = E // zs
    mine = local_experts // 2
    sub = w_qkv.shape[0] // 3
    orow = w_out.shape[0]
    all_rows = dps * rows
    all_seqs = dps * seqs

    def unit_perm(t, back):
        pairs = []
        for i in range(dps):
            for j in range(zs):
                dest = (3 * i + (3 * j + t) // zs) % dps
                src_dev, dst_dev = i * zs + j, dest * zs + j
                pairs.append((dst_dev, src_dev) if back else (src_dev, dst_dev))
        return pairs

    moved = [
        lax.ppermute(w_qkv[t * sub : (t + 1) * sub], ALL, unit_perm(t, False)) for t in range(3)
    ]
    slots, slot_steps = gather_z(jnp.concatenate(moved, axis=0), zs, zi)
    tok_pieces = gather_dp(tokens, dps)
    inv3 = pow(3, -1, dps)
    slot_of = [[0, 0, 0] for _ in range(dps)]
    type_of = [[0, 0, 0] for _ in range(dps)]
    for i in range(dps):
        for s in range(3):
            src = (inv3 * (i - s)) % dps
            kind = (3 * src + s) // dps
            slot_of[i][kind] = s
            type_of[i][s] = kind
    slot_of = jnp.asarray(slot_of, jnp.int32)[di]
    type_of = jnp.asarray(type_of, jnp.int32)[di]

    mini = jnp.concatenate(
        [
            norm_gains.reshape(-1),
            w_router.reshape(-1),
            segments.astype(bf16).reshape(-1),
            routes.astype(bf16).reshape(-1),
        ]
    )
    mini = after(mini, *slot_steps[1])
    minis = lax.all_to_all(
        jnp.broadcast_to(mini[None], (world,) + mini.shape), ALL, 0, 0, tiled=True
    )
    at = 0
    split = []
    for part in (norm_gains, w_router, segments, routes):
        split.append(minis[:, at : at + part.size])
        at += part.size
    gains_f = split[0].reshape(D, 4).astype(f32)
    router_low = split[1].reshape(D, E)
    router_f = router_low.astype(f32)
    seg_all = split[2].reshape(dps, zs, seqs, LEN)
    seg_own = lax.dynamic_index_in_dim(seg_all, zi, 1, keepdims=False)
    seg_own = seg_own[jnp.asarray(relative(dps)) ^ di].reshape(all_seqs, LEN)
    routes_all = split[3].reshape(dps // 2, 2, zs, rows, TOP)
    routes_own = lax.dynamic_index_in_dim(routes_all, qi, 0, keepdims=False)
    routes_own = routes_own[jnp.stack([ci, 1 - ci])][:, (zi - jnp.arange(zs)) % zs]
    routes_g = routes_own.reshape(2 * zs * rows, TOP).astype(jnp.int32)
    position = jnp.arange(LEN)
    causal = position[:, None] >= position[None, :]
    mask = (causal[None] & (seg_own[:, :, None] == seg_own[:, None, :])).astype(f32)
    own_gains = lax.dynamic_slice(gains_f, (di * width, 0), (width, 4))
    gain_rows = jnp.pad(own_gains[:, 1:3].T, ((0, 6), (0, 0)))
    cos_table, sin_table = rope_tables(LEN, HD)
    cos_full = jnp.tile(jnp.concatenate([cos_table, cos_table], axis=1), (BLOCK // LEN, 1))
    sin_full = jnp.tile(jnp.concatenate([-sin_table, sin_table], axis=1), (BLOCK // LEN, 1))

    qkv_slots = true_order(slots, zs, zi).reshape(3, width, D)
    w_three = jnp.concatenate(
        [lax.dynamic_index_in_dim(qkv_slots, slot_of[k], 0, keepdims=False) for k in range(3)],
        axis=0,
    )
    out_cols = after(w_out, *slot_steps[2]).reshape(orow, dps, width).transpose(1, 0, 2)
    out_cols = jnp.broadcast_to(out_cols[:, None], (dps, zs, orow, width))
    w_out_c = lax.all_to_all(
        out_cols.reshape(world, orow, width), ALL, 0, 0, tiled=True
    ).reshape(D, width)
    dy_blocks, dy_steps = gather_z(after(cotangent, *slot_steps[-1]), zs, zi)

    def in_core_order(own, got):
        first = ci == 0
        return jnp.where(first, own, got), jnp.where(first, got, own)

    def core_half(weight):
        split = weight.reshape((2, mine) + weight.shape[1:])
        got = swap_core(lax.dynamic_index_in_dim(split, 1 - ci, 0, keepdims=False))
        own = lax.dynamic_index_in_dim(split, ci, 0, keepdims=False)
        both = in_core_order(own, got)
        return [jnp.concatenate([half[e] for half in both], axis=0) for e in range(mine)]

    gu_half = core_half(after(w_gate_up, *slot_steps[1]))
    down_half = core_half(after(w_down, *slot_steps[1]))
    blocks = all_rows // BLOCK
    half = blocks // 2
    own_spec, other_spec = pieces_spec(half, D // 2)
    piece_specs = [own_spec, own_spec, other_spec, other_spec]
    part_specs = list(pieces_spec(half, D))
    part_shapes = [shape_of(all_rows // 2, D, bf16)] * 2
    hidden_one, raw, sums = run_blocks(
        functools.partial(qkv_kernel, width, half),
        all_rows,
        piece_specs + [whole((1, D)), whole((3 * width, D))],
        [by_rows(D), by_rows(3 * width), across(8)],
        [
            shape_of(all_rows, D, bf16),
            shape_of(all_rows, 3 * width, f32),
            shape_of(8, all_rows, f32),
        ],
        tuple(tok_pieces) + (gains_f[:, 0][None], w_three),
    )
    sums = sum_dp(sums, dps)
    mask_spec = pl.BlockSpec((BLOCK // LEN, LEN, LEN), lambda i: (i, 0, 0))
    table_specs = [whole((8, width)), whole((BLOCK, HD)), whole((BLOCK, HD)), mask_spec]
    tables = (gain_rows, cos_full, sin_full, mask)
    attended, own, other = run_blocks(
        functools.partial(attend_kernel, width, half),
        all_rows,
        [by_rows(3 * width), across(8)] + table_specs + [whole((D, width))],
        [by_rows(width)] + part_specs,
        [shape_of(all_rows, width, bf16)] + part_shapes,
        (raw, sums) + tables + (w_out_c,),
    )
    attn_out, _, attn_last = scatter_dp(own, other, dps)

    expert_w = []
    for e in range(mine):
        if e > 0:
            gu_half[e], down_half[e] = all_after([gu_half[e], down_half[e]], attn_last)
        expert_w.append(
            (
                lax.all_gather(gu_half[e], "q", axis=0, tiled=True),
                lax.all_gather(down_half[e], "q", axis=0, tiled=True),
            )
        )

    x_float = tokens.astype(f32)
    inverse_one = inverse_rms(x_float)
    normed_one = x_float * inverse_one
    residual = x_float + attn_out
    inverse_two = inverse_rms(residual)
    normed_two = residual * inverse_two
    hidden_two = (normed_two * gains_f[:, 3]).astype(bf16)
    router_probs = jax.nn.softmax(mm(hidden_two, router_low, 1, 0), axis=-1)

    dy_g = both_cores(dy_blocks)
    hidden_blocks, _ = gather_z(after(hidden_two, *dy_steps[-1]), zs, zi, {2: [dy_g, router_probs]})
    hidden_g = both_cores(hidden_blocks)
    router_g = jax.nn.softmax(mm(hidden_g, router_low, 1, 0), axis=-1)
    dy_f = dy_g.astype(f32)
    first_expert = zi * local_experts + ci * mine

    early = [w for pair in expert_w for w in pair]
    early = list(lax.optimization_barrier(tuple(early[:-1]))) + early[-1:]
    expert_w = [tuple(early[2 * e : 2 * e + 2]) for e in range(mine)]

    passes = []
    for e in range(mine):
        gate_up, down = expert_w[e]
        expert = first_expert + e
        picked = jnp.any(routes_g == expert, axis=1, keepdims=True)
        prob = jnp.sum(
            jnp.where(jnp.arange(E)[None] == expert, router_g, 0.0), axis=1, keepdims=True
        )
        gate_val = jnp.where(picked, prob, 0.0)
        hidden_e = after(hidden_g, passes[-1]["act"]) if passes else hidden_g
        gate_and_up = mm(hidden_e, gate_up, 1, 1)
        g_part = gate_and_up[:, :FF]
        u_part = gate_and_up[:, FF:]
        sig = jax.nn.sigmoid(g_part)
        silu = g_part * sig
        act = (silu * u_part).astype(bf16)
        expert_out = mm(act, down, 1, 1).astype(bf16).astype(f32)
        grad_gate = jnp.where(picked[:, 0], jnp.sum(dy_f * expert_out, axis=1), 0.0)
        grad_eo = (gate_val * dy_f).astype(bf16)
        grad_act = mm(grad_eo, down, 1, 0)
        grad_g = grad_act * u_part * sig * (1.0 + g_part * (1.0 - sig))
        grad_u = grad_act * silu
        grad_g, grad_u = grad_g.astype(bf16), grad_u.astype(bf16)
        grad_both = jnp.concatenate([grad_g, grad_u], axis=-1)
        rows_back = mm(grad_both, gate_up, 1, 0).astype(bf16).astype(f32)
        dn = mm(grad_eo, act, 0, 0).astype(bf16)
        passes.append(
            dict(
                out=gate_val * expert_out,
                back=rows_back,
                gate=grad_gate,
                both=(grad_g, grad_u),
                act=act,
                dn=lax.psum_scatter(dn, "q", scatter_dimension=0, tiled=True),
            )
        )

    hid_part = sum([p["back"] for p in passes[1:]], passes[0]["back"])
    out_part = sum([p["out"] for p in passes[1:]], passes[0]["out"])
    cols = jnp.stack([p["gate"] for p in passes], axis=0).reshape(mine, 2, zs, rows)
    cols = jnp.where(ci == 0, cols, cols[:, ::-1])
    cols = cols[:, :, (zi - jnp.arange(zs)) % zs]
    hid_mixed = mix_cores(hid_part.astype(bf16))
    out_mixed = mix_cores(out_part.astype(bf16))
    gus = []

    def fill(*deps):
        p = passes[len(gus)]
        gus.append(weight_grad(*all_after(p["both"], deps), hidden_g))
        return gus[-1:]

    hid_gates = {2: lambda steps: fill(hid_mixed), 3: lambda steps: [cols, out_mixed]}
    if mine > 1:
        hid_gates[3] = lambda steps: fill(*steps[0]) + [cols, out_mixed]
    hid_sum, hid_steps = scatter_z(z_blocks(hid_mixed, zs), hid_gates)
    while len(gus) < mine:
        fill(*hid_steps[1])
    grad_hidden = hid_sum
    got = lax.all_to_all(
        cols.transpose(1, 2, 0, 3).reshape(2 * zs, mine, rows), ("c", "z"), 0, 0, tiled=True
    )
    gp = got.reshape(2, zs, mine, rows).transpose(1, 0, 2, 3).reshape(E, rows).T

    grad_logits = router_probs * (gp - jnp.sum(router_probs * gp, axis=-1, keepdims=True))
    grad_router = lax.dot_general(
        hidden_two.astype(f32), grad_logits, (((0,), (0,)), ((), ())), precision=PRECISE
    )
    grad_hidden = grad_hidden + jnp.dot(grad_logits, router_f.T, precision=PRECISE)
    gain_two = jnp.sum(grad_hidden * normed_two, axis=0)
    grad_residual = cotangent.astype(f32) + norm_back(
        grad_hidden * gains_f[:, 3], normed_two, inverse_two
    )

    def core_back(parts):
        stacked = jnp.stack(parts, axis=0)
        split = stacked.reshape((mine, 2, stacked.shape[1] // 2, stacked.shape[2]))
        got = swap_core(lax.dynamic_index_in_dim(split, 1 - ci, 1, keepdims=False))
        own = lax.dynamic_index_in_dim(split, ci, 1, keepdims=False)
        return jnp.concatenate(in_core_order(own, got), axis=0).astype(f32)

    grad_pieces = []

    def out_gate(steps):
        if len(steps) == 1:
            grad_pieces.extend(
                gather_dp(grad_residual.astype(bf16), dps, gate=gus[-1:] + list(steps[0]))
            )
        return []

    out_total, out_steps = scatter_z(
        z_blocks(after(out_mixed, *hid_steps[-1]), zs), {s: out_gate for s in range(2, zs)}
    )
    gus = [after(gu, *hid_steps[0]) for gu in gus[:-1]] + [after(gus[-1], *grad_pieces)]
    gus = [lax.psum_scatter(gu, "q", scatter_dimension=0, tiled=True) for gu in gus]
    back, dv, dots, gain_sums, grad_out_c = run_blocks(
        functools.partial(attend_back_kernel, width, half),
        all_rows,
        [by_rows(3 * width), across(8)] + table_specs + [whole((D, width)), by_rows(width)]
        + piece_specs,
        [by_rows(2 * width), by_rows(width), across(8), whole((8, width)), whole((D, width))],
        [
            shape_of(all_rows, 2 * width, f32),
            shape_of(all_rows, width, bf16),
            shape_of(8, all_rows, f32),
            shape_of(8, width, f32),
            shape_of(D, width, f32),
        ],
        (raw, sums) + tables + (w_out_c, attended) + tuple(grad_pieces),
    )

    def z_parts(value):
        return [
            lax.dynamic_index_in_dim(value, (zi - k) % zs, 0, keepdims=False) for k in range(zs)
        ]

    dots = sum_dp(after(dots, *out_steps[1]), dps)
    grad_projected, own, other = run_blocks(
        functools.partial(project_back_kernel, width, half),
        all_rows,
        [
            by_rows(3 * width), across(8), by_rows(2 * width), by_rows(width), across(8),
            whole((3 * width, D)),
        ],
        [by_rows(3 * width)] + part_specs,
        [shape_of(all_rows, 3 * width, bf16)] + part_shapes,
        (raw, sums, back, dv, dots, w_three),
    )
    grad_h1, h1_summed, h1_last = scatter_dp(own, other, dps)
    gain_one = jnp.sum(grad_h1 * normed_one, axis=0)
    grad_tokens = grad_residual + norm_back(grad_h1 * gains_f[:, 0], normed_one, inverse_one)
    result = residual + out_total

    hidden_late = after(hidden_one, *out_steps[-1])
    grad_three = mm(grad_projected, hidden_late, 0, 0).astype(bf16).reshape(3, width, D)
    grad_slots = jnp.concatenate(
        [lax.dynamic_index_in_dim(grad_three, type_of[s], 0, keepdims=True) for s in range(3)],
        axis=0,
    )
    grad_cols = grad_out_c.astype(bf16).reshape(dps, zs, orow, width).transpose(1, 2, 0, 3)
    parts = jnp.concatenate(
        [grad_slots.reshape(zs, 3 * sub, D), grad_cols.reshape(zs, orow, D)], axis=1
    )
    dns = [p["dn"] for p in passes]
    grad_down = core_back([after(dns[0], grad_projected)] + dns[1:])
    own_sum, own_steps = scatter_z(z_parts(parts), {s: lambda steps: [] if steps else [h1_summed] for s in range(1, zs)})
    grad_gate_up = core_back([after(gus[0], *own_steps[1])] + gus[1:])
    own_sum = after(own_sum.astype(bf16), grad_down)
    grad_qkv = jnp.concatenate(
        [
            lax.ppermute(own_sum[t * sub : (t + 1) * sub], ALL, unit_perm(t, True))
            for t in range(3)
        ],
        axis=0,
    ).astype(f32)
    own_cols = own_sum[3 * sub :].reshape(orow, dps, width).transpose(1, 0, 2)
    grad_out = (
        lax.all_to_all(own_cols, DP, 0, 0, tiled=True)
        .transpose(1, 0, 2)
        .reshape(orow, D)
        .astype(f32)
    )

    shard_cols = lax.dynamic_update_slice(jnp.zeros((D, 2), f32), gain_sums[:2].T, (di * width, 0))
    small_grads = jnp.concatenate(
        [gain_one[:, None], shard_cols, gain_two[:, None], grad_router], axis=1
    )
    small_own = jnp.sum(
        lax.all_to_all(
            small_grads.reshape(world, D * (E + 4) // world), ALL, 0, 0, tiled=True
        ),
        axis=0,
    ).reshape(D // world, E + 4)

    return (
        result.astype(bf16),
        grad_tokens,
        grad_qkv,
        grad_out,
        small_own[:, :4],
        small_own[:, 4:],
        grad_gate_up,
        grad_down,
    )


def solution(mesh):
    dps, zs = mesh.shape["dp"], mesh.shape["fsdp"]
    inner = Mesh(mesh.devices.reshape(dps // 2, 2, zs), ALL)
    rows = P(ALL, None)
    experts = P("z", DP, None)
    in_specs = (rows,) * 8 + (experts,) * 2
    out_specs = (rows,) * 6 + (experts,) * 2
    return jax.shard_map(
        per_device, mesh=inner, in_specs=in_specs, out_specs=out_specs, check_vma=False
    )
```

```python
import functools

import jax
import jax.numpy as jnp
from jax import lax
from jax.experimental import pallas as pl
from jax.experimental.pallas import tpu as pltpu
from jax.sharding import Mesh
from jax.sharding import PartitionSpec as P

D = 2048
H = 16
HD = 128
FF = 1024
TOP = 8
E = 16
LEN = 96

NORM_EPS = 1e-05
ROPE_BASE = 10000.0
PRECISE = lax.Precision.HIGHEST
DP = ("q", "c")
ALL = ("q", "c", "z")
f32 = jnp.float32
bf16 = jnp.bfloat16


def inverse_rms(field_in):
    return lax.rsqrt(jnp.mean(field_in * field_in, axis=-1, keepdims=True) + NORM_EPS)


def rope_tables(length, head_dim):
    half_dim = head_dim // 2
    frequency = ROPE_BASE ** (-(jnp.arange(half_dim).astype(f32) * 2.0) / head_dim)
    angles = jnp.arange(length).astype(f32)[:, None] * frequency[None, :]
    return jnp.cos(angles), jnp.sin(angles)


def norm_back(grad_normed, normed, inverse):
    return inverse * (grad_normed - normed * jnp.mean(grad_normed * normed, axis=-1, keepdims=True))


def mm(a, b, ca, cb):
    return lax.dot_general(a, b, (((ca,), (cb,)), ((), ())), preferred_element_type=f32)


def after(value, *deps):
    return lax.optimization_barrier((value,) + tuple(deps))[0]


def flip(value, size, bit):
    return lax.ppermute(value, DP, [(i, i ^ (1 << bit)) for i in range(size)])


def relative(size):
    return [high * 2 + core for core in range(2) for high in range(size // 2)]


def bit_lists(size):
    high = list(range(1, size.bit_length() - 1))
    return high, high[::-1]


def gather_dp(value, size, gate=()):
    width = value.shape[-1] // 2
    pieces = []
    for part, order in zip((value[:, :width], value[:, width:]), bit_lists(size)):
        out, have = part, []
        for bit in order:
            axis = sum(1 for other in have if other > bit)
            out = jnp.stack([out, flip(out, size, bit)], axis=axis)
            have.append(bit)
        pieces.append(out.reshape(-1, width))
    sent = [after(piece, *gate) for piece in pieces] if gate else pieces
    return pieces + [flip(piece, size, 0) for piece in sent]


def scatter_dp(own, other, size):
    rows, width = own.shape[0] * 2 // size, own.shape[1]
    got = flip(other, size, 0)
    summed = (own.astype(f32) + got.astype(f32)).astype(bf16)
    highs = size.bit_length() - 2
    halves, last = [], []
    for half, order in enumerate(bit_lists(size)):
        cur = summed[:, half * (width // 2) : (half + 1) * (width // 2)]
        cur = cur.reshape([2] * highs + [rows, width // 2])
        left = list(range(highs, 0, -1))
        for k, bit in enumerate(order):
            axis = left.index(bit)
            left.remove(bit)
            keep = lax.index_in_dim(cur, 0, axis, keepdims=False)
            send = lax.index_in_dim(cur, 1, axis, keepdims=False)
            brought = flip(send, size, bit)
            total = keep.astype(f32) + brought.astype(f32)
            cur = total if k == len(order) - 1 else total.astype(bf16)
        halves.append(cur)
        last.append(brought)
    return jnp.concatenate(halves, axis=-1), summed, last


def sum_dp(value, size):
    count = size.bit_length() - 1
    shape = value.shape
    value = value[:2].reshape((2,) + (2,) * count + (-1,))
    for bit in range(count):
        value = value + jnp.flip(flip(value, size, bit), 1 if bit == 0 else count - bit + 1)
    return jnp.pad(value.reshape(2, shape[1]), ((0, 6), (0, 0)))


def line(value, zs, step):
    return lax.ppermute(value, "z", [(j, j + step) for j in range(zs) if 0 <= j + step < zs])


def all_after(values, deps):
    return list(lax.optimization_barrier(tuple(values) + tuple(deps))[: len(values)])


def gather_z(value, zs, zi, gates={}):
    right, left = [value], [value]
    for s in range(1, zs):
        sent = all_after([right[-1], left[-1]], gates[s]) if s in gates else [right[-1], left[-1]]
        right.append(line(sent[0], zs, 1))
        left.append(line(sent[1], zs, -1))
    blocks = [value] + [jnp.where(zi >= k, right[k], left[zs - k]) for k in range(1, zs)]
    return blocks, list(zip(right, left))


def true_order(blocks, zs, zi):
    out = jnp.zeros((zs,) + blocks[0].shape, blocks[0].dtype)
    for k, block in enumerate(blocks):
        out = lax.dynamic_update_index_in_dim(out, block, (zi - k) % zs, 0)
    return out


def scatter_z(parts, gates={}):
    zs = len(parts)
    right, left = None, None
    steps = []
    for s in range(1, zs):
        go_right = parts[s] if right is None else (parts[s].astype(f32) + right).astype(bf16)
        go_left = parts[zs - s] if left is None else (parts[zs - s].astype(f32) + left).astype(bf16)
        if s in gates:
            go_right, go_left = all_after([go_right, go_left], gates[s](steps))
        got_right, got_left = line(go_right, zs, 1), line(go_left, zs, -1)
        steps.append((got_right, got_left))
        right, left = got_right.astype(f32), got_left.astype(f32)
    return parts[0].astype(f32) + right + left, steps


def swap_core(value):
    return lax.ppermute(value, "c", [(0, 1), (1, 0)])


def both_cores(blocks):
    got = jnp.concatenate(blocks, axis=0)
    return jnp.concatenate([got, swap_core(got)], axis=0)


def mix_cores(parts):
    half = parts.shape[0] // 2
    return (parts[:half].astype(f32) + swap_core(parts[half:]).astype(f32)).astype(bf16)


def z_blocks(mixed, zs):
    block = mixed.shape[0] // zs
    return [mixed[k * block : (k + 1) * block] for k in range(zs)]


BLOCK = 4 * LEN


def kdot(a, b, ca, cb):
    return lax.dot_general(a, b, (((ca,), (cb,)), ((), ())), preferred_element_type=f32)


def to_rows(first, second):
    lane = lax.broadcasted_iota(jnp.int32, (first.shape[0], 128), 1)
    both = jnp.where(lane == 0, first, jnp.where(lane == 1, second, 0.0))
    return both.T[:8]


def to_cols(block):
    cols = jnp.concatenate([block] * 16, axis=0).T
    return cols[:, 0:1], cols[:, 1:2]


def own_rows(half):
    return pl.program_id(0) < half


def picked_rows(half, own_ref, other_ref):
    return jnp.where(own_rows(half), own_ref[...].astype(f32), other_ref[...].astype(f32))


def store_rows(half, own_ref, other_ref, value):
    @pl.when(own_rows(half))
    def _():
        own_ref[...] = value

    @pl.when(jnp.logical_not(own_rows(half)))
    def _():
        other_ref[...] = value


def qkv_kernel(
    width, half, a_own, b_own, a_other, b_other, gain_ref, w_ref, hid_ref, raw_ref, sum_ref
):
    x_a = picked_rows(half, a_own, a_other)
    x_b = picked_rows(half, b_own, b_other)
    square = jnp.sum(x_a * x_a, axis=-1, keepdims=True) + jnp.sum(x_b * x_b, axis=-1, keepdims=True)
    inverse = lax.rsqrt(square / D + NORM_EPS)
    hid_ref[:, : D // 2] = (x_a * inverse * gain_ref[:, : D // 2]).astype(bf16)
    hid_ref[:, D // 2 :] = (x_b * inverse * gain_ref[:, D // 2 :]).astype(bf16)
    raw = kdot(hid_ref[...], w_ref[...], 1, 1)
    raw_ref[...] = raw
    q, k = raw[:, :width], raw[:, width : 2 * width]
    sum_ref[...] = to_rows(
        jnp.sum(q * q, axis=-1, keepdims=True), jnp.sum(k * k, axis=-1, keepdims=True)
    )


def spin(x, cos, sin):
    return x * cos + pltpu.roll(x, HD // 2, 1) * sin


def heads_of(raw, inv_q, inv_k, gain_ref, cos, sin, width, head):
    lo = head * HD
    normed_q = raw[:, lo : lo + HD] * inv_q
    normed_k = raw[:, width + lo : width + lo + HD] * inv_k
    query = spin(normed_q * gain_ref[0:1, lo : lo + HD], cos, sin).astype(bf16)
    key = spin(normed_k * gain_ref[1:2, lo : lo + HD], cos, sin).astype(bf16)
    value = raw[:, 2 * width + lo : 2 * width + lo + HD].astype(bf16)
    return normed_q, normed_k, query, key, value


def probs_of(query, key, mask):
    scores = jnp.where(mask > 0.5, kdot(query, key, 1, 1) * HD ** (-0.5), -1e30)
    scores = jnp.exp(scores - jnp.max(scores, axis=-1, keepdims=True))
    return scores / jnp.sum(scores, axis=-1, keepdims=True)


def inverses(sum_ref):
    ss_q, ss_k = to_cols(sum_ref[...])
    return lax.rsqrt(ss_q / D + NORM_EPS), lax.rsqrt(ss_k / D + NORM_EPS)


def attend_kernel(
    width, half, raw_ref, sum_ref, gain_ref, cos_ref, sin_ref, mask_ref, w_ref,
    att_ref, own_ref, other_ref,
):
    inv_q, inv_k = inverses(sum_ref)
    raw = raw_ref[...]
    cos, sin = cos_ref[...], sin_ref[...]
    for head in range(width // HD):
        _, _, query, key, value = heads_of(raw, inv_q, inv_k, gain_ref, cos, sin, width, head)
        for s in range(BLOCK // LEN):
            at = slice(s * LEN, (s + 1) * LEN)
            probs = probs_of(query[at], key[at], mask_ref[s])
            att_ref[at, head * HD : (head + 1) * HD] = kdot(
                probs.astype(bf16), value[at], 1, 0
            ).astype(bf16)
    store_rows(half, own_ref, other_ref, kdot(att_ref[...], w_ref[...], 1, 1).astype(bf16))


def attend_back_kernel(
    width, half, raw_ref, sum_ref, gain_ref, cos_ref, sin_ref, mask_ref, w_ref, att_ref,
    a_own, b_own, a_other, b_other, back_ref, dv_ref, dot_ref, gsum_ref, gout_ref,
):
    inv_q, inv_k = inverses(sum_ref)
    raw = raw_ref[...]
    cos, sin = cos_ref[...], sin_ref[...]
    grad_a = picked_rows(half, a_own, a_other).astype(bf16)
    grad_b = picked_rows(half, b_own, b_other).astype(bf16)
    grad_heads = kdot(grad_a, w_ref[: D // 2], 1, 0) + kdot(grad_b, w_ref[D // 2 :], 1, 0)
    grad_heads = grad_heads.astype(bf16)

    @pl.when(pl.program_id(0) == 0)
    def _():
        gsum_ref[...] = jnp.zeros_like(gsum_ref)
        gout_ref[...] = jnp.zeros_like(gout_ref)

    gout_ref[: D // 2] += kdot(grad_a, att_ref[...], 0, 0)
    gout_ref[D // 2 :] += kdot(grad_b, att_ref[...], 0, 0)

    dot_q = dot_k = 0.0
    for head in range(width // HD):
        lo = head * HD
        normed_q, normed_k, query, key, value = heads_of(
            raw, inv_q, inv_k, gain_ref, cos, sin, width, head
        )
        grads_q, grads_k = [], []
        for s in range(BLOCK // LEN):
            at = slice(s * LEN, (s + 1) * LEN)
            probs = probs_of(query[at], key[at], mask_ref[s])
            grad = grad_heads[at, lo : lo + HD]
            grad_probs = kdot(grad, value[at], 1, 1)
            dv_ref[at, lo : lo + HD] = kdot(probs.astype(bf16), grad, 0, 0).astype(bf16)
            delta = jnp.sum(probs * grad_probs, axis=-1, keepdims=True)
            grad_scores = (probs * (grad_probs - delta)).astype(bf16)
            grads_q.append(kdot(grad_scores, key[at], 1, 0))
            grads_k.append(kdot(grad_scores, query[at], 0, 0))
        grad_nq = spin(jnp.concatenate(grads_q, axis=0) * HD ** (-0.5), cos, -sin)
        grad_nk = spin(jnp.concatenate(grads_k, axis=0) * HD ** (-0.5), cos, -sin)
        prod_q, prod_k = grad_nq * normed_q, grad_nk * normed_k
        gsum_ref[0:1, lo : lo + HD] += jnp.sum(prod_q, axis=0, keepdims=True)
        gsum_ref[1:2, lo : lo + HD] += jnp.sum(prod_k, axis=0, keepdims=True)
        gain_q, gain_k = gain_ref[0:1, lo : lo + HD], gain_ref[1:2, lo : lo + HD]
        dot_q = dot_q + jnp.sum(prod_q * gain_q, axis=-1, keepdims=True)
        dot_k = dot_k + jnp.sum(prod_k * gain_k, axis=-1, keepdims=True)
        back_ref[:, lo : lo + HD] = grad_nq * gain_q
        back_ref[:, width + lo : width + lo + HD] = grad_nk * gain_k
    dot_ref[...] = to_rows(dot_q, dot_k)


def project_back_kernel(
    width, half, raw_ref, sum_ref, back_ref, dv_ref, dot_ref, w_ref, proj_ref, own_ref, other_ref
):
    inv_q, inv_k = inverses(sum_ref)
    mean_q, mean_k = to_cols(dot_ref[...] / D)
    normed_q = raw_ref[:, :width] * inv_q
    normed_k = raw_ref[:, width : 2 * width] * inv_k
    proj_ref[:, :width] = (inv_q * (back_ref[:, :width] - normed_q * mean_q)).astype(bf16)
    proj_ref[:, width : 2 * width] = (
        inv_k * (back_ref[:, width:] - normed_k * mean_k)
    ).astype(bf16)
    proj_ref[:, 2 * width :] = dv_ref[...]
    store_rows(half, own_ref, other_ref, kdot(proj_ref[...], w_ref[...], 1, 0).astype(bf16))


def by_rows(cols):
    return pl.BlockSpec((BLOCK, cols), lambda i: (i, 0))


def pieces_spec(half, cols):
    own = pl.BlockSpec((BLOCK, cols), lambda i: (jnp.minimum(i, half - 1), 0))
    other = pl.BlockSpec((BLOCK, cols), lambda i: (jnp.maximum(i - half, 0), 0))
    return own, other


def across(rows):
    return pl.BlockSpec((rows, BLOCK), lambda i: (0, i))


def whole(shape):
    return pl.BlockSpec(shape, lambda i: (0,) * len(shape))


def run_blocks(body, rows, in_specs, out_specs, out_shape, args):
    return pl.pallas_call(
        body,
        grid=(rows // BLOCK,),
        in_specs=in_specs,
        out_specs=out_specs,
        out_shape=out_shape,
        cost_estimate=pl.CostEstimate(flops=1, bytes_accessed=1, transcendentals=0),
    )(*args)


def weight_grad_kernel(half, g_ref, u_ref, b_ref, out_ref):
    @pl.when(pl.program_id(1) < half)
    def _():
        out_ref[...] = kdot(g_ref[...], b_ref[...], 0, 0).astype(bf16)

    @pl.when(pl.program_id(1) >= half)
    def _():
        out_ref[...] = kdot(u_ref[...], b_ref[...], 0, 0).astype(bf16)


def weight_grad(g, u, b):
    tile_a, tile_b = 512, 1024
    half = g.shape[1] // tile_a
    return pl.pallas_call(
        functools.partial(weight_grad_kernel, half),
        grid=(b.shape[1] // tile_b, 2 * half),
        in_specs=[
            pl.BlockSpec((g.shape[0], tile_a), lambda n, m: (0, jnp.minimum(m, half - 1))),
            pl.BlockSpec((u.shape[0], tile_a), lambda n, m: (0, jnp.maximum(m - half, 0))),
            pl.BlockSpec((b.shape[0], tile_b), lambda n, m: (0, n)),
        ],
        out_specs=pl.BlockSpec((tile_a, tile_b), lambda n, m: (m, n)),
        out_shape=jax.ShapeDtypeStruct((2 * g.shape[1], b.shape[1]), bf16),
        cost_estimate=pl.CostEstimate(flops=1, bytes_accessed=1, transcendentals=0),
    )(g, u, b)


def shape_of(rows, cols, dtype):
    return jax.ShapeDtypeStruct((rows, cols), dtype)


def per_device(
    tokens, cotangent, segments, routes, w_qkv, w_out, norm_gains, w_router, w_gate_up, w_down
):
    zs = lax.axis_size("z")
    dps = lax.axis_size("q") * 2
    world = dps * zs
    qi, ci, zi = lax.axis_index("q"), lax.axis_index("c"), lax.axis_index("z")
    di = qi * 2 + ci
    rows = tokens.shape[0]
    seqs = rows // LEN
    width = D // dps
    local_experts = E // zs
    mine = local_experts // 2
    sub = w_qkv.shape[0] // 3
    orow = w_out.shape[0]
    all_rows = dps * rows
    all_seqs = dps * seqs

    def unit_perm(t, back):
        pairs = []
        for i in range(dps):
            for j in range(zs):
                dest = (3 * i + (3 * j + t) // zs) % dps
                src_dev, dst_dev = i * zs + j, dest * zs + j
                pairs.append((dst_dev, src_dev) if back else (src_dev, dst_dev))
        return pairs

    moved = [
        lax.ppermute(w_qkv[t * sub : (t + 1) * sub], ALL, unit_perm(t, False)) for t in range(3)
    ]
    tok_pieces = gather_dp(tokens, dps)
    slots, slot_steps = gather_z(
        jnp.concatenate(moved, axis=0), zs, zi,
        {s: [] if s < zs - 1 else tok_pieces[:2] for s in range(2, zs)},
    )
    inv3 = pow(3, -1, dps)
    slot_of = [[0, 0, 0] for _ in range(dps)]
    type_of = [[0, 0, 0] for _ in range(dps)]
    for i in range(dps):
        for s in range(3):
            src = (inv3 * (i - s)) % dps
            kind = (3 * src + s) // dps
            slot_of[i][kind] = s
            type_of[i][s] = kind
    slot_of = jnp.asarray(slot_of, jnp.int32)[di]
    type_of = jnp.asarray(type_of, jnp.int32)[di]

    mini = jnp.concatenate(
        [
            norm_gains.reshape(-1),
            w_router.reshape(-1),
            segments.astype(bf16).reshape(-1),
            routes.astype(bf16).reshape(-1),
        ]
    )
    mini = after(mini, *slot_steps[1])
    minis = lax.all_to_all(
        jnp.broadcast_to(mini[None], (world,) + mini.shape), ALL, 0, 0, tiled=True
    )
    at = 0
    split = []
    for part in (norm_gains, w_router, segments, routes):
        split.append(minis[:, at : at + part.size])
        at += part.size
    gains_f = split[0].reshape(D, 4).astype(f32)
    router_low = split[1].reshape(D, E)
    router_f = router_low.astype(f32)
    seg_all = split[2].reshape(dps, zs, seqs, LEN)
    seg_own = lax.dynamic_index_in_dim(seg_all, zi, 1, keepdims=False)
    seg_own = seg_own[jnp.asarray(relative(dps)) ^ di].reshape(all_seqs, LEN)
    routes_all = split[3].reshape(dps // 2, 2, zs, rows, TOP)
    routes_own = lax.dynamic_index_in_dim(routes_all, qi, 0, keepdims=False)
    routes_own = routes_own[jnp.stack([ci, 1 - ci])][:, (zi - jnp.arange(zs)) % zs]
    routes_g = routes_own.reshape(2 * zs * rows, TOP).astype(jnp.int32)
    position = jnp.arange(LEN)
    causal = position[:, None] >= position[None, :]
    mask = (causal[None] & (seg_own[:, :, None] == seg_own[:, None, :])).astype(f32)
    own_gains = lax.dynamic_slice(gains_f, (di * width, 0), (width, 4))
    gain_rows = jnp.pad(own_gains[:, 1:3].T, ((0, 6), (0, 0)))
    cos_table, sin_table = rope_tables(LEN, HD)
    cos_full = jnp.tile(jnp.concatenate([cos_table, cos_table], axis=1), (BLOCK // LEN, 1))
    sin_full = jnp.tile(jnp.concatenate([-sin_table, sin_table], axis=1), (BLOCK // LEN, 1))

    qkv_slots = true_order(slots, zs, zi).reshape(3, width, D)
    w_three = jnp.concatenate(
        [lax.dynamic_index_in_dim(qkv_slots, slot_of[k], 0, keepdims=False) for k in range(3)],
        axis=0,
    )
    out_cols = after(w_out, *slot_steps[-1]).reshape(orow, dps, width).transpose(1, 0, 2)
    out_cols = jnp.broadcast_to(out_cols[:, None], (dps, zs, orow, width))
    w_out_c = lax.all_to_all(
        out_cols.reshape(world, orow, width), ALL, 0, 0, tiled=True
    ).reshape(D, width)
    dy_all = lax.all_gather(after(cotangent, *slot_steps[2]), "z", axis=0)
    dy_blocks = [
        lax.dynamic_index_in_dim(dy_all, (zi - k) % zs, 0, keepdims=False) for k in range(zs)
    ]

    def in_core_order(own, got):
        first = ci == 0
        return jnp.where(first, own, got), jnp.where(first, got, own)

    def core_half(weight):
        split = weight.reshape((2, mine) + weight.shape[1:])
        got = swap_core(lax.dynamic_index_in_dim(split, 1 - ci, 0, keepdims=False))
        own = lax.dynamic_index_in_dim(split, ci, 0, keepdims=False)
        both = in_core_order(own, got)
        return [jnp.concatenate([half[e] for half in both], axis=0) for e in range(mine)]

    gu_half = core_half(after(w_gate_up, *slot_steps[-1]))
    down_half = core_half(after(w_down, *moved))
    blocks = all_rows // BLOCK
    half = blocks // 2
    own_spec, other_spec = pieces_spec(half, D // 2)
    piece_specs = [own_spec, own_spec, other_spec, other_spec]
    part_specs = list(pieces_spec(half, D))
    part_shapes = [shape_of(all_rows // 2, D, bf16)] * 2
    hidden_one, raw, sums = run_blocks(
        functools.partial(qkv_kernel, width, half),
        all_rows,
        piece_specs + [whole((1, D)), whole((3 * width, D))],
        [by_rows(D), by_rows(3 * width), across(8)],
        [
            shape_of(all_rows, D, bf16),
            shape_of(all_rows, 3 * width, f32),
            shape_of(8, all_rows, f32),
        ],
        tuple(tok_pieces) + (gains_f[:, 0][None], w_three),
    )
    sums = sum_dp(sums, dps)
    mask_spec = pl.BlockSpec((BLOCK // LEN, LEN, LEN), lambda i: (i, 0, 0))
    table_specs = [whole((8, width)), whole((BLOCK, HD)), whole((BLOCK, HD)), mask_spec]
    tables = (gain_rows, cos_full, sin_full, mask)
    attended, own, other = run_blocks(
        functools.partial(attend_kernel, width, half),
        all_rows,
        [by_rows(3 * width), across(8)] + table_specs + [whole((D, width))],
        [by_rows(width)] + part_specs,
        [shape_of(all_rows, width, bf16)] + part_shapes,
        (raw, sums) + tables + (w_out_c,),
    )
    attn_out, _, attn_last = scatter_dp(own, other, dps)

    expert_w = []
    for e in range(mine):
        if e > 0:
            gu_half[e], down_half[e] = all_after([gu_half[e], down_half[e]], attn_last)
        expert_w.append(
            (
                lax.all_gather(gu_half[e], "q", axis=0, tiled=True),
                lax.all_gather(down_half[e], "q", axis=0, tiled=True),
            )
        )

    x_float = tokens.astype(f32)
    inverse_one = inverse_rms(x_float)
    normed_one = x_float * inverse_one
    residual = x_float + attn_out
    inverse_two = inverse_rms(residual)
    normed_two = residual * inverse_two
    hidden_two = (normed_two * gains_f[:, 3]).astype(bf16)
    router_probs = jax.nn.softmax(mm(hidden_two, router_low, 1, 0), axis=-1)

    dy_g = both_cores(dy_blocks)
    hidden_blocks, _ = gather_z(hidden_two, zs, zi, {2: [dy_g, router_probs]})
    hidden_g = both_cores(hidden_blocks)
    router_g = jax.nn.softmax(mm(hidden_g, router_low, 1, 0), axis=-1)
    dy_f = dy_g.astype(f32)
    first_expert = zi * local_experts + ci * mine

    passes = []
    for e in range(mine):
        gate_up, down = expert_w[e]
        expert = first_expert + e
        picked = jnp.any(routes_g == expert, axis=1, keepdims=True)
        prob = jnp.sum(
            jnp.where(jnp.arange(E)[None] == expert, router_g, 0.0), axis=1, keepdims=True
        )
        gate_val = jnp.where(picked, prob, 0.0)
        hidden_e = after(hidden_g, passes[-1]["rows"]) if passes else hidden_g
        gate_and_up = mm(hidden_e, gate_up, 1, 1)
        g_part = gate_and_up[:, :FF]
        u_part = gate_and_up[:, FF:]
        sig = jax.nn.sigmoid(g_part)
        silu = g_part * sig
        act = (silu * u_part).astype(bf16)
        expert_out = mm(act, down, 1, 1).astype(bf16).astype(f32)
        grad_gate = jnp.where(picked[:, 0], jnp.sum(dy_f * expert_out, axis=1), 0.0)
        grad_eo = (gate_val * dy_f).astype(bf16)
        grad_act = mm(grad_eo, down, 1, 0)
        grad_g = grad_act * u_part * sig * (1.0 + g_part * (1.0 - sig))
        grad_u = grad_act * silu
        grad_g, grad_u = grad_g.astype(bf16), grad_u.astype(bf16)
        grad_both = jnp.concatenate([grad_g, grad_u], axis=-1)
        rows_back = mm(grad_both, gate_up, 1, 0).astype(bf16)
        dn = mm(grad_eo, act, 0, 0).astype(bf16)
        passes.append(
            dict(
                out=gate_val * expert_out,
                back=rows_back.astype(f32),
                rows=rows_back,
                gate=grad_gate,
                both=(grad_g, grad_u),
                dn=lax.psum_scatter(dn, "q", scatter_dimension=0, tiled=True),
            )
        )

    hid_part = sum([p["back"] for p in passes[1:]], passes[0]["back"])
    out_part = sum([p["out"] for p in passes[1:]], passes[0]["out"])
    cols = jnp.stack([p["gate"] for p in passes], axis=0).reshape(mine, 2, zs, rows)
    cols = jnp.where(ci == 0, cols, cols[:, ::-1])
    cols = cols[:, :, (zi - jnp.arange(zs)) % zs]
    hid_mixed = mix_cores(hid_part.astype(bf16))
    out_mixed = mix_cores(out_part.astype(bf16))
    gus = []

    def fill(*deps):
        p = passes[len(gus)]
        gus.append(weight_grad(*all_after(p["both"], deps), hidden_g))
        return gus[-1:]

    hid_gates = {2: lambda steps: fill(hid_mixed), 3: lambda steps: [cols, out_mixed]}
    if mine > 1:
        hid_gates[3] = lambda steps: fill(*steps[0]) + [cols, out_mixed]
    hid_sum, hid_steps = scatter_z(z_blocks(hid_mixed, zs), hid_gates)
    while len(gus) < mine:
        fill(*hid_steps[1])
    grad_hidden = hid_sum
    got = lax.all_to_all(
        cols.transpose(1, 2, 0, 3).reshape(2 * zs, mine, rows), ("c", "z"), 0, 0, tiled=True
    )
    gp = got.reshape(2, zs, mine, rows).transpose(1, 0, 2, 3).reshape(E, rows).T

    grad_logits = router_probs * (gp - jnp.sum(router_probs * gp, axis=-1, keepdims=True))
    grad_router = lax.dot_general(
        hidden_two.astype(f32), grad_logits, (((0,), (0,)), ((), ())), precision=PRECISE
    )
    grad_hidden = grad_hidden + jnp.dot(grad_logits, router_f.T, precision=PRECISE)
    gain_two = jnp.sum(grad_hidden * normed_two, axis=0)
    grad_residual = cotangent.astype(f32) + norm_back(
        grad_hidden * gains_f[:, 3], normed_two, inverse_two
    )

    def core_back(parts):
        stacked = jnp.stack(parts, axis=0)
        split = stacked.reshape((mine, 2, stacked.shape[1] // 2, stacked.shape[2]))
        got = swap_core(lax.dynamic_index_in_dim(split, 1 - ci, 1, keepdims=False))
        own = lax.dynamic_index_in_dim(split, ci, 1, keepdims=False)
        return jnp.concatenate(in_core_order(own, got), axis=0).astype(f32)

    grad_pieces = []

    def out_gate(steps):
        if len(steps) == 1:
            grad_pieces.extend(
                gather_dp(grad_residual.astype(bf16), dps, gate=gus[-1:] + list(steps[0]))
            )
        return []

    out_total, out_steps = scatter_z(
        z_blocks(after(out_mixed, *hid_steps[-1]), zs), {s: out_gate for s in range(2, zs)}
    )
    gus = [after(gu, *hid_steps[0]) for gu in gus[:-1]] + [after(gus[-1], *grad_pieces)]
    gus = [lax.psum_scatter(gu, "q", scatter_dimension=0, tiled=True) for gu in gus]
    back, dv, dots, gain_sums, grad_out_c = run_blocks(
        functools.partial(attend_back_kernel, width, half),
        all_rows,
        [by_rows(3 * width), across(8)] + table_specs + [whole((D, width)), by_rows(width)]
        + piece_specs,
        [by_rows(2 * width), by_rows(width), across(8), whole((8, width)), whole((D, width))],
        [
            shape_of(all_rows, 2 * width, f32),
            shape_of(all_rows, width, bf16),
            shape_of(8, all_rows, f32),
            shape_of(8, width, f32),
            shape_of(D, width, f32),
        ],
        (raw, sums) + tables + (w_out_c, attended) + tuple(grad_pieces),
    )

    def z_parts(value):
        return [
            lax.dynamic_index_in_dim(value, (zi - k) % zs, 0, keepdims=False) for k in range(zs)
        ]

    dots = sum_dp(after(dots, *out_steps[1]), dps)
    grad_projected, own, other = run_blocks(
        functools.partial(project_back_kernel, width, half),
        all_rows,
        [
            by_rows(3 * width), across(8), by_rows(2 * width), by_rows(width), across(8),
            whole((3 * width, D)),
        ],
        [by_rows(3 * width)] + part_specs,
        [shape_of(all_rows, 3 * width, bf16)] + part_shapes,
        (raw, sums, back, dv, dots, w_three),
    )
    grad_h1, h1_summed, h1_last = scatter_dp(own, other, dps)
    gain_one = jnp.sum(grad_h1 * normed_one, axis=0)
    grad_tokens = grad_residual + norm_back(grad_h1 * gains_f[:, 0], normed_one, inverse_one)
    result = residual + out_total

    hidden_late = after(hidden_one, *out_steps[-1])
    grad_three = mm(grad_projected, hidden_late, 0, 0).astype(bf16).reshape(3, width, D)
    grad_slots = jnp.concatenate(
        [lax.dynamic_index_in_dim(grad_three, type_of[s], 0, keepdims=True) for s in range(3)],
        axis=0,
    )
    grad_cols = grad_out_c.astype(bf16).reshape(dps, zs, orow, width).transpose(1, 2, 0, 3)
    parts = jnp.concatenate(
        [grad_slots.reshape(zs, 3 * sub, D), grad_cols.reshape(zs, orow, D)], axis=1
    )
    dns = [p["dn"] for p in passes]
    grad_down = core_back([after(dns[0], grad_projected)] + dns[1:])
    own_sum, own_steps = scatter_z(z_parts(parts), {s: lambda steps: [] if steps else [h1_summed] for s in range(1, zs)})
    grad_gate_up = core_back([after(gus[0], *own_steps[1])] + gus[1:])
    own_sum = after(own_sum.astype(bf16), grad_down)
    grad_qkv = jnp.concatenate(
        [
            lax.ppermute(own_sum[t * sub : (t + 1) * sub], ALL, unit_perm(t, True))
            for t in range(3)
        ],
        axis=0,
    ).astype(f32)
    own_cols = own_sum[3 * sub :].reshape(orow, dps, width).transpose(1, 0, 2)
    grad_out = (
        lax.all_to_all(own_cols, DP, 0, 0, tiled=True)
        .transpose(1, 0, 2)
        .reshape(orow, D)
        .astype(f32)
    )

    shard_cols = lax.dynamic_update_slice(jnp.zeros((D, 2), f32), gain_sums[:2].T, (di * width, 0))
    small_grads = jnp.concatenate(
        [gain_one[:, None], shard_cols, gain_two[:, None], grad_router], axis=1
    )
    small_own = jnp.sum(
        lax.all_to_all(
            small_grads.reshape(world, D * (E + 4) // world), ALL, 0, 0, tiled=True
        ),
        axis=0,
    ).reshape(D // world, E + 4)

    return (
        result.astype(bf16),
        grad_tokens,
        grad_qkv,
        grad_out,
        small_own[:, :4],
        small_own[:, 4:],
        grad_gate_up,
        grad_down,
    )


def solution(mesh):
    dps, zs = mesh.shape["dp"], mesh.shape["fsdp"]
    inner = Mesh(mesh.devices.reshape(dps // 2, 2, zs), ALL)
    rows = P(ALL, None)
    experts = P("z", DP, None)
    in_specs = (rows,) * 8 + (experts,) * 2
    out_specs = (rows,) * 6 + (experts,) * 2
    return jax.shard_map(
        per_device, mesh=inner, in_specs=in_specs, out_specs=out_specs, check_vma=False
    )
```

```python
import functools

import jax
import jax.numpy as jnp
from jax import lax
from jax.experimental import pallas as pl
from jax.experimental.pallas import tpu as pltpu
from jax.sharding import Mesh
from jax.sharding import PartitionSpec as P

D = 2048
H = 16
HD = 128
FF = 1024
TOP = 8
E = 16
LEN = 96

NORM_EPS = 1e-05
ROPE_BASE = 10000.0
PRECISE = lax.Precision.HIGHEST
DP = ("q", "c")
ALL = ("q", "c", "z")
f32 = jnp.float32
bf16 = jnp.bfloat16


def inverse_rms(field_in):
    return lax.rsqrt(jnp.mean(field_in * field_in, axis=-1, keepdims=True) + NORM_EPS)


def rope_tables(length, head_dim):
    half_dim = head_dim // 2
    frequency = ROPE_BASE ** (-(jnp.arange(half_dim).astype(f32) * 2.0) / head_dim)
    angles = jnp.arange(length).astype(f32)[:, None] * frequency[None, :]
    return jnp.cos(angles), jnp.sin(angles)


def norm_back(grad_normed, normed, inverse):
    return inverse * (grad_normed - normed * jnp.mean(grad_normed * normed, axis=-1, keepdims=True))


def mm(a, b, ca, cb):
    return lax.dot_general(a, b, (((ca,), (cb,)), ((), ())), preferred_element_type=f32)


def after(value, *deps):
    return lax.optimization_barrier((value,) + tuple(deps))[0]


def flip(value, size, bit):
    return lax.ppermute(value, DP, [(i, i ^ (1 << bit)) for i in range(size)])


def relative(size):
    return [high * 2 + core for core in range(2) for high in range(size // 2)]


def bit_lists(size):
    high = list(range(1, size.bit_length() - 1))
    return high, high[::-1]


def gather_dp(value, size, gate=()):
    width = value.shape[-1] // 2
    pieces = []
    for part, order in zip((value[:, :width], value[:, width:]), bit_lists(size)):
        out, have = part, []
        for bit in order:
            axis = sum(1 for other in have if other > bit)
            out = jnp.stack([out, flip(out, size, bit)], axis=axis)
            have.append(bit)
        pieces.append(out.reshape(-1, width))
    sent = [after(piece, *gate) for piece in pieces] if gate else pieces
    return pieces + [flip(piece, size, 0) for piece in sent]


def scatter_dp(own, other, size):
    rows, width = own.shape[0] * 2 // size, own.shape[1]
    got = flip(other, size, 0)
    summed = (own.astype(f32) + got.astype(f32)).astype(bf16)
    highs = size.bit_length() - 2
    halves, last = [], []
    for half, order in enumerate(bit_lists(size)):
        cur = summed[:, half * (width // 2) : (half + 1) * (width // 2)]
        cur = cur.reshape([2] * highs + [rows, width // 2])
        left = list(range(highs, 0, -1))
        for k, bit in enumerate(order):
            axis = left.index(bit)
            left.remove(bit)
            keep = lax.index_in_dim(cur, 0, axis, keepdims=False)
            send = lax.index_in_dim(cur, 1, axis, keepdims=False)
            brought = flip(send, size, bit)
            total = keep.astype(f32) + brought.astype(f32)
            cur = total if k == len(order) - 1 else total.astype(bf16)
        halves.append(cur)
        last.append(brought)
    return jnp.concatenate(halves, axis=-1), summed, last


def sum_dp(value, size):
    count = size.bit_length() - 1
    shape = value.shape
    value = value[:2].reshape((2,) + (2,) * count + (-1,))
    for bit in range(count):
        value = value + jnp.flip(flip(value, size, bit), 1 if bit == 0 else count - bit + 1)
    return jnp.pad(value.reshape(2, shape[1]), ((0, 6), (0, 0)))


def line(value, zs, step):
    return lax.ppermute(value, "z", [(j, j + step) for j in range(zs) if 0 <= j + step < zs])


def all_after(values, deps):
    return list(lax.optimization_barrier(tuple(values) + tuple(deps))[: len(values)])


def gather_z(value, zs, zi, gates={}):
    right, left = [value], [value]
    for s in range(1, zs):
        sent = all_after([right[-1], left[-1]], gates[s]) if s in gates else [right[-1], left[-1]]
        right.append(line(sent[0], zs, 1))
        left.append(line(sent[1], zs, -1))
    blocks = [value] + [jnp.where(zi >= k, right[k], left[zs - k]) for k in range(1, zs)]
    return blocks, list(zip(right, left))


def true_order(blocks, zs, zi):
    out = jnp.zeros((zs,) + blocks[0].shape, blocks[0].dtype)
    for k, block in enumerate(blocks):
        out = lax.dynamic_update_index_in_dim(out, block, (zi - k) % zs, 0)
    return out


def scatter_z(parts, gates={}):
    zs = len(parts)
    right, left = None, None
    steps = []
    for s in range(1, zs):
        go_right = parts[s] if right is None else (parts[s].astype(f32) + right).astype(bf16)
        go_left = parts[zs - s] if left is None else (parts[zs - s].astype(f32) + left).astype(bf16)
        if s in gates:
            go_right, go_left = all_after([go_right, go_left], gates[s](steps))
        got_right, got_left = line(go_right, zs, 1), line(go_left, zs, -1)
        steps.append((got_right, got_left))
        right, left = got_right.astype(f32), got_left.astype(f32)
    return parts[0].astype(f32) + right + left, steps


def swap_core(value):
    return lax.ppermute(value, "c", [(0, 1), (1, 0)])


def both_cores(blocks):
    got = jnp.concatenate(blocks, axis=0)
    return jnp.concatenate([got, swap_core(got)], axis=0)


def mix_cores(parts):
    half = parts.shape[0] // 2
    return (parts[:half].astype(f32) + swap_core(parts[half:]).astype(f32)).astype(bf16)


def z_blocks(mixed, zs):
    block = mixed.shape[0] // zs
    return [mixed[k * block : (k + 1) * block] for k in range(zs)]


BLOCK = 4 * LEN


def kdot(a, b, ca, cb):
    return lax.dot_general(a, b, (((ca,), (cb,)), ((), ())), preferred_element_type=f32)


def to_rows(first, second):
    lane = lax.broadcasted_iota(jnp.int32, (first.shape[0], 128), 1)
    both = jnp.where(lane == 0, first, jnp.where(lane == 1, second, 0.0))
    return both.T[:8]


def to_cols(block):
    cols = jnp.concatenate([block] * 16, axis=0).T
    return cols[:, 0:1], cols[:, 1:2]


def own_rows(half):
    return pl.program_id(0) < half


def picked_rows(half, own_ref, other_ref):
    return jnp.where(own_rows(half), own_ref[...].astype(f32), other_ref[...].astype(f32))


def store_rows(half, own_ref, other_ref, value):
    @pl.when(own_rows(half))
    def _():
        own_ref[...] = value

    @pl.when(jnp.logical_not(own_rows(half)))
    def _():
        other_ref[...] = value


def qkv_kernel(
    width, half, a_own, b_own, a_other, b_other, gain_ref, w_ref, hid_ref, raw_ref, sum_ref
):
    x_a = picked_rows(half, a_own, a_other)
    x_b = picked_rows(half, b_own, b_other)
    square = jnp.sum(x_a * x_a, axis=-1, keepdims=True) + jnp.sum(x_b * x_b, axis=-1, keepdims=True)
    inverse = lax.rsqrt(square / D + NORM_EPS)
    hid_ref[:, : D // 2] = (x_a * inverse * gain_ref[:, : D // 2]).astype(bf16)
    hid_ref[:, D // 2 :] = (x_b * inverse * gain_ref[:, D // 2 :]).astype(bf16)
    raw = kdot(hid_ref[...], w_ref[...], 1, 1)
    raw_ref[...] = raw
    q, k = raw[:, :width], raw[:, width : 2 * width]
    sum_ref[...] = to_rows(
        jnp.sum(q * q, axis=-1, keepdims=True), jnp.sum(k * k, axis=-1, keepdims=True)
    )


def spin(x, cos, sin):
    return x * cos + pltpu.roll(x, HD // 2, 1) * sin


def heads_of(raw, inv_q, inv_k, gain_ref, cos, sin, width, head):
    lo = head * HD
    normed_q = raw[:, lo : lo + HD] * inv_q
    normed_k = raw[:, width + lo : width + lo + HD] * inv_k
    query = spin(normed_q * gain_ref[0:1, lo : lo + HD], cos, sin).astype(bf16)
    key = spin(normed_k * gain_ref[1:2, lo : lo + HD], cos, sin).astype(bf16)
    value = raw[:, 2 * width + lo : 2 * width + lo + HD].astype(bf16)
    return normed_q, normed_k, query, key, value


def probs_of(query, key, mask):
    scores = jnp.where(mask > 0.5, kdot(query, key, 1, 1) * HD ** (-0.5), -1e30)
    scores = jnp.exp(scores - jnp.max(scores, axis=-1, keepdims=True))
    return scores / jnp.sum(scores, axis=-1, keepdims=True)


def inverses(sum_ref):
    ss_q, ss_k = to_cols(sum_ref[...])
    return lax.rsqrt(ss_q / D + NORM_EPS), lax.rsqrt(ss_k / D + NORM_EPS)


def attend_kernel(
    width, half, raw_ref, sum_ref, gain_ref, cos_ref, sin_ref, mask_ref, w_ref,
    att_ref, own_ref, other_ref,
):
    inv_q, inv_k = inverses(sum_ref)
    raw = raw_ref[...]
    cos, sin = cos_ref[...], sin_ref[...]
    for head in range(width // HD):
        _, _, query, key, value = heads_of(raw, inv_q, inv_k, gain_ref, cos, sin, width, head)
        for s in range(BLOCK // LEN):
            at = slice(s * LEN, (s + 1) * LEN)
            probs = probs_of(query[at], key[at], mask_ref[s])
            att_ref[at, head * HD : (head + 1) * HD] = kdot(
                probs.astype(bf16), value[at], 1, 0
            ).astype(bf16)
    store_rows(half, own_ref, other_ref, kdot(att_ref[...], w_ref[...], 1, 1).astype(bf16))


def attend_back_kernel(
    width, half, raw_ref, sum_ref, gain_ref, cos_ref, sin_ref, mask_ref, w_ref, att_ref,
    a_own, b_own, a_other, b_other, back_ref, dv_ref, dot_ref, gsum_ref, gout_ref,
):
    inv_q, inv_k = inverses(sum_ref)
    raw = raw_ref[...]
    cos, sin = cos_ref[...], sin_ref[...]
    grad_a = picked_rows(half, a_own, a_other).astype(bf16)
    grad_b = picked_rows(half, b_own, b_other).astype(bf16)
    grad_heads = kdot(grad_a, w_ref[: D // 2], 1, 0) + kdot(grad_b, w_ref[D // 2 :], 1, 0)
    grad_heads = grad_heads.astype(bf16)

    @pl.when(pl.program_id(0) == 0)
    def _():
        gsum_ref[...] = jnp.zeros_like(gsum_ref)
        gout_ref[...] = jnp.zeros_like(gout_ref)

    gout_ref[: D // 2] += kdot(grad_a, att_ref[...], 0, 0)
    gout_ref[D // 2 :] += kdot(grad_b, att_ref[...], 0, 0)

    dot_q = dot_k = 0.0
    for head in range(width // HD):
        lo = head * HD
        normed_q, normed_k, query, key, value = heads_of(
            raw, inv_q, inv_k, gain_ref, cos, sin, width, head
        )
        grads_q, grads_k = [], []
        for s in range(BLOCK // LEN):
            at = slice(s * LEN, (s + 1) * LEN)
            probs = probs_of(query[at], key[at], mask_ref[s])
            grad = grad_heads[at, lo : lo + HD]
            grad_probs = kdot(grad, value[at], 1, 1)
            dv_ref[at, lo : lo + HD] = kdot(probs.astype(bf16), grad, 0, 0).astype(bf16)
            delta = jnp.sum(probs * grad_probs, axis=-1, keepdims=True)
            grad_scores = (probs * (grad_probs - delta)).astype(bf16)
            grads_q.append(kdot(grad_scores, key[at], 1, 0))
            grads_k.append(kdot(grad_scores, query[at], 0, 0))
        grad_nq = spin(jnp.concatenate(grads_q, axis=0) * HD ** (-0.5), cos, -sin)
        grad_nk = spin(jnp.concatenate(grads_k, axis=0) * HD ** (-0.5), cos, -sin)
        prod_q, prod_k = grad_nq * normed_q, grad_nk * normed_k
        gsum_ref[0:1, lo : lo + HD] += jnp.sum(prod_q, axis=0, keepdims=True)
        gsum_ref[1:2, lo : lo + HD] += jnp.sum(prod_k, axis=0, keepdims=True)
        gain_q, gain_k = gain_ref[0:1, lo : lo + HD], gain_ref[1:2, lo : lo + HD]
        dot_q = dot_q + jnp.sum(prod_q * gain_q, axis=-1, keepdims=True)
        dot_k = dot_k + jnp.sum(prod_k * gain_k, axis=-1, keepdims=True)
        back_ref[:, lo : lo + HD] = grad_nq * gain_q
        back_ref[:, width + lo : width + lo + HD] = grad_nk * gain_k
    dot_ref[...] = to_rows(dot_q, dot_k)


def project_back_kernel(
    width, half, raw_ref, sum_ref, back_ref, dv_ref, dot_ref, w_ref, proj_ref, own_ref, other_ref
):
    inv_q, inv_k = inverses(sum_ref)
    mean_q, mean_k = to_cols(dot_ref[...] / D)
    normed_q = raw_ref[:, :width] * inv_q
    normed_k = raw_ref[:, width : 2 * width] * inv_k
    proj_ref[:, :width] = (inv_q * (back_ref[:, :width] - normed_q * mean_q)).astype(bf16)
    proj_ref[:, width : 2 * width] = (
        inv_k * (back_ref[:, width:] - normed_k * mean_k)
    ).astype(bf16)
    proj_ref[:, 2 * width :] = dv_ref[...]
    store_rows(half, own_ref, other_ref, kdot(proj_ref[...], w_ref[...], 1, 0).astype(bf16))


def by_rows(cols):
    return pl.BlockSpec((BLOCK, cols), lambda i: (i, 0))


def pieces_spec(half, cols):
    own = pl.BlockSpec((BLOCK, cols), lambda i: (jnp.minimum(i, half - 1), 0))
    other = pl.BlockSpec((BLOCK, cols), lambda i: (jnp.maximum(i - half, 0), 0))
    return own, other


def across(rows):
    return pl.BlockSpec((rows, BLOCK), lambda i: (0, i))


def whole(shape):
    return pl.BlockSpec(shape, lambda i: (0,) * len(shape))


def run_blocks(body, rows, in_specs, out_specs, out_shape, args):
    return pl.pallas_call(
        body,
        grid=(rows // BLOCK,),
        in_specs=in_specs,
        out_specs=out_specs,
        out_shape=out_shape,
        cost_estimate=pl.CostEstimate(flops=1, bytes_accessed=1, transcendentals=0),
    )(*args)


def weight_grad_kernel(half, g_ref, u_ref, b_ref, out_ref):
    @pl.when(pl.program_id(1) < half)
    def _():
        out_ref[...] = kdot(g_ref[...], b_ref[...], 0, 0).astype(bf16)

    @pl.when(pl.program_id(1) >= half)
    def _():
        out_ref[...] = kdot(u_ref[...], b_ref[...], 0, 0).astype(bf16)


def weight_grad(g, u, b):
    tile_a, tile_b = 512, 1024
    half = g.shape[1] // tile_a
    return pl.pallas_call(
        functools.partial(weight_grad_kernel, half),
        grid=(b.shape[1] // tile_b, 2 * half),
        in_specs=[
            pl.BlockSpec((g.shape[0], tile_a), lambda n, m: (0, jnp.minimum(m, half - 1))),
            pl.BlockSpec((u.shape[0], tile_a), lambda n, m: (0, jnp.maximum(m - half, 0))),
            pl.BlockSpec((b.shape[0], tile_b), lambda n, m: (0, n)),
        ],
        out_specs=pl.BlockSpec((tile_a, tile_b), lambda n, m: (m, n)),
        out_shape=jax.ShapeDtypeStruct((2 * g.shape[1], b.shape[1]), bf16),
        cost_estimate=pl.CostEstimate(flops=1, bytes_accessed=1, transcendentals=0),
    )(g, u, b)


def shape_of(rows, cols, dtype):
    return jax.ShapeDtypeStruct((rows, cols), dtype)


def per_device(
    tokens, cotangent, segments, routes, w_qkv, w_out, norm_gains, w_router, w_gate_up, w_down
):
    zs = lax.axis_size("z")
    dps = lax.axis_size("q") * 2
    world = dps * zs
    qi, ci, zi = lax.axis_index("q"), lax.axis_index("c"), lax.axis_index("z")
    di = qi * 2 + ci
    rows = tokens.shape[0]
    seqs = rows // LEN
    width = D // dps
    local_experts = E // zs
    mine = local_experts // 2
    sub = w_qkv.shape[0] // 3
    orow = w_out.shape[0]
    all_rows = dps * rows
    all_seqs = dps * seqs

    def unit_perm(t, back):
        pairs = []
        for i in range(dps):
            for j in range(zs):
                dest = (3 * i + (3 * j + t) // zs) % dps
                src_dev, dst_dev = i * zs + j, dest * zs + j
                pairs.append((dst_dev, src_dev) if back else (src_dev, dst_dev))
        return pairs

    moved = [
        lax.ppermute(w_qkv[t * sub : (t + 1) * sub], ALL, unit_perm(t, False)) for t in range(3)
    ]
    def in_core_order(own, got):
        first = ci == 0
        return jnp.where(first, own, got), jnp.where(first, got, own)

    def core_half(weight):
        split = weight.reshape((2, mine) + weight.shape[1:])
        got = swap_core(lax.dynamic_index_in_dim(split, 1 - ci, 0, keepdims=False))
        own = lax.dynamic_index_in_dim(split, ci, 0, keepdims=False)
        both = in_core_order(own, got)
        return [jnp.concatenate([half[e] for half in both], axis=0) for e in range(mine)]

    down_half = core_half(w_down)

    mini = jnp.concatenate(
        [
            norm_gains.reshape(-1),
            w_router.reshape(-1),
            segments.astype(bf16).reshape(-1),
            routes.astype(bf16).reshape(-1),
        ]
    )
    minis = lax.all_to_all(
        jnp.broadcast_to(mini[None], (world,) + mini.shape), ALL, 0, 0, tiled=True
    )

    tok_pieces = gather_dp(tokens, dps)
    slots, slot_steps = gather_z(
        after(jnp.concatenate(moved, axis=0), minis, *down_half), zs, zi,
        {s: [] if s < zs - 1 else tok_pieces[:2] for s in range(2, zs)},
    )
    inv3 = pow(3, -1, dps)
    slot_of = [[0, 0, 0] for _ in range(dps)]
    type_of = [[0, 0, 0] for _ in range(dps)]
    for i in range(dps):
        for s in range(3):
            src = (inv3 * (i - s)) % dps
            kind = (3 * src + s) // dps
            slot_of[i][kind] = s
            type_of[i][s] = kind
    slot_of = jnp.asarray(slot_of, jnp.int32)[di]
    type_of = jnp.asarray(type_of, jnp.int32)[di]

    at = 0
    split = []
    for part in (norm_gains, w_router, segments, routes):
        split.append(minis[:, at : at + part.size])
        at += part.size
    gains_f = split[0].reshape(D, 4).astype(f32)
    router_low = split[1].reshape(D, E)
    router_f = router_low.astype(f32)
    seg_all = split[2].reshape(dps, zs, seqs, LEN)
    seg_own = lax.dynamic_index_in_dim(seg_all, zi, 1, keepdims=False)
    seg_own = seg_own[jnp.asarray(relative(dps)) ^ di].reshape(all_seqs, LEN)
    routes_all = split[3].reshape(dps // 2, 2, zs, rows, TOP)
    routes_own = lax.dynamic_index_in_dim(routes_all, qi, 0, keepdims=False)
    routes_own = routes_own[jnp.stack([ci, 1 - ci])][:, (zi - jnp.arange(zs)) % zs]
    routes_g = routes_own.reshape(2 * zs * rows, TOP).astype(jnp.int32)
    position = jnp.arange(LEN)
    causal = position[:, None] >= position[None, :]
    mask = (causal[None] & (seg_own[:, :, None] == seg_own[:, None, :])).astype(f32)
    own_gains = lax.dynamic_slice(gains_f, (di * width, 0), (width, 4))
    gain_rows = jnp.pad(own_gains[:, 1:3].T, ((0, 6), (0, 0)))
    cos_table, sin_table = rope_tables(LEN, HD)
    cos_full = jnp.tile(jnp.concatenate([cos_table, cos_table], axis=1), (BLOCK // LEN, 1))
    sin_full = jnp.tile(jnp.concatenate([-sin_table, sin_table], axis=1), (BLOCK // LEN, 1))

    qkv_slots = true_order(slots, zs, zi).reshape(3, width, D)
    w_three = jnp.concatenate(
        [lax.dynamic_index_in_dim(qkv_slots, slot_of[k], 0, keepdims=False) for k in range(3)],
        axis=0,
    )
    out_cols = after(w_out, *slot_steps[-1]).reshape(orow, dps, width).transpose(1, 0, 2)
    out_cols = jnp.broadcast_to(out_cols[:, None], (dps, zs, orow, width))
    w_out_c = lax.all_to_all(
        out_cols.reshape(world, orow, width), ALL, 0, 0, tiled=True
    ).reshape(D, width)
    first_down = lax.all_gather(down_half[0], "q", axis=0, tiled=True)
    dy_all = lax.all_gather(after(cotangent, first_down, *slot_steps[-1]), "z", axis=0)
    dy_blocks = [
        lax.dynamic_index_in_dim(dy_all, (zi - k) % zs, 0, keepdims=False) for k in range(zs)
    ]

    blocks = all_rows // BLOCK
    half = blocks // 2
    own_spec, other_spec = pieces_spec(half, D // 2)
    piece_specs = [own_spec, own_spec, other_spec, other_spec]
    part_specs = list(pieces_spec(half, D))
    part_shapes = [shape_of(all_rows // 2, D, bf16)] * 2
    hidden_one, raw, sums = run_blocks(
        functools.partial(qkv_kernel, width, half),
        all_rows,
        piece_specs + [whole((1, D)), whole((3 * width, D))],
        [by_rows(D), by_rows(3 * width), across(8)],
        [
            shape_of(all_rows, D, bf16),
            shape_of(all_rows, 3 * width, f32),
            shape_of(8, all_rows, f32),
        ],
        tuple(tok_pieces) + (gains_f[:, 0][None], w_three),
    )
    gu_half = core_half(after(w_gate_up, hidden_one))
    sums = sum_dp(sums, dps)
    mask_spec = pl.BlockSpec((BLOCK // LEN, LEN, LEN), lambda i: (i, 0, 0))
    table_specs = [whole((8, width)), whole((BLOCK, HD)), whole((BLOCK, HD)), mask_spec]
    tables = (gain_rows, cos_full, sin_full, mask)
    attended, own, other = run_blocks(
        functools.partial(attend_kernel, width, half),
        all_rows,
        [by_rows(3 * width), across(8)] + table_specs + [whole((D, width))],
        [by_rows(width)] + part_specs,
        [shape_of(all_rows, width, bf16)] + part_shapes,
        (raw, sums) + tables + (w_out_c,),
    )
    attn_out, _, attn_last = scatter_dp(own, other, dps)

    expert_w = []
    for e in range(mine):
        if e > 0:
            gu_half[e], down_half[e] = all_after([gu_half[e], down_half[e]], attn_last)
        expert_w.append(
            (
                lax.all_gather(gu_half[e], "q", axis=0, tiled=True),
                lax.all_gather(down_half[e], "q", axis=0, tiled=True) if e else first_down,
            )
        )

    x_float = tokens.astype(f32)
    inverse_one = inverse_rms(x_float)
    normed_one = x_float * inverse_one
    residual = x_float + attn_out
    inverse_two = inverse_rms(residual)
    normed_two = residual * inverse_two
    hidden_two = (normed_two * gains_f[:, 3]).astype(bf16)
    router_probs = jax.nn.softmax(mm(hidden_two, router_low, 1, 0), axis=-1)

    dy_g = both_cores(dy_blocks)
    hidden_blocks, _ = gather_z(hidden_two, zs, zi, {2: [dy_g, router_probs]})
    hidden_g = both_cores(hidden_blocks)
    router_g = jax.nn.softmax(mm(hidden_g, router_low, 1, 0), axis=-1)
    dy_f = dy_g.astype(f32)
    first_expert = zi * local_experts + ci * mine

    passes = []
    for e in range(mine):
        gate_up, down = expert_w[e]
        expert = first_expert + e
        picked = jnp.any(routes_g == expert, axis=1, keepdims=True)
        prob = jnp.sum(
            jnp.where(jnp.arange(E)[None] == expert, router_g, 0.0), axis=1, keepdims=True
        )
        gate_val = jnp.where(picked, prob, 0.0)
        hidden_e = after(hidden_g, passes[-1]["rows"]) if passes else hidden_g
        gate_and_up = mm(hidden_e, gate_up, 1, 1)
        g_part = gate_and_up[:, :FF]
        u_part = gate_and_up[:, FF:]
        sig = jax.nn.sigmoid(g_part)
        silu = g_part * sig
        act = (silu * u_part).astype(bf16)
        expert_out = mm(act, down, 1, 1).astype(bf16).astype(f32)
        grad_gate = jnp.where(picked[:, 0], jnp.sum(dy_f * expert_out, axis=1), 0.0)
        grad_eo = (gate_val * dy_f).astype(bf16)
        grad_act = mm(grad_eo, down, 1, 0)
        grad_g = grad_act * u_part * sig * (1.0 + g_part * (1.0 - sig))
        grad_u = grad_act * silu
        grad_g, grad_u = grad_g.astype(bf16), grad_u.astype(bf16)
        grad_both = jnp.concatenate([grad_g, grad_u], axis=-1)
        rows_back = mm(grad_both, gate_up, 1, 0).astype(bf16)
        dn = mm(grad_eo, act, 0, 0).astype(bf16)
        passes.append(
            dict(
                out=gate_val * expert_out,
                back=rows_back.astype(f32),
                rows=rows_back,
                gate=grad_gate,
                both=(grad_g, grad_u),
                dn=lax.psum_scatter(dn, "q", scatter_dimension=0, tiled=True),
            )
        )

    hid_part = sum([p["back"] for p in passes[1:]], passes[0]["back"])
    out_part = sum([p["out"] for p in passes[1:]], passes[0]["out"])
    cols = jnp.stack([p["gate"] for p in passes], axis=0).reshape(mine, 2, zs, rows)
    cols = jnp.where(ci == 0, cols, cols[:, ::-1])
    cols = cols[:, :, (zi - jnp.arange(zs)) % zs]
    hid_mixed = mix_cores(hid_part.astype(bf16))
    out_mixed = mix_cores(out_part.astype(bf16))
    gus = []

    def fill(*deps):
        p = passes[len(gus)]
        gus.append(weight_grad(*all_after(p["both"], deps), hidden_g))
        return gus[-1:]

    hid_gates = {2: lambda steps: fill(hid_mixed), 3: lambda steps: [cols, out_mixed]}
    if mine > 1:
        hid_gates[3] = lambda steps: fill(*steps[0]) + [cols, out_mixed]
    hid_sum, hid_steps = scatter_z(z_blocks(hid_mixed, zs), hid_gates)
    while len(gus) < mine:
        fill(*hid_steps[1])
    grad_hidden = hid_sum
    got = lax.all_to_all(
        cols.transpose(1, 2, 0, 3).reshape(2 * zs, mine, rows), ("c", "z"), 0, 0, tiled=True
    )
    gp = got.reshape(2, zs, mine, rows).transpose(1, 0, 2, 3).reshape(E, rows).T

    grad_logits = router_probs * (gp - jnp.sum(router_probs * gp, axis=-1, keepdims=True))
    grad_router = lax.dot_general(
        hidden_two.astype(f32), grad_logits, (((0,), (0,)), ((), ())), precision=PRECISE
    )
    grad_hidden = grad_hidden + jnp.dot(grad_logits, router_f.T, precision=PRECISE)
    gain_two = jnp.sum(grad_hidden * normed_two, axis=0)
    grad_residual = cotangent.astype(f32) + norm_back(
        grad_hidden * gains_f[:, 3], normed_two, inverse_two
    )

    def core_back(parts):
        stacked = jnp.stack(parts, axis=0)
        split = stacked.reshape((mine, 2, stacked.shape[1] // 2, stacked.shape[2]))
        got = swap_core(lax.dynamic_index_in_dim(split, 1 - ci, 1, keepdims=False))
        own = lax.dynamic_index_in_dim(split, ci, 1, keepdims=False)
        return jnp.concatenate(in_core_order(own, got), axis=0).astype(f32)

    grad_pieces = []

    def out_gate(steps):
        if len(steps) == 1:
            grad_pieces.extend(
                gather_dp(grad_residual.astype(bf16), dps, gate=gus[-1:] + list(steps[0]))
            )
        return []

    out_total, out_steps = scatter_z(
        z_blocks(after(out_mixed, *hid_steps[-1]), zs), {s: out_gate for s in range(2, zs)}
    )
    gus = [after(gu, *hid_steps[0]) for gu in gus[:-1]] + [after(gus[-1], *grad_pieces)]
    gus = [lax.psum_scatter(gu, "q", scatter_dimension=0, tiled=True) for gu in gus]
    back, dv, dots, gain_sums, grad_out_c = run_blocks(
        functools.partial(attend_back_kernel, width, half),
        all_rows,
        [by_rows(3 * width), across(8)] + table_specs + [whole((D, width)), by_rows(width)]
        + piece_specs,
        [by_rows(2 * width), by_rows(width), across(8), whole((8, width)), whole((D, width))],
        [
            shape_of(all_rows, 2 * width, f32),
            shape_of(all_rows, width, bf16),
            shape_of(8, all_rows, f32),
            shape_of(8, width, f32),
            shape_of(D, width, f32),
        ],
        (raw, sums) + tables + (w_out_c, attended) + tuple(grad_pieces),
    )

    def z_parts(value):
        return [
            lax.dynamic_index_in_dim(value, (zi - k) % zs, 0, keepdims=False) for k in range(zs)
        ]

    dots = sum_dp(after(dots, *out_steps[1]), dps)
    grad_projected, own, other = run_blocks(
        functools.partial(project_back_kernel, width, half),
        all_rows,
        [
            by_rows(3 * width), across(8), by_rows(2 * width), by_rows(width), across(8),
            whole((3 * width, D)),
        ],
        [by_rows(3 * width)] + part_specs,
        [shape_of(all_rows, 3 * width, bf16)] + part_shapes,
        (raw, sums, back, dv, dots, w_three),
    )
    grad_h1, h1_summed, h1_last = scatter_dp(own, other, dps)
    gain_one = jnp.sum(grad_h1 * normed_one, axis=0)
    grad_tokens = grad_residual + norm_back(grad_h1 * gains_f[:, 0], normed_one, inverse_one)
    result = residual + out_total

    hidden_late = after(hidden_one, *out_steps[-1])
    grad_three = mm(grad_projected, hidden_late, 0, 0).astype(bf16).reshape(3, width, D)
    grad_slots = jnp.concatenate(
        [lax.dynamic_index_in_dim(grad_three, type_of[s], 0, keepdims=True) for s in range(3)],
        axis=0,
    )
    grad_cols = grad_out_c.astype(bf16).reshape(dps, zs, orow, width).transpose(1, 2, 0, 3)
    parts = jnp.concatenate(
        [grad_slots.reshape(zs, 3 * sub, D), grad_cols.reshape(zs, orow, D)], axis=1
    )
    dns = [p["dn"] for p in passes]
    grad_down = core_back([after(dns[0], grad_projected)] + dns[1:])
    own_sum, own_steps = scatter_z(z_parts(parts), {s: lambda steps: [] if steps else [h1_summed] for s in range(1, zs)})
    grad_gate_up = core_back([after(gus[0], *own_steps[1])] + gus[1:])
    own_sum = after(own_sum.astype(bf16), grad_down)
    grad_qkv = jnp.concatenate(
        [
            lax.ppermute(own_sum[t * sub : (t + 1) * sub], ALL, unit_perm(t, True))
            for t in range(3)
        ],
        axis=0,
    ).astype(f32)
    own_cols = own_sum[3 * sub :].reshape(orow, dps, width).transpose(1, 0, 2)
    grad_out = (
        lax.all_to_all(own_cols, DP, 0, 0, tiled=True)
        .transpose(1, 0, 2)
        .reshape(orow, D)
        .astype(f32)
    )

    shard_cols = lax.dynamic_update_slice(jnp.zeros((D, 2), f32), gain_sums[:2].T, (di * width, 0))
    small_grads = jnp.concatenate(
        [gain_one[:, None], shard_cols, gain_two[:, None], grad_router], axis=1
    )
    small_own = jnp.sum(
        lax.all_to_all(
            small_grads.reshape(world, D * (E + 4) // world), ALL, 0, 0, tiled=True
        ),
        axis=0,
    ).reshape(D // world, E + 4)

    return (
        result.astype(bf16),
        grad_tokens,
        grad_qkv,
        grad_out,
        small_own[:, :4],
        small_own[:, 4:],
        grad_gate_up,
        grad_down,
    )


def solution(mesh):
    dps, zs = mesh.shape["dp"], mesh.shape["fsdp"]
    inner = Mesh(mesh.devices.reshape(dps // 2, 2, zs), ALL)
    rows = P(ALL, None)
    experts = P("z", DP, None)
    in_specs = (rows,) * 8 + (experts,) * 2
    out_specs = (rows,) * 6 + (experts,) * 2
    return jax.shard_map(
        per_device, mesh=inner, in_specs=in_specs, out_specs=out_specs, check_vma=False
    )
```

```python
import functools

import jax
import jax.numpy as jnp
from jax import lax
from jax.experimental import pallas as pl
from jax.experimental.pallas import tpu as pltpu
from jax.sharding import Mesh
from jax.sharding import PartitionSpec as P

D = 2048
H = 16
HD = 128
FF = 1024
TOP = 8
E = 16
LEN = 96

NORM_EPS = 1e-05
ROPE_BASE = 10000.0
PRECISE = lax.Precision.HIGHEST
DP = ("q", "c")
ALL = ("q", "c", "z")
f32 = jnp.float32
bf16 = jnp.bfloat16


def inverse_rms(field_in):
    return lax.rsqrt(jnp.mean(field_in * field_in, axis=-1, keepdims=True) + NORM_EPS)


def rope_tables(length, head_dim):
    half_dim = head_dim // 2
    frequency = ROPE_BASE ** (-(jnp.arange(half_dim).astype(f32) * 2.0) / head_dim)
    angles = jnp.arange(length).astype(f32)[:, None] * frequency[None, :]
    return jnp.cos(angles), jnp.sin(angles)


def norm_back(grad_normed, normed, inverse):
    return inverse * (grad_normed - normed * jnp.mean(grad_normed * normed, axis=-1, keepdims=True))


def mm(a, b, ca, cb):
    return lax.dot_general(a, b, (((ca,), (cb,)), ((), ())), preferred_element_type=f32)


def after(value, *deps):
    return lax.optimization_barrier((value,) + tuple(deps))[0]


def flip(value, size, bit):
    return lax.ppermute(value, DP, [(i, i ^ (1 << bit)) for i in range(size)])


def relative(size):
    return [high * 2 + core for core in range(2) for high in range(size // 2)]


def bit_lists(size):
    high = list(range(1, size.bit_length() - 1))
    return high, high[::-1]


def gather_dp(value, size, gate=()):
    width = value.shape[-1] // 2
    pieces = []
    for part, order in zip((value[:, :width], value[:, width:]), bit_lists(size)):
        out, have = part, []
        for bit in order:
            axis = sum(1 for other in have if other > bit)
            out = jnp.stack([out, flip(out, size, bit)], axis=axis)
            have.append(bit)
        pieces.append(out.reshape(-1, width))
    sent = [after(piece, *gate) for piece in pieces] if gate else pieces
    return pieces + [flip(piece, size, 0) for piece in sent]


def scatter_dp(own, other, size):
    rows, width = own.shape[0] * 2 // size, own.shape[1]
    got = flip(other, size, 0)
    summed = (own.astype(f32) + got.astype(f32)).astype(bf16)
    highs = size.bit_length() - 2
    halves, last = [], []
    for half, order in enumerate(bit_lists(size)):
        cur = summed[:, half * (width // 2) : (half + 1) * (width // 2)]
        cur = cur.reshape([2] * highs + [rows, width // 2])
        left = list(range(highs, 0, -1))
        for k, bit in enumerate(order):
            axis = left.index(bit)
            left.remove(bit)
            keep = lax.index_in_dim(cur, 0, axis, keepdims=False)
            send = lax.index_in_dim(cur, 1, axis, keepdims=False)
            brought = flip(send, size, bit)
            total = keep.astype(f32) + brought.astype(f32)
            cur = total if k == len(order) - 1 else total.astype(bf16)
        halves.append(cur)
        last.append(brought)
    return jnp.concatenate(halves, axis=-1), summed, last


def sum_dp(value, size):
    count = size.bit_length() - 1
    shape = value.shape
    value = value[:2].reshape((2,) + (2,) * count + (-1,))
    for bit in range(count):
        value = value + jnp.flip(flip(value, size, bit), 1 if bit == 0 else count - bit + 1)
    return jnp.pad(value.reshape(2, shape[1]), ((0, 6), (0, 0)))


def line(value, zs, step):
    return lax.ppermute(value, "z", [(j, j + step) for j in range(zs) if 0 <= j + step < zs])


def all_after(values, deps):
    return list(lax.optimization_barrier(tuple(values) + tuple(deps))[: len(values)])


def gather_z(value, zs, zi, gates={}):
    right, left = [value], [value]
    for s in range(1, zs):
        sent = all_after([right[-1], left[-1]], gates[s]) if s in gates else [right[-1], left[-1]]
        right.append(line(sent[0], zs, 1))
        left.append(line(sent[1], zs, -1))
    blocks = [value] + [jnp.where(zi >= k, right[k], left[zs - k]) for k in range(1, zs)]
    return blocks, list(zip(right, left))


def true_order(blocks, zs, zi):
    out = jnp.zeros((zs,) + blocks[0].shape, blocks[0].dtype)
    for k, block in enumerate(blocks):
        out = lax.dynamic_update_index_in_dim(out, block, (zi - k) % zs, 0)
    return out


def scatter_z(parts, gates={}):
    zs = len(parts)
    right, left = None, None
    steps = []
    for s in range(1, zs):
        go_right = parts[s] if right is None else (parts[s].astype(f32) + right).astype(bf16)
        go_left = parts[zs - s] if left is None else (parts[zs - s].astype(f32) + left).astype(bf16)
        if s in gates:
            go_right, go_left = all_after([go_right, go_left], gates[s](steps))
        got_right, got_left = line(go_right, zs, 1), line(go_left, zs, -1)
        steps.append((got_right, got_left))
        right, left = got_right.astype(f32), got_left.astype(f32)
    return parts[0].astype(f32) + right + left, steps


def swap_core(value):
    return lax.ppermute(value, "c", [(0, 1), (1, 0)])


def both_cores(blocks):
    got = jnp.concatenate(blocks, axis=0)
    return jnp.concatenate([got, swap_core(got)], axis=0)


def mix_cores(parts):
    half = parts.shape[0] // 2
    return (parts[:half].astype(f32) + swap_core(parts[half:]).astype(f32)).astype(bf16)


def z_blocks(mixed, zs):
    block = mixed.shape[0] // zs
    return [mixed[k * block : (k + 1) * block] for k in range(zs)]


BLOCK = 4 * LEN


def kdot(a, b, ca, cb):
    return lax.dot_general(a, b, (((ca,), (cb,)), ((), ())), preferred_element_type=f32)


def to_rows(first, second):
    lane = lax.broadcasted_iota(jnp.int32, (first.shape[0], 128), 1)
    both = jnp.where(lane == 0, first, jnp.where(lane == 1, second, 0.0))
    return both.T[:8]


def to_cols(block):
    cols = jnp.concatenate([block] * 16, axis=0).T
    return cols[:, 0:1], cols[:, 1:2]


def own_rows(half):
    return pl.program_id(0) < half


def picked_rows(half, own_ref, other_ref):
    return jnp.where(own_rows(half), own_ref[...].astype(f32), other_ref[...].astype(f32))


def store_rows(half, own_ref, other_ref, value):
    @pl.when(own_rows(half))
    def _():
        own_ref[...] = value

    @pl.when(jnp.logical_not(own_rows(half)))
    def _():
        other_ref[...] = value


def qkv_kernel(
    width, half, a_own, b_own, a_other, b_other, gain_ref, w_ref, hid_ref, raw_ref, sum_ref
):
    x_a = picked_rows(half, a_own, a_other)
    x_b = picked_rows(half, b_own, b_other)
    square = jnp.sum(x_a * x_a, axis=-1, keepdims=True) + jnp.sum(x_b * x_b, axis=-1, keepdims=True)
    inverse = lax.rsqrt(square / D + NORM_EPS)
    hid_ref[:, : D // 2] = (x_a * inverse * gain_ref[:, : D // 2]).astype(bf16)
    hid_ref[:, D // 2 :] = (x_b * inverse * gain_ref[:, D // 2 :]).astype(bf16)
    raw = kdot(hid_ref[...], w_ref[...], 1, 1)
    raw_ref[...] = raw
    q, k = raw[:, :width], raw[:, width : 2 * width]
    sum_ref[...] = to_rows(
        jnp.sum(q * q, axis=-1, keepdims=True), jnp.sum(k * k, axis=-1, keepdims=True)
    )


def spin(x, cos, sin):
    return x * cos + pltpu.roll(x, HD // 2, 1) * sin


def heads_of(raw, inv_q, inv_k, gain_ref, cos, sin, width, head):
    lo = head * HD
    normed_q = raw[:, lo : lo + HD] * inv_q
    normed_k = raw[:, width + lo : width + lo + HD] * inv_k
    query = spin(normed_q * gain_ref[0:1, lo : lo + HD], cos, sin).astype(bf16)
    key = spin(normed_k * gain_ref[1:2, lo : lo + HD], cos, sin).astype(bf16)
    value = raw[:, 2 * width + lo : 2 * width + lo + HD].astype(bf16)
    return normed_q, normed_k, query, key, value


def probs_of(query, key, mask):
    scores = jnp.where(mask > 0.5, kdot(query, key, 1, 1) * HD ** (-0.5), -1e30)
    scores = jnp.exp(scores - jnp.max(scores, axis=-1, keepdims=True))
    return scores / jnp.sum(scores, axis=-1, keepdims=True)


def inverses(sum_ref):
    ss_q, ss_k = to_cols(sum_ref[...])
    return lax.rsqrt(ss_q / D + NORM_EPS), lax.rsqrt(ss_k / D + NORM_EPS)


def attend_kernel(
    width, half, raw_ref, sum_ref, gain_ref, cos_ref, sin_ref, mask_ref, w_ref,
    att_ref, own_ref, other_ref,
):
    inv_q, inv_k = inverses(sum_ref)
    raw = raw_ref[...]
    cos, sin = cos_ref[...], sin_ref[...]
    for head in range(width // HD):
        _, _, query, key, value = heads_of(raw, inv_q, inv_k, gain_ref, cos, sin, width, head)
        for s in range(BLOCK // LEN):
            at = slice(s * LEN, (s + 1) * LEN)
            probs = probs_of(query[at], key[at], mask_ref[s])
            att_ref[at, head * HD : (head + 1) * HD] = kdot(
                probs.astype(bf16), value[at], 1, 0
            ).astype(bf16)
    store_rows(half, own_ref, other_ref, kdot(att_ref[...], w_ref[...], 1, 1).astype(bf16))


def attend_back_kernel(
    width, half, raw_ref, sum_ref, gain_ref, cos_ref, sin_ref, mask_ref, w_ref, att_ref,
    a_own, b_own, a_other, b_other, back_ref, dv_ref, dot_ref, gsum_ref, gout_ref,
):
    inv_q, inv_k = inverses(sum_ref)
    raw = raw_ref[...]
    cos, sin = cos_ref[...], sin_ref[...]
    grad_a = picked_rows(half, a_own, a_other).astype(bf16)
    grad_b = picked_rows(half, b_own, b_other).astype(bf16)
    grad_heads = kdot(grad_a, w_ref[: D // 2], 1, 0) + kdot(grad_b, w_ref[D // 2 :], 1, 0)
    grad_heads = grad_heads.astype(bf16)

    @pl.when(pl.program_id(0) == 0)
    def _():
        gsum_ref[...] = jnp.zeros_like(gsum_ref)
        gout_ref[...] = jnp.zeros_like(gout_ref)

    gout_ref[: D // 2] += kdot(grad_a, att_ref[...], 0, 0)
    gout_ref[D // 2 :] += kdot(grad_b, att_ref[...], 0, 0)

    dot_q = dot_k = 0.0
    for head in range(width // HD):
        lo = head * HD
        normed_q, normed_k, query, key, value = heads_of(
            raw, inv_q, inv_k, gain_ref, cos, sin, width, head
        )
        grads_q, grads_k = [], []
        for s in range(BLOCK // LEN):
            at = slice(s * LEN, (s + 1) * LEN)
            probs = probs_of(query[at], key[at], mask_ref[s])
            grad = grad_heads[at, lo : lo + HD]
            grad_probs = kdot(grad, value[at], 1, 1)
            dv_ref[at, lo : lo + HD] = kdot(probs.astype(bf16), grad, 0, 0).astype(bf16)
            delta = jnp.sum(probs * grad_probs, axis=-1, keepdims=True)
            grad_scores = (probs * (grad_probs - delta)).astype(bf16)
            grads_q.append(kdot(grad_scores, key[at], 1, 0))
            grads_k.append(kdot(grad_scores, query[at], 0, 0))
        grad_nq = spin(jnp.concatenate(grads_q, axis=0) * HD ** (-0.5), cos, -sin)
        grad_nk = spin(jnp.concatenate(grads_k, axis=0) * HD ** (-0.5), cos, -sin)
        prod_q, prod_k = grad_nq * normed_q, grad_nk * normed_k
        gsum_ref[0:1, lo : lo + HD] += jnp.sum(prod_q, axis=0, keepdims=True)
        gsum_ref[1:2, lo : lo + HD] += jnp.sum(prod_k, axis=0, keepdims=True)
        gain_q, gain_k = gain_ref[0:1, lo : lo + HD], gain_ref[1:2, lo : lo + HD]
        dot_q = dot_q + jnp.sum(prod_q * gain_q, axis=-1, keepdims=True)
        dot_k = dot_k + jnp.sum(prod_k * gain_k, axis=-1, keepdims=True)
        back_ref[:, lo : lo + HD] = grad_nq * gain_q
        back_ref[:, width + lo : width + lo + HD] = grad_nk * gain_k
    dot_ref[...] = to_rows(dot_q, dot_k)


def project_back_kernel(
    width, half, raw_ref, sum_ref, back_ref, dv_ref, dot_ref, w_ref, proj_ref, own_ref, other_ref
):
    inv_q, inv_k = inverses(sum_ref)
    mean_q, mean_k = to_cols(dot_ref[...] / D)
    normed_q = raw_ref[:, :width] * inv_q
    normed_k = raw_ref[:, width : 2 * width] * inv_k
    proj_ref[:, :width] = (inv_q * (back_ref[:, :width] - normed_q * mean_q)).astype(bf16)
    proj_ref[:, width : 2 * width] = (
        inv_k * (back_ref[:, width:] - normed_k * mean_k)
    ).astype(bf16)
    proj_ref[:, 2 * width :] = dv_ref[...]
    store_rows(half, own_ref, other_ref, kdot(proj_ref[...], w_ref[...], 1, 0).astype(bf16))


def by_rows(cols):
    return pl.BlockSpec((BLOCK, cols), lambda i: (i, 0))


def pieces_spec(half, cols):
    own = pl.BlockSpec((BLOCK, cols), lambda i: (jnp.minimum(i, half - 1), 0))
    other = pl.BlockSpec((BLOCK, cols), lambda i: (jnp.maximum(i - half, 0), 0))
    return own, other


def across(rows):
    return pl.BlockSpec((rows, BLOCK), lambda i: (0, i))


def whole(shape):
    return pl.BlockSpec(shape, lambda i: (0,) * len(shape))


def run_blocks(body, rows, in_specs, out_specs, out_shape, args):
    return pl.pallas_call(
        body,
        grid=(rows // BLOCK,),
        in_specs=in_specs,
        out_specs=out_specs,
        out_shape=out_shape,
        cost_estimate=pl.CostEstimate(flops=1, bytes_accessed=1, transcendentals=0),
    )(*args)


def weight_grad_kernel(half, g_ref, u_ref, b_ref, out_ref):
    @pl.when(pl.program_id(1) < half)
    def _():
        out_ref[...] = kdot(g_ref[...], b_ref[...], 0, 0).astype(bf16)

    @pl.when(pl.program_id(1) >= half)
    def _():
        out_ref[...] = kdot(u_ref[...], b_ref[...], 0, 0).astype(bf16)


def weight_grad(g, u, b):
    tile_a, tile_b = 512, 1024
    half = g.shape[1] // tile_a
    return pl.pallas_call(
        functools.partial(weight_grad_kernel, half),
        grid=(b.shape[1] // tile_b, 2 * half),
        in_specs=[
            pl.BlockSpec((g.shape[0], tile_a), lambda n, m: (0, jnp.minimum(m, half - 1))),
            pl.BlockSpec((u.shape[0], tile_a), lambda n, m: (0, jnp.maximum(m - half, 0))),
            pl.BlockSpec((b.shape[0], tile_b), lambda n, m: (0, n)),
        ],
        out_specs=pl.BlockSpec((tile_a, tile_b), lambda n, m: (m, n)),
        out_shape=jax.ShapeDtypeStruct((2 * g.shape[1], b.shape[1]), bf16),
        cost_estimate=pl.CostEstimate(flops=1, bytes_accessed=1, transcendentals=0),
    )(g, u, b)


def shape_of(rows, cols, dtype):
    return jax.ShapeDtypeStruct((rows, cols), dtype)


def per_device(
    tokens, cotangent, segments, routes, w_qkv, w_out, norm_gains, w_router, w_gate_up, w_down
):
    zs = lax.axis_size("z")
    dps = lax.axis_size("q") * 2
    world = dps * zs
    qi, ci, zi = lax.axis_index("q"), lax.axis_index("c"), lax.axis_index("z")
    di = qi * 2 + ci
    rows = tokens.shape[0]
    seqs = rows // LEN
    width = D // dps
    local_experts = E // zs
    mine = local_experts // 2
    sub = w_qkv.shape[0] // 3
    orow = w_out.shape[0]
    all_rows = dps * rows
    all_seqs = dps * seqs

    def unit_perm(t, back):
        pairs = []
        for i in range(dps):
            for j in range(zs):
                dest = (3 * i + (3 * j + t) // zs) % dps
                src_dev, dst_dev = i * zs + j, dest * zs + j
                pairs.append((dst_dev, src_dev) if back else (src_dev, dst_dev))
        return pairs

    moved = [
        lax.ppermute(w_qkv[t * sub : (t + 1) * sub], ALL, unit_perm(t, False)) for t in range(3)
    ]
    def in_core_order(own, got):
        first = ci == 0
        return jnp.where(first, own, got), jnp.where(first, got, own)

    def core_half(weight):
        split = weight.reshape((2, mine) + weight.shape[1:])
        got = swap_core(lax.dynamic_index_in_dim(split, 1 - ci, 0, keepdims=False))
        own = lax.dynamic_index_in_dim(split, ci, 0, keepdims=False)
        both = in_core_order(own, got)
        return [jnp.concatenate([half[e] for half in both], axis=0) for e in range(mine)]

    down_half = core_half(w_down)

    mini = jnp.concatenate(
        [
            norm_gains.reshape(-1),
            w_router.reshape(-1),
            segments.astype(bf16).reshape(-1),
            routes.astype(bf16).reshape(-1),
        ]
    )
    minis = lax.all_to_all(
        jnp.broadcast_to(mini[None], (world,) + mini.shape), ALL, 0, 0, tiled=True
    )

    tok_pieces = gather_dp(tokens, dps)
    slots, slot_steps = gather_z(
        after(jnp.concatenate(moved, axis=0), minis, *down_half), zs, zi,
        {s: [] if s < zs - 1 else tok_pieces[:2] for s in range(2, zs)},
    )
    inv3 = pow(3, -1, dps)
    slot_of = [[0, 0, 0] for _ in range(dps)]
    type_of = [[0, 0, 0] for _ in range(dps)]
    for i in range(dps):
        for s in range(3):
            src = (inv3 * (i - s)) % dps
            kind = (3 * src + s) // dps
            slot_of[i][kind] = s
            type_of[i][s] = kind
    slot_of = jnp.asarray(slot_of, jnp.int32)[di]
    type_of = jnp.asarray(type_of, jnp.int32)[di]

    at = 0
    split = []
    for part in (norm_gains, w_router, segments, routes):
        split.append(minis[:, at : at + part.size])
        at += part.size
    gains_f = split[0].reshape(D, 4).astype(f32)
    router_low = split[1].reshape(D, E)
    router_f = router_low.astype(f32)
    seg_all = split[2].reshape(dps, zs, seqs, LEN)
    seg_own = lax.dynamic_index_in_dim(seg_all, zi, 1, keepdims=False)
    seg_own = seg_own[jnp.asarray(relative(dps)) ^ di].reshape(all_seqs, LEN)
    routes_all = split[3].reshape(dps // 2, 2, zs, rows, TOP)
    routes_own = lax.dynamic_index_in_dim(routes_all, qi, 0, keepdims=False)
    routes_own = routes_own[jnp.stack([ci, 1 - ci])][:, (zi - jnp.arange(zs)) % zs]
    routes_g = routes_own.reshape(2 * zs * rows, TOP).astype(jnp.int32)
    position = jnp.arange(LEN)
    causal = position[:, None] >= position[None, :]
    mask = (causal[None] & (seg_own[:, :, None] == seg_own[:, None, :])).astype(f32)
    own_gains = lax.dynamic_slice(gains_f, (di * width, 0), (width, 4))
    gain_rows = jnp.pad(own_gains[:, 1:3].T, ((0, 6), (0, 0)))
    cos_table, sin_table = rope_tables(LEN, HD)
    cos_full = jnp.tile(jnp.concatenate([cos_table, cos_table], axis=1), (BLOCK // LEN, 1))
    sin_full = jnp.tile(jnp.concatenate([-sin_table, sin_table], axis=1), (BLOCK // LEN, 1))

    qkv_slots = true_order(slots, zs, zi).reshape(3, width, D)
    w_three = jnp.concatenate(
        [lax.dynamic_index_in_dim(qkv_slots, slot_of[k], 0, keepdims=False) for k in range(3)],
        axis=0,
    )
    out_cols = after(w_out, *slot_steps[-1]).reshape(orow, dps, width).transpose(1, 0, 2)
    out_cols = jnp.broadcast_to(out_cols[:, None], (dps, zs, orow, width))
    w_out_c = lax.all_to_all(
        out_cols.reshape(world, orow, width), ALL, 0, 0, tiled=True
    ).reshape(D, width)
    first_down = lax.all_gather(after(down_half[0], *slot_steps[1]), "q", axis=0, tiled=True)
    dy_all = lax.all_gather(cotangent, "z", axis=0)
    dy_blocks = [
        lax.dynamic_index_in_dim(dy_all, (zi - k) % zs, 0, keepdims=False) for k in range(zs)
    ]

    blocks = all_rows // BLOCK
    half = blocks // 2
    own_spec, other_spec = pieces_spec(half, D // 2)
    piece_specs = [own_spec, own_spec, other_spec, other_spec]
    part_specs = list(pieces_spec(half, D))
    part_shapes = [shape_of(all_rows // 2, D, bf16)] * 2
    hidden_one, raw, sums = run_blocks(
        functools.partial(qkv_kernel, width, half),
        all_rows,
        piece_specs + [whole((1, D)), whole((3 * width, D))],
        [by_rows(D), by_rows(3 * width), across(8)],
        [
            shape_of(all_rows, D, bf16),
            shape_of(all_rows, 3 * width, f32),
            shape_of(8, all_rows, f32),
        ],
        tuple(tok_pieces) + (after(gains_f[:, 0][None], dy_all), w_three),
    )
    gu_half = core_half(after(w_gate_up, hidden_one))
    sums = sum_dp(sums, dps)
    mask_spec = pl.BlockSpec((BLOCK // LEN, LEN, LEN), lambda i: (i, 0, 0))
    table_specs = [whole((8, width)), whole((BLOCK, HD)), whole((BLOCK, HD)), mask_spec]
    tables = (gain_rows, cos_full, sin_full, mask)
    attended, own, other = run_blocks(
        functools.partial(attend_kernel, width, half),
        all_rows,
        [by_rows(3 * width), across(8)] + table_specs + [whole((D, width))],
        [by_rows(width)] + part_specs,
        [shape_of(all_rows, width, bf16)] + part_shapes,
        (raw, sums) + tables + (w_out_c,),
    )
    attn_out, _, attn_last = scatter_dp(own, other, dps)

    expert_w = []
    for e in range(mine):
        if e > 0:
            gu_half[e], down_half[e] = all_after([gu_half[e], down_half[e]], attn_last)
        expert_w.append(
            (
                lax.all_gather(gu_half[e], "q", axis=0, tiled=True),
                lax.all_gather(down_half[e], "q", axis=0, tiled=True) if e else first_down,
            )
        )

    x_float = tokens.astype(f32)
    inverse_one = inverse_rms(x_float)
    normed_one = x_float * inverse_one
    residual = x_float + attn_out
    inverse_two = inverse_rms(residual)
    normed_two = residual * inverse_two
    hidden_two = (normed_two * gains_f[:, 3]).astype(bf16)
    router_probs = jax.nn.softmax(mm(hidden_two, router_low, 1, 0), axis=-1)

    dy_g = both_cores(dy_blocks)
    hidden_blocks, _ = gather_z(hidden_two, zs, zi, {2: [dy_g, router_probs]})
    hidden_g = both_cores(hidden_blocks)
    router_g = jax.nn.softmax(mm(hidden_g, router_low, 1, 0), axis=-1)
    dy_f = dy_g.astype(f32)
    first_expert = zi * local_experts + ci * mine

    passes = []
    for e in range(mine):
        gate_up, down = expert_w[e]
        expert = first_expert + e
        picked = jnp.any(routes_g == expert, axis=1, keepdims=True)
        prob = jnp.sum(
            jnp.where(jnp.arange(E)[None] == expert, router_g, 0.0), axis=1, keepdims=True
        )
        gate_val = jnp.where(picked, prob, 0.0)
        hidden_e = after(hidden_g, passes[-1]["rows"]) if passes else hidden_g
        gate_and_up = mm(hidden_e, gate_up, 1, 1)
        g_part = gate_and_up[:, :FF]
        u_part = gate_and_up[:, FF:]
        sig = jax.nn.sigmoid(g_part)
        silu = g_part * sig
        act = (silu * u_part).astype(bf16)
        expert_out = mm(act, down, 1, 1).astype(bf16).astype(f32)
        grad_gate = jnp.where(picked[:, 0], jnp.sum(dy_f * expert_out, axis=1), 0.0)
        grad_eo = (gate_val * dy_f).astype(bf16)
        grad_act = mm(grad_eo, down, 1, 0)
        grad_g = grad_act * u_part * sig * (1.0 + g_part * (1.0 - sig))
        grad_u = grad_act * silu
        grad_g, grad_u = grad_g.astype(bf16), grad_u.astype(bf16)
        grad_both = jnp.concatenate([grad_g, grad_u], axis=-1)
        rows_back = mm(grad_both, gate_up, 1, 0).astype(bf16)
        dn = mm(grad_eo, act, 0, 0).astype(bf16)
        passes.append(
            dict(
                out=gate_val * expert_out,
                back=rows_back.astype(f32),
                rows=rows_back,
                gate=grad_gate,
                both=(grad_g, grad_u),
                dn=lax.psum_scatter(dn, "q", scatter_dimension=0, tiled=True),
            )
        )

    hid_part = sum([p["back"] for p in passes[1:]], passes[0]["back"])
    out_part = sum([p["out"] for p in passes[1:]], passes[0]["out"])
    cols = jnp.stack([p["gate"] for p in passes], axis=0).reshape(mine, 2, zs, rows)
    cols = jnp.where(ci == 0, cols, cols[:, ::-1])
    cols = cols[:, :, (zi - jnp.arange(zs)) % zs]
    hid_mixed = mix_cores(hid_part.astype(bf16))
    out_mixed = mix_cores(out_part.astype(bf16))
    gus = []

    def fill(*deps):
        p = passes[len(gus)]
        gus.append(weight_grad(*all_after(p["both"], deps), hidden_g))
        return gus[-1:]

    hid_gates = {2: lambda steps: fill(hid_mixed), 3: lambda steps: [cols, out_mixed]}
    if mine > 1:
        hid_gates[3] = lambda steps: fill(*steps[0]) + [cols, out_mixed]
    hid_sum, hid_steps = scatter_z(z_blocks(hid_mixed, zs), hid_gates)
    while len(gus) < mine:
        fill(*hid_steps[1])
    grad_hidden = hid_sum
    got = lax.all_to_all(
        cols.transpose(1, 2, 0, 3).reshape(2 * zs, mine, rows), ("c", "z"), 0, 0, tiled=True
    )
    gp = got.reshape(2, zs, mine, rows).transpose(1, 0, 2, 3).reshape(E, rows).T

    grad_logits = router_probs * (gp - jnp.sum(router_probs * gp, axis=-1, keepdims=True))
    grad_router = lax.dot_general(
        hidden_two.astype(f32), grad_logits, (((0,), (0,)), ((), ())), precision=PRECISE
    )
    grad_hidden = grad_hidden + jnp.dot(grad_logits, router_f.T, precision=PRECISE)
    gain_two = jnp.sum(grad_hidden * normed_two, axis=0)
    grad_residual = cotangent.astype(f32) + norm_back(
        grad_hidden * gains_f[:, 3], normed_two, inverse_two
    )

    def core_back(parts):
        stacked = jnp.stack(parts, axis=0)
        split = stacked.reshape((mine, 2, stacked.shape[1] // 2, stacked.shape[2]))
        got = swap_core(lax.dynamic_index_in_dim(split, 1 - ci, 1, keepdims=False))
        own = lax.dynamic_index_in_dim(split, ci, 1, keepdims=False)
        return jnp.concatenate(in_core_order(own, got), axis=0).astype(f32)

    grad_pieces = []

    def out_gate(steps):
        if len(steps) == 1:
            grad_pieces.extend(
                gather_dp(grad_residual.astype(bf16), dps, gate=gus[-1:] + list(steps[0]))
            )
        return []

    out_total, out_steps = scatter_z(
        z_blocks(after(out_mixed, *hid_steps[-1]), zs), {s: out_gate for s in range(2, zs)}
    )
    gus = [after(gu, *hid_steps[0]) for gu in gus[:-1]] + [after(gus[-1], *grad_pieces)]
    gus = [lax.psum_scatter(gu, "q", scatter_dimension=0, tiled=True) for gu in gus]
    back, dv, dots, gain_sums, grad_out_c = run_blocks(
        functools.partial(attend_back_kernel, width, half),
        all_rows,
        [by_rows(3 * width), across(8)] + table_specs + [whole((D, width)), by_rows(width)]
        + piece_specs,
        [by_rows(2 * width), by_rows(width), across(8), whole((8, width)), whole((D, width))],
        [
            shape_of(all_rows, 2 * width, f32),
            shape_of(all_rows, width, bf16),
            shape_of(8, all_rows, f32),
            shape_of(8, width, f32),
            shape_of(D, width, f32),
        ],
        (raw, sums) + tables + (w_out_c, attended) + tuple(grad_pieces),
    )

    def z_parts(value):
        return [
            lax.dynamic_index_in_dim(value, (zi - k) % zs, 0, keepdims=False) for k in range(zs)
        ]

    dots = sum_dp(after(dots, *out_steps[1]), dps)
    grad_projected, own, other = run_blocks(
        functools.partial(project_back_kernel, width, half),
        all_rows,
        [
            by_rows(3 * width), across(8), by_rows(2 * width), by_rows(width), across(8),
            whole((3 * width, D)),
        ],
        [by_rows(3 * width)] + part_specs,
        [shape_of(all_rows, 3 * width, bf16)] + part_shapes,
        (raw, sums, back, dv, dots, w_three),
    )
    grad_h1, h1_summed, h1_last = scatter_dp(own, other, dps)
    gain_one = jnp.sum(grad_h1 * normed_one, axis=0)
    grad_tokens = grad_residual + norm_back(grad_h1 * gains_f[:, 0], normed_one, inverse_one)
    result = residual + out_total

    hidden_late = after(hidden_one, *out_steps[-1])
    grad_three = mm(grad_projected, hidden_late, 0, 0).astype(bf16).reshape(3, width, D)
    grad_slots = jnp.concatenate(
        [lax.dynamic_index_in_dim(grad_three, type_of[s], 0, keepdims=True) for s in range(3)],
        axis=0,
    )
    grad_cols = grad_out_c.astype(bf16).reshape(dps, zs, orow, width).transpose(1, 2, 0, 3)
    parts = jnp.concatenate(
        [grad_slots.reshape(zs, 3 * sub, D), grad_cols.reshape(zs, orow, D)], axis=1
    )
    dns = [p["dn"] for p in passes]
    grad_down = core_back([after(dns[0], grad_projected)] + dns[1:])
    own_sum, own_steps = scatter_z(z_parts(parts), {s: lambda steps: [] if steps else [h1_summed] for s in range(1, zs)})
    grad_gate_up = core_back([after(gus[0], *own_steps[1])] + gus[1:])
    own_sum = after(own_sum.astype(bf16), grad_down)
    grad_qkv = jnp.concatenate(
        [
            lax.ppermute(own_sum[t * sub : (t + 1) * sub], ALL, unit_perm(t, True))
            for t in range(3)
        ],
        axis=0,
    ).astype(f32)
    own_cols = own_sum[3 * sub :].reshape(orow, dps, width).transpose(1, 0, 2)
    grad_out = (
        lax.all_to_all(own_cols, DP, 0, 0, tiled=True)
        .transpose(1, 0, 2)
        .reshape(orow, D)
        .astype(f32)
    )

    shard_cols = lax.dynamic_update_slice(jnp.zeros((D, 2), f32), gain_sums[:2].T, (di * width, 0))
    small_grads = jnp.concatenate(
        [gain_one[:, None], shard_cols, gain_two[:, None], grad_router], axis=1
    )
    small_own = jnp.sum(
        lax.all_to_all(
            small_grads.reshape(world, D * (E + 4) // world), ALL, 0, 0, tiled=True
        ),
        axis=0,
    ).reshape(D // world, E + 4)

    return (
        result.astype(bf16),
        grad_tokens,
        grad_qkv,
        grad_out,
        small_own[:, :4],
        small_own[:, 4:],
        grad_gate_up,
        grad_down,
    )


def solution(mesh):
    dps, zs = mesh.shape["dp"], mesh.shape["fsdp"]
    inner = Mesh(mesh.devices.reshape(dps // 2, 2, zs), ALL)
    rows = P(ALL, None)
    experts = P("z", DP, None)
    in_specs = (rows,) * 8 + (experts,) * 2
    out_specs = (rows,) * 6 + (experts,) * 2
    return jax.shard_map(
        per_device, mesh=inner, in_specs=in_specs, out_specs=out_specs, check_vma=False
    )
```

```python
import functools

import jax
import jax.numpy as jnp
from jax import lax
from jax.experimental import pallas as pl
from jax.experimental.pallas import tpu as pltpu
from jax.sharding import Mesh
from jax.sharding import PartitionSpec as P

D = 2048
H = 16
HD = 128
FF = 1024
TOP = 8
E = 16
LEN = 96

NORM_EPS = 1e-05
ROPE_BASE = 10000.0
PRECISE = lax.Precision.HIGHEST
DP = ("q", "c")
ALL = ("q", "c", "z")
f32 = jnp.float32
bf16 = jnp.bfloat16


def inverse_rms(field_in):
    return lax.rsqrt(jnp.mean(field_in * field_in, axis=-1, keepdims=True) + NORM_EPS)


def rope_tables(length, head_dim):
    half_dim = head_dim // 2
    frequency = ROPE_BASE ** (-(jnp.arange(half_dim).astype(f32) * 2.0) / head_dim)
    angles = jnp.arange(length).astype(f32)[:, None] * frequency[None, :]
    return jnp.cos(angles), jnp.sin(angles)


def norm_back(grad_normed, normed, inverse):
    return inverse * (grad_normed - normed * jnp.mean(grad_normed * normed, axis=-1, keepdims=True))


def mm(a, b, ca, cb):
    return lax.dot_general(a, b, (((ca,), (cb,)), ((), ())), preferred_element_type=f32)


def after(value, *deps):
    return lax.optimization_barrier((value,) + tuple(deps))[0]


def flip(value, size, bit):
    return lax.ppermute(value, DP, [(i, i ^ (1 << bit)) for i in range(size)])


def relative(size):
    return [high * 2 + core for core in range(2) for high in range(size // 2)]


def bit_lists(size):
    high = list(range(1, size.bit_length() - 1))
    return high, high[::-1]


def gather_dp(value, size, gate=()):
    width = value.shape[-1] // 2
    pieces = []
    for part, order in zip((value[:, :width], value[:, width:]), bit_lists(size)):
        out, have = part, []
        for bit in order:
            axis = sum(1 for other in have if other > bit)
            out = jnp.stack([out, flip(out, size, bit)], axis=axis)
            have.append(bit)
        pieces.append(out.reshape(-1, width))
    sent = [after(piece, *gate) for piece in pieces] if gate else pieces
    return pieces + [flip(piece, size, 0) for piece in sent]


def scatter_dp(own, other, size):
    rows, width = own.shape[0] * 2 // size, own.shape[1]
    got = flip(other, size, 0)
    summed = (own.astype(f32) + got.astype(f32)).astype(bf16)
    highs = size.bit_length() - 2
    halves, last = [], []
    for half, order in enumerate(bit_lists(size)):
        cur = summed[:, half * (width // 2) : (half + 1) * (width // 2)]
        cur = cur.reshape([2] * highs + [rows, width // 2])
        left = list(range(highs, 0, -1))
        for k, bit in enumerate(order):
            axis = left.index(bit)
            left.remove(bit)
            keep = lax.index_in_dim(cur, 0, axis, keepdims=False)
            send = lax.index_in_dim(cur, 1, axis, keepdims=False)
            brought = flip(send, size, bit)
            total = keep.astype(f32) + brought.astype(f32)
            cur = total if k == len(order) - 1 else total.astype(bf16)
        halves.append(cur)
        last.append(brought)
    return jnp.concatenate(halves, axis=-1), summed, last


def sum_dp(value, size):
    count = size.bit_length() - 1
    shape = value.shape
    value = value[:2].reshape((2,) + (2,) * count + (-1,))
    for bit in range(count):
        value = value + jnp.flip(flip(value, size, bit), 1 if bit == 0 else count - bit + 1)
    return jnp.pad(value.reshape(2, shape[1]), ((0, 6), (0, 0)))


def line(value, zs, step):
    return lax.ppermute(value, "z", [(j, j + step) for j in range(zs) if 0 <= j + step < zs])


def all_after(values, deps):
    return list(lax.optimization_barrier(tuple(values) + tuple(deps))[: len(values)])


def gather_z(value, zs, zi, gates={}):
    right, left = [value], [value]
    for s in range(1, zs):
        sent = all_after([right[-1], left[-1]], gates[s]) if s in gates else [right[-1], left[-1]]
        right.append(line(sent[0], zs, 1))
        left.append(line(sent[1], zs, -1))
    blocks = [value] + [jnp.where(zi >= k, right[k], left[zs - k]) for k in range(1, zs)]
    return blocks, list(zip(right, left))


def true_order(blocks, zs, zi):
    out = jnp.zeros((zs,) + blocks[0].shape, blocks[0].dtype)
    for k, block in enumerate(blocks):
        out = lax.dynamic_update_index_in_dim(out, block, (zi - k) % zs, 0)
    return out


def scatter_z(parts, gates={}):
    zs = len(parts)
    right, left = None, None
    steps = []
    for s in range(1, zs):
        go_right = parts[s] if right is None else (parts[s].astype(f32) + right).astype(bf16)
        go_left = parts[zs - s] if left is None else (parts[zs - s].astype(f32) + left).astype(bf16)
        if s in gates:
            go_right, go_left = all_after([go_right, go_left], gates[s](steps))
        got_right, got_left = line(go_right, zs, 1), line(go_left, zs, -1)
        steps.append((got_right, got_left))
        right, left = got_right.astype(f32), got_left.astype(f32)
    return parts[0].astype(f32) + right + left, steps


def swap_core(value):
    return lax.ppermute(value, "c", [(0, 1), (1, 0)])


def both_cores(blocks):
    got = jnp.concatenate(blocks, axis=0)
    return jnp.concatenate([got, swap_core(got)], axis=0)


def mix_cores(parts):
    half = parts.shape[0] // 2
    return (parts[:half].astype(f32) + swap_core(parts[half:]).astype(f32)).astype(bf16)


def z_blocks(mixed, zs):
    block = mixed.shape[0] // zs
    return [mixed[k * block : (k + 1) * block] for k in range(zs)]


BLOCK = 4 * LEN


def kdot(a, b, ca, cb):
    return lax.dot_general(a, b, (((ca,), (cb,)), ((), ())), preferred_element_type=f32)


def to_rows(first, second):
    lane = lax.broadcasted_iota(jnp.int32, (first.shape[0], 128), 1)
    both = jnp.where(lane == 0, first, jnp.where(lane == 1, second, 0.0))
    return both.T[:8]


def to_cols(block):
    cols = jnp.concatenate([block] * 16, axis=0).T
    return cols[:, 0:1], cols[:, 1:2]


def own_rows(half):
    return pl.program_id(0) < half


def picked_rows(half, own_ref, other_ref):
    return jnp.where(own_rows(half), own_ref[...].astype(f32), other_ref[...].astype(f32))


def store_rows(half, own_ref, other_ref, value):
    @pl.when(own_rows(half))
    def _():
        own_ref[...] = value

    @pl.when(jnp.logical_not(own_rows(half)))
    def _():
        other_ref[...] = value


def qkv_kernel(
    width, half, a_own, b_own, a_other, b_other, gain_ref, w_ref, hid_ref, raw_ref, sum_ref
):
    x_a = picked_rows(half, a_own, a_other)
    x_b = picked_rows(half, b_own, b_other)
    square = jnp.sum(x_a * x_a, axis=-1, keepdims=True) + jnp.sum(x_b * x_b, axis=-1, keepdims=True)
    inverse = lax.rsqrt(square / D + NORM_EPS)
    hid_ref[:, : D // 2] = (x_a * inverse * gain_ref[:, : D // 2]).astype(bf16)
    hid_ref[:, D // 2 :] = (x_b * inverse * gain_ref[:, D // 2 :]).astype(bf16)
    raw = kdot(hid_ref[...], w_ref[...], 1, 1)
    raw_ref[...] = raw
    q, k = raw[:, :width], raw[:, width : 2 * width]
    sum_ref[...] = to_rows(
        jnp.sum(q * q, axis=-1, keepdims=True), jnp.sum(k * k, axis=-1, keepdims=True)
    )


def spin(x, cos, sin):
    return x * cos + pltpu.roll(x, HD // 2, 1) * sin


def heads_of(raw, inv_q, inv_k, gain_ref, cos, sin, width, head):
    lo = head * HD
    normed_q = raw[:, lo : lo + HD] * inv_q
    normed_k = raw[:, width + lo : width + lo + HD] * inv_k
    query = spin(normed_q * gain_ref[0:1, lo : lo + HD], cos, sin).astype(bf16)
    key = spin(normed_k * gain_ref[1:2, lo : lo + HD], cos, sin).astype(bf16)
    value = raw[:, 2 * width + lo : 2 * width + lo + HD].astype(bf16)
    return normed_q, normed_k, query, key, value


def probs_of(query, key, mask):
    scores = jnp.where(mask > 0.5, kdot(query, key, 1, 1) * HD ** (-0.5), -1e30)
    scores = jnp.exp(scores - jnp.max(scores, axis=-1, keepdims=True))
    return scores / jnp.sum(scores, axis=-1, keepdims=True)


def inverses(sum_ref):
    ss_q, ss_k = to_cols(sum_ref[...])
    return lax.rsqrt(ss_q / D + NORM_EPS), lax.rsqrt(ss_k / D + NORM_EPS)


def attend_kernel(
    width, half, raw_ref, sum_ref, gain_ref, cos_ref, sin_ref, mask_ref, w_ref,
    att_ref, own_ref, other_ref,
):
    inv_q, inv_k = inverses(sum_ref)
    raw = raw_ref[...]
    cos, sin = cos_ref[...], sin_ref[...]
    for head in range(width // HD):
        _, _, query, key, value = heads_of(raw, inv_q, inv_k, gain_ref, cos, sin, width, head)
        for s in range(BLOCK // LEN):
            at = slice(s * LEN, (s + 1) * LEN)
            probs = probs_of(query[at], key[at], mask_ref[s])
            att_ref[at, head * HD : (head + 1) * HD] = kdot(
                probs.astype(bf16), value[at], 1, 0
            ).astype(bf16)
    store_rows(half, own_ref, other_ref, kdot(att_ref[...], w_ref[...], 1, 1).astype(bf16))


def attend_back_kernel(
    width, half, raw_ref, sum_ref, gain_ref, cos_ref, sin_ref, mask_ref, w_ref, att_ref,
    a_own, b_own, a_other, b_other, back_ref, dv_ref, dot_ref, gsum_ref, gout_ref,
):
    inv_q, inv_k = inverses(sum_ref)
    raw = raw_ref[...]
    cos, sin = cos_ref[...], sin_ref[...]
    grad_a = picked_rows(half, a_own, a_other).astype(bf16)
    grad_b = picked_rows(half, b_own, b_other).astype(bf16)
    grad_heads = kdot(grad_a, w_ref[: D // 2], 1, 0) + kdot(grad_b, w_ref[D // 2 :], 1, 0)
    grad_heads = grad_heads.astype(bf16)

    @pl.when(pl.program_id(0) == 0)
    def _():
        gsum_ref[...] = jnp.zeros_like(gsum_ref)
        gout_ref[...] = jnp.zeros_like(gout_ref)

    gout_ref[: D // 2] += kdot(grad_a, att_ref[...], 0, 0)
    gout_ref[D // 2 :] += kdot(grad_b, att_ref[...], 0, 0)

    dot_q = dot_k = 0.0
    for head in range(width // HD):
        lo = head * HD
        normed_q, normed_k, query, key, value = heads_of(
            raw, inv_q, inv_k, gain_ref, cos, sin, width, head
        )
        grads_q, grads_k = [], []
        for s in range(BLOCK // LEN):
            at = slice(s * LEN, (s + 1) * LEN)
            probs = probs_of(query[at], key[at], mask_ref[s])
            grad = grad_heads[at, lo : lo + HD]
            grad_probs = kdot(grad, value[at], 1, 1)
            dv_ref[at, lo : lo + HD] = kdot(probs.astype(bf16), grad, 0, 0).astype(bf16)
            delta = jnp.sum(probs * grad_probs, axis=-1, keepdims=True)
            grad_scores = (probs * (grad_probs - delta)).astype(bf16)
            grads_q.append(kdot(grad_scores, key[at], 1, 0))
            grads_k.append(kdot(grad_scores, query[at], 0, 0))
        grad_nq = spin(jnp.concatenate(grads_q, axis=0) * HD ** (-0.5), cos, -sin)
        grad_nk = spin(jnp.concatenate(grads_k, axis=0) * HD ** (-0.5), cos, -sin)
        prod_q, prod_k = grad_nq * normed_q, grad_nk * normed_k
        gsum_ref[0:1, lo : lo + HD] += jnp.sum(prod_q, axis=0, keepdims=True)
        gsum_ref[1:2, lo : lo + HD] += jnp.sum(prod_k, axis=0, keepdims=True)
        gain_q, gain_k = gain_ref[0:1, lo : lo + HD], gain_ref[1:2, lo : lo + HD]
        dot_q = dot_q + jnp.sum(prod_q * gain_q, axis=-1, keepdims=True)
        dot_k = dot_k + jnp.sum(prod_k * gain_k, axis=-1, keepdims=True)
        back_ref[:, lo : lo + HD] = grad_nq * gain_q
        back_ref[:, width + lo : width + lo + HD] = grad_nk * gain_k
    dot_ref[...] = to_rows(dot_q, dot_k)


def project_back_kernel(
    width, half, raw_ref, sum_ref, back_ref, dv_ref, dot_ref, w_ref, proj_ref, own_ref, other_ref
):
    inv_q, inv_k = inverses(sum_ref)
    mean_q, mean_k = to_cols(dot_ref[...] / D)
    normed_q = raw_ref[:, :width] * inv_q
    normed_k = raw_ref[:, width : 2 * width] * inv_k
    proj_ref[:, :width] = (inv_q * (back_ref[:, :width] - normed_q * mean_q)).astype(bf16)
    proj_ref[:, width : 2 * width] = (
        inv_k * (back_ref[:, width:] - normed_k * mean_k)
    ).astype(bf16)
    proj_ref[:, 2 * width :] = dv_ref[...]
    store_rows(half, own_ref, other_ref, kdot(proj_ref[...], w_ref[...], 1, 0).astype(bf16))


def by_rows(cols):
    return pl.BlockSpec((BLOCK, cols), lambda i: (i, 0))


def pieces_spec(half, cols):
    own = pl.BlockSpec((BLOCK, cols), lambda i: (jnp.minimum(i, half - 1), 0))
    other = pl.BlockSpec((BLOCK, cols), lambda i: (jnp.maximum(i - half, 0), 0))
    return own, other


def across(rows):
    return pl.BlockSpec((rows, BLOCK), lambda i: (0, i))


def whole(shape):
    return pl.BlockSpec(shape, lambda i: (0,) * len(shape))


def run_blocks(body, rows, in_specs, out_specs, out_shape, args):
    return pl.pallas_call(
        body,
        grid=(rows // BLOCK,),
        in_specs=in_specs,
        out_specs=out_specs,
        out_shape=out_shape,
        cost_estimate=pl.CostEstimate(flops=1, bytes_accessed=1, transcendentals=0),
    )(*args)


def weight_grad_kernel(half, g_ref, u_ref, b_ref, out_ref):
    @pl.when(pl.program_id(1) < half)
    def _():
        out_ref[...] = kdot(g_ref[...], b_ref[...], 0, 0).astype(bf16)

    @pl.when(pl.program_id(1) >= half)
    def _():
        out_ref[...] = kdot(u_ref[...], b_ref[...], 0, 0).astype(bf16)


def weight_grad(g, u, b):
    tile_a, tile_b = 512, 1024
    half = g.shape[1] // tile_a
    return pl.pallas_call(
        functools.partial(weight_grad_kernel, half),
        grid=(b.shape[1] // tile_b, 2 * half),
        in_specs=[
            pl.BlockSpec((g.shape[0], tile_a), lambda n, m: (0, jnp.minimum(m, half - 1))),
            pl.BlockSpec((u.shape[0], tile_a), lambda n, m: (0, jnp.maximum(m - half, 0))),
            pl.BlockSpec((b.shape[0], tile_b), lambda n, m: (0, n)),
        ],
        out_specs=pl.BlockSpec((tile_a, tile_b), lambda n, m: (m, n)),
        out_shape=jax.ShapeDtypeStruct((2 * g.shape[1], b.shape[1]), bf16),
        cost_estimate=pl.CostEstimate(flops=1, bytes_accessed=1, transcendentals=0),
    )(g, u, b)


def shape_of(rows, cols, dtype):
    return jax.ShapeDtypeStruct((rows, cols), dtype)


def per_device(
    tokens, cotangent, segments, routes, w_qkv, w_out, norm_gains, w_router, w_gate_up, w_down
):
    zs = lax.axis_size("z")
    dps = lax.axis_size("q") * 2
    world = dps * zs
    qi, ci, zi = lax.axis_index("q"), lax.axis_index("c"), lax.axis_index("z")
    di = qi * 2 + ci
    rows = tokens.shape[0]
    seqs = rows // LEN
    width = D // dps
    local_experts = E // zs
    mine = local_experts // 2
    sub = w_qkv.shape[0] // 3
    orow = w_out.shape[0]
    all_rows = dps * rows
    all_seqs = dps * seqs

    def unit_perm(t, back):
        pairs = []
        for i in range(dps):
            for j in range(zs):
                dest = (3 * i + (3 * j + t) // zs) % dps
                src_dev, dst_dev = i * zs + j, dest * zs + j
                pairs.append((dst_dev, src_dev) if back else (src_dev, dst_dev))
        return pairs

    moved = [
        lax.ppermute(w_qkv[t * sub : (t + 1) * sub], ALL, unit_perm(t, False)) for t in range(3)
    ]
    def in_core_order(own, got):
        first = ci == 0
        return jnp.where(first, own, got), jnp.where(first, got, own)

    def core_half(weight):
        split = weight.reshape((2, mine) + weight.shape[1:])
        got = swap_core(lax.dynamic_index_in_dim(split, 1 - ci, 0, keepdims=False))
        own = lax.dynamic_index_in_dim(split, ci, 0, keepdims=False)
        both = in_core_order(own, got)
        return [jnp.concatenate([half[e] for half in both], axis=0) for e in range(mine)]

    down_half = core_half(w_down)

    mini = jnp.concatenate(
        [
            norm_gains.reshape(-1),
            w_router.reshape(-1),
            segments.astype(bf16).reshape(-1),
            routes.astype(bf16).reshape(-1),
        ]
    )
    minis = lax.all_to_all(
        jnp.broadcast_to(mini[None], (world,) + mini.shape), ALL, 0, 0, tiled=True
    )

    tok_pieces = gather_dp(tokens, dps)
    slots, slot_steps = gather_z(
        after(jnp.concatenate(moved, axis=0), minis, *down_half), zs, zi,
        {s: [] if s < zs - 1 else tok_pieces[:2] for s in range(2, zs)},
    )
    inv3 = pow(3, -1, dps)
    slot_of = [[0, 0, 0] for _ in range(dps)]
    type_of = [[0, 0, 0] for _ in range(dps)]
    for i in range(dps):
        for s in range(3):
            src = (inv3 * (i - s)) % dps
            kind = (3 * src + s) // dps
            slot_of[i][kind] = s
            type_of[i][s] = kind
    slot_of = jnp.asarray(slot_of, jnp.int32)[di]
    type_of = jnp.asarray(type_of, jnp.int32)[di]

    at = 0
    split = []
    for part in (norm_gains, w_router, segments, routes):
        split.append(minis[:, at : at + part.size])
        at += part.size
    gains_f = split[0].reshape(D, 4).astype(f32)
    router_low = split[1].reshape(D, E)
    router_f = router_low.astype(f32)
    seg_all = split[2].reshape(dps, zs, seqs, LEN)
    seg_own = lax.dynamic_index_in_dim(seg_all, zi, 1, keepdims=False)
    seg_own = seg_own[jnp.asarray(relative(dps)) ^ di].reshape(all_seqs, LEN)
    routes_all = split[3].reshape(dps // 2, 2, zs, rows, TOP)
    routes_own = lax.dynamic_index_in_dim(routes_all, qi, 0, keepdims=False)
    routes_own = routes_own[jnp.stack([ci, 1 - ci])][:, (zi - jnp.arange(zs)) % zs]
    routes_g = routes_own.reshape(2 * zs * rows, TOP).astype(jnp.int32)
    position = jnp.arange(LEN)
    causal = position[:, None] >= position[None, :]
    mask = (causal[None] & (seg_own[:, :, None] == seg_own[:, None, :])).astype(f32)
    own_gains = lax.dynamic_slice(gains_f, (di * width, 0), (width, 4))
    gain_rows = jnp.pad(own_gains[:, 1:3].T, ((0, 6), (0, 0)))
    cos_table, sin_table = rope_tables(LEN, HD)
    cos_full = jnp.tile(jnp.concatenate([cos_table, cos_table], axis=1), (BLOCK // LEN, 1))
    sin_full = jnp.tile(jnp.concatenate([-sin_table, sin_table], axis=1), (BLOCK // LEN, 1))

    qkv_slots = true_order(slots, zs, zi).reshape(3, width, D)
    w_three = jnp.concatenate(
        [lax.dynamic_index_in_dim(qkv_slots, slot_of[k], 0, keepdims=False) for k in range(3)],
        axis=0,
    )
    out_cols = after(w_out, *slot_steps[2]).reshape(orow, dps, width).transpose(1, 0, 2)
    out_cols = jnp.broadcast_to(out_cols[:, None], (dps, zs, orow, width))
    w_out_c = lax.all_to_all(
        out_cols.reshape(world, orow, width), ALL, 0, 0, tiled=True
    ).reshape(D, width)
    first_down = lax.all_gather(down_half[0], "q", axis=0, tiled=True)
    dy_all = lax.all_gather(after(cotangent, first_down, *slot_steps[-1]), "z", axis=0)
    dy_blocks = [
        lax.dynamic_index_in_dim(dy_all, (zi - k) % zs, 0, keepdims=False) for k in range(zs)
    ]

    blocks = all_rows // BLOCK
    half = blocks // 2
    own_spec, other_spec = pieces_spec(half, D // 2)
    piece_specs = [own_spec, own_spec, other_spec, other_spec]
    part_specs = list(pieces_spec(half, D))
    part_shapes = [shape_of(all_rows // 2, D, bf16)] * 2
    hidden_one, raw, sums = run_blocks(
        functools.partial(qkv_kernel, width, half),
        all_rows,
        piece_specs + [whole((1, D)), whole((3 * width, D))],
        [by_rows(D), by_rows(3 * width), across(8)],
        [
            shape_of(all_rows, D, bf16),
            shape_of(all_rows, 3 * width, f32),
            shape_of(8, all_rows, f32),
        ],
        tuple(tok_pieces) + (after(gains_f[:, 0][None], w_out_c), w_three),
    )
    gu_half = core_half(after(w_gate_up, hidden_one))
    sums = sum_dp(sums, dps)
    mask_spec = pl.BlockSpec((BLOCK // LEN, LEN, LEN), lambda i: (i, 0, 0))
    table_specs = [whole((8, width)), whole((BLOCK, HD)), whole((BLOCK, HD)), mask_spec]
    tables = (gain_rows, cos_full, sin_full, mask)
    attended, own, other = run_blocks(
        functools.partial(attend_kernel, width, half),
        all_rows,
        [by_rows(3 * width), across(8)] + table_specs + [whole((D, width))],
        [by_rows(width)] + part_specs,
        [shape_of(all_rows, width, bf16)] + part_shapes,
        (raw, sums) + tables + (w_out_c,),
    )
    attn_out, _, attn_last = scatter_dp(own, other, dps)

    expert_w = []
    for e in range(mine):
        if e > 0:
            gu_half[e], down_half[e] = all_after([gu_half[e], down_half[e]], attn_last)
        expert_w.append(
            (
                lax.all_gather(gu_half[e], "q", axis=0, tiled=True),
                lax.all_gather(down_half[e], "q", axis=0, tiled=True) if e else first_down,
            )
        )

    x_float = tokens.astype(f32)
    inverse_one = inverse_rms(x_float)
    normed_one = x_float * inverse_one
    residual = x_float + attn_out
    inverse_two = inverse_rms(residual)
    normed_two = residual * inverse_two
    hidden_two = (normed_two * gains_f[:, 3]).astype(bf16)
    router_probs = jax.nn.softmax(mm(hidden_two, router_low, 1, 0), axis=-1)

    dy_g = both_cores(dy_blocks)
    hidden_blocks, _ = gather_z(hidden_two, zs, zi, {2: [dy_g, router_probs]})
    hidden_g = both_cores(hidden_blocks)
    router_g = jax.nn.softmax(mm(hidden_g, router_low, 1, 0), axis=-1)
    dy_f = dy_g.astype(f32)
    first_expert = zi * local_experts + ci * mine

    passes = []
    for e in range(mine):
        gate_up, down = expert_w[e]
        expert = first_expert + e
        picked = jnp.any(routes_g == expert, axis=1, keepdims=True)
        prob = jnp.sum(
            jnp.where(jnp.arange(E)[None] == expert, router_g, 0.0), axis=1, keepdims=True
        )
        gate_val = jnp.where(picked, prob, 0.0)
        hidden_e = after(hidden_g, passes[-1]["rows"]) if passes else hidden_g
        gate_and_up = mm(hidden_e, gate_up, 1, 1)
        g_part = gate_and_up[:, :FF]
        u_part = gate_and_up[:, FF:]
        sig = jax.nn.sigmoid(g_part)
        silu = g_part * sig
        act = (silu * u_part).astype(bf16)
        expert_out = mm(act, down, 1, 1).astype(bf16).astype(f32)
        grad_gate = jnp.where(picked[:, 0], jnp.sum(dy_f * expert_out, axis=1), 0.0)
        grad_eo = (gate_val * dy_f).astype(bf16)
        grad_act = mm(grad_eo, down, 1, 0)
        grad_g = grad_act * u_part * sig * (1.0 + g_part * (1.0 - sig))
        grad_u = grad_act * silu
        grad_g, grad_u = grad_g.astype(bf16), grad_u.astype(bf16)
        grad_both = jnp.concatenate([grad_g, grad_u], axis=-1)
        rows_back = mm(grad_both, gate_up, 1, 0).astype(bf16)
        dn = mm(grad_eo, act, 0, 0).astype(bf16)
        passes.append(
            dict(
                out=gate_val * expert_out,
                back=rows_back.astype(f32),
                rows=rows_back,
                gate=grad_gate,
                both=(grad_g, grad_u),
                dn=lax.psum_scatter(dn, "q", scatter_dimension=0, tiled=True),
            )
        )

    hid_part = sum([p["back"] for p in passes[1:]], passes[0]["back"])
    out_part = sum([p["out"] for p in passes[1:]], passes[0]["out"])
    cols = jnp.stack([p["gate"] for p in passes], axis=0).reshape(mine, 2, zs, rows)
    cols = jnp.where(ci == 0, cols, cols[:, ::-1])
    cols = cols[:, :, (zi - jnp.arange(zs)) % zs]
    hid_mixed = mix_cores(hid_part.astype(bf16))
    out_mixed = mix_cores(out_part.astype(bf16))
    gus = []

    def fill(*deps):
        p = passes[len(gus)]
        gus.append(weight_grad(*all_after(p["both"], deps), hidden_g))
        return gus[-1:]

    hid_gates = {2: lambda steps: fill(hid_mixed), 3: lambda steps: [cols, out_mixed]}
    if mine > 1:
        hid_gates[3] = lambda steps: fill(*steps[0]) + [cols, out_mixed]
    hid_sum, hid_steps = scatter_z(z_blocks(hid_mixed, zs), hid_gates)
    while len(gus) < mine:
        fill(*hid_steps[1])
    grad_hidden = hid_sum
    got = lax.all_to_all(
        cols.transpose(1, 2, 0, 3).reshape(2 * zs, mine, rows), ("c", "z"), 0, 0, tiled=True
    )
    gp = got.reshape(2, zs, mine, rows).transpose(1, 0, 2, 3).reshape(E, rows).T

    grad_logits = router_probs * (gp - jnp.sum(router_probs * gp, axis=-1, keepdims=True))
    grad_router = lax.dot_general(
        hidden_two.astype(f32), grad_logits, (((0,), (0,)), ((), ())), precision=PRECISE
    )
    grad_hidden = grad_hidden + jnp.dot(grad_logits, router_f.T, precision=PRECISE)
    gain_two = jnp.sum(grad_hidden * normed_two, axis=0)
    grad_residual = cotangent.astype(f32) + norm_back(
        grad_hidden * gains_f[:, 3], normed_two, inverse_two
    )

    def core_back(parts):
        stacked = jnp.stack(parts, axis=0)
        split = stacked.reshape((mine, 2, stacked.shape[1] // 2, stacked.shape[2]))
        got = swap_core(lax.dynamic_index_in_dim(split, 1 - ci, 1, keepdims=False))
        own = lax.dynamic_index_in_dim(split, ci, 1, keepdims=False)
        return jnp.concatenate(in_core_order(own, got), axis=0).astype(f32)

    grad_pieces = []

    def out_gate(steps):
        if len(steps) == 1:
            grad_pieces.extend(
                gather_dp(grad_residual.astype(bf16), dps, gate=gus[-1:] + list(steps[0]))
            )
        return []

    out_total, out_steps = scatter_z(
        z_blocks(after(out_mixed, *hid_steps[-1]), zs), {s: out_gate for s in range(2, zs)}
    )
    gus = [after(gu, *hid_steps[0]) for gu in gus[:-1]] + [after(gus[-1], *grad_pieces)]
    gus = [lax.psum_scatter(gu, "q", scatter_dimension=0, tiled=True) for gu in gus]
    back, dv, dots, gain_sums, grad_out_c = run_blocks(
        functools.partial(attend_back_kernel, width, half),
        all_rows,
        [by_rows(3 * width), across(8)] + table_specs + [whole((D, width)), by_rows(width)]
        + piece_specs,
        [by_rows(2 * width), by_rows(width), across(8), whole((8, width)), whole((D, width))],
        [
            shape_of(all_rows, 2 * width, f32),
            shape_of(all_rows, width, bf16),
            shape_of(8, all_rows, f32),
            shape_of(8, width, f32),
            shape_of(D, width, f32),
        ],
        (raw, sums) + tables + (w_out_c, attended) + tuple(grad_pieces),
    )

    def z_parts(value):
        return [
            lax.dynamic_index_in_dim(value, (zi - k) % zs, 0, keepdims=False) for k in range(zs)
        ]

    dots = sum_dp(after(dots, *out_steps[1]), dps)
    grad_projected, own, other = run_blocks(
        functools.partial(project_back_kernel, width, half),
        all_rows,
        [
            by_rows(3 * width), across(8), by_rows(2 * width), by_rows(width), across(8),
            whole((3 * width, D)),
        ],
        [by_rows(3 * width)] + part_specs,
        [shape_of(all_rows, 3 * width, bf16)] + part_shapes,
        (raw, sums, back, dv, dots, w_three),
    )
    grad_h1, h1_summed, h1_last = scatter_dp(own, other, dps)
    gain_one = jnp.sum(grad_h1 * normed_one, axis=0)
    grad_tokens = grad_residual + norm_back(grad_h1 * gains_f[:, 0], normed_one, inverse_one)
    result = residual + out_total

    hidden_late = after(hidden_one, *out_steps[-1])
    grad_three = mm(grad_projected, hidden_late, 0, 0).astype(bf16).reshape(3, width, D)
    grad_slots = jnp.concatenate(
        [lax.dynamic_index_in_dim(grad_three, type_of[s], 0, keepdims=True) for s in range(3)],
        axis=0,
    )
    grad_cols = grad_out_c.astype(bf16).reshape(dps, zs, orow, width).transpose(1, 2, 0, 3)
    parts = jnp.concatenate(
        [grad_slots.reshape(zs, 3 * sub, D), grad_cols.reshape(zs, orow, D)], axis=1
    )
    dns = [p["dn"] for p in passes]
    grad_down = core_back([after(dns[0], grad_projected)] + dns[1:])
    own_sum, own_steps = scatter_z(z_parts(parts), {s: lambda steps: [] if steps else [h1_summed] for s in range(1, zs)})
    grad_gate_up = core_back([after(gus[0], *own_steps[1])] + gus[1:])
    own_sum = after(own_sum.astype(bf16), grad_down)
    grad_qkv = jnp.concatenate(
        [
            lax.ppermute(own_sum[t * sub : (t + 1) * sub], ALL, unit_perm(t, True))
            for t in range(3)
        ],
        axis=0,
    ).astype(f32)
    own_cols = own_sum[3 * sub :].reshape(orow, dps, width).transpose(1, 0, 2)
    grad_out = (
        lax.all_to_all(own_cols, DP, 0, 0, tiled=True)
        .transpose(1, 0, 2)
        .reshape(orow, D)
        .astype(f32)
    )

    shard_cols = lax.dynamic_update_slice(jnp.zeros((D, 2), f32), gain_sums[:2].T, (di * width, 0))
    small_grads = jnp.concatenate(
        [gain_one[:, None], shard_cols, gain_two[:, None], grad_router], axis=1
    )
    small_own = jnp.sum(
        lax.all_to_all(
            small_grads.reshape(world, D * (E + 4) // world), ALL, 0, 0, tiled=True
        ),
        axis=0,
    ).reshape(D // world, E + 4)

    return (
        result.astype(bf16),
        grad_tokens,
        grad_qkv,
        grad_out,
        small_own[:, :4],
        small_own[:, 4:],
        grad_gate_up,
        grad_down,
    )


def solution(mesh):
    dps, zs = mesh.shape["dp"], mesh.shape["fsdp"]
    inner = Mesh(mesh.devices.reshape(dps // 2, 2, zs), ALL)
    rows = P(ALL, None)
    experts = P("z", DP, None)
    in_specs = (rows,) * 8 + (experts,) * 2
    out_specs = (rows,) * 6 + (experts,) * 2
    return jax.shard_map(
        per_device, mesh=inner, in_specs=in_specs, out_specs=out_specs, check_vma=False
    )
```
